32 devices in a mesh: groups: 2 (over x), replica: 2 (over core), tensor: 8 (over z, y).
Axes of the slice: x: 2, y: 2, z: 4, core: 2. Of those that a mesh axis runs over, the one named last changes fastest.
Arguments:
- hidden: bfloat16 [128, 8192], P(('groups', 'replica'), 'tensor'), parts along dimension 0, may hold values from -6 to 6
- w_query: bfloat16 [8192, 8192], P(None, 'tensor'), may hold values from -0.0625 to 0.0625
- output_weight: bfloat16 [8192, 8192], P('tensor'), may hold values from -0.09375 to 0.09375
- keys: bfloat16 [128, 8, 32, 128], P(('groups', 'replica')), parts along dimension 0
- values: bfloat16 [128, 8, 32, 128], P(('groups', 'replica')), parts along dimension 0, may hold values from -6 to 6
- query_down_maps: bfloat16 [16, 64, 8192], P(('groups', 'replica'), None, 'tensor'), parts along dimension 0, may hold values from -0.0625 to 0.0625
- query_up_maps: bfloat16 [16, 64, 8192], P(('groups', 'replica'), None, 'tensor'), parts along dimension 0, may hold values from -0.75 to 0.75
- output_down_maps: bfloat16 [16, 64, 8192], P(('groups', 'replica'), None, 'tensor'), parts along dimension 0, may hold values from -0.0625 to 0.0625
- output_up_maps: bfloat16 [16, 64, 8192], P(('groups', 'replica'), None, 'tensor'), parts along dimension 0, may hold values from -0.75 to 0.75
- adapter_ids: int32 [128], P('groups'), parts along dimension 0, may hold values from 0 to 7
- owner_map: int32 [16], P('groups'), parts along dimension 0, may hold values from 0 to 7, each once
- kv_lengths: int32 [128], P(('groups', 'replica')), parts along dimension 0, may hold values from 1 to 32, as said below
Outputs:
- attn_out: bfloat16 [128, 8192], P(('groups', 'replica'), 'tensor'), parts along dimension 0
The draws below stay inside these ranges and needn't reach their ends.
There are 2 independent parts, one for each index of `groups`. The reference program is written for one: setup_inputs(seed, part) draws one part's arguments, and reference() takes and returns one part's arrays. A program takes and returns all parts, laid end to end along the dimension named above; an argument that names none is the same for every part. Nothing has to cross between parts.
Inputs may be any that keep to these rules, and one draw needn't show every extreme that they name: `owner_map`: every request's adapter has a slot; slot s is stored at replica index s // 4. Request r attends to its first kv_lengths[r] cached positions; some request holds all 32.
All inputs are finite; a program needn't handle non-finite values.
Results may differ from the reference program's by a relative error of at most 0.0092.
Values may be sent and summed in bfloat16 or wider, within the bound.
No kernel may reach another device: no remote copies, remote signals or barrier semaphores. Data moves between devices by JAX's collectives and lax.ppermute only.
A program may use at most 128 MiB of HBM per device.

```python
import math
import jax
import jax.numpy as jnp
import numpy as np
from jax import lax

D = 8192
HEADS = 64
HD = 128
KVS = 8
RANK = 64
LEN = 32
QW = 8192
REQS = 64
ADAPTERS = 8


def draw_keys(key, part):
    first = jax.random.fold_in(key, 11)
    drawn_projection = jax.random.normal(first, (REQS, KVS, LEN, HD), jnp.float32)
    return drawn_projection.astype(jnp.bfloat16)


def draw_kv_lengths(key, part):
    lengths = jax.random.randint(jax.random.fold_in(key, 21), (REQS,), 1, LEN + 1, dtype=jnp.int32)
    return lengths.at[0].set(LEN)


def place_ends(array, rng, least, largest):
    shape = array.shape
    spot = [jax.random.randint(jax.random.fold_in(rng, axis), (), 0, shape[axis]) for axis in range(len(shape))]
    array = array.at[tuple(spot)].set(least)
    longest = shape.index(max(shape))
    spot[longest] = (spot[longest] + 1) % shape[longest]
    return array.at[tuple(spot)].set(largest)


def strengthened(array, stream_key, source, target, shards_of, factor):
    def block_of(dim):
        return (jnp.arange(array.shape[dim]) // (array.shape[dim] // shards_of)).reshape((-1,) + (1,) * (array.ndim - 1 - dim))

    near = jax.random.permutation(stream_key, shards_of)[block_of(target)]
    second = (block_of(target) + shards_of // 2) % shards_of
    return jnp.where((block_of(source) == near) | (block_of(source) == second), factor * array, array)


def block_levels(own_key, shape, shards, smallest, high):
    loudness = 1.0
    for dim, parts in shards:
        draws = jax.random.uniform(jax.random.fold_in(jax.random.fold_in(own_key, 6), dim), (parts,), jnp.float32, smallest / len(shards), high / len(shards))
        loudness = loudness * jnp.repeat(jnp.exp(draws), shape[dim] // parts).reshape((-1,) + (1,) * (len(shape) - 1 - dim))
    return loudness


def rank_bounds(number_of, skew):
    portions = [(1 << 20) // math.isqrt(standing ** skew) + 1 for standing in range(1, number_of + 1)]
    spread = 1 + sum(portions) // (1 << 30)
    return np.cumsum(np.array([max(1, weight // spread) for weight in portions]))


def skewed_ids(stream_key, shape, count, slope):
    table = rank_bounds(count, slope)
    ticket = jax.random.randint(jax.random.fold_in(stream_key, 1), shape, 0, int(table[count - 1]))
    standing = jnp.searchsorted(jnp.asarray(table, jnp.int32), ticket, side="right")
    return jax.random.permutation(jax.random.fold_in(stream_key, 2), count)[standing].astype(jnp.int32)


def noise(stream_key, dims, spread, bound, split=(), kind=jnp.bfloat16):
    loudness = block_levels(stream_key, dims, split, -0.22, 0.18) if split else 1.0
    drawn = jax.random.normal(stream_key, dims, jnp.float32) * spread * loudness
    return jnp.minimum(jnp.maximum(drawn, -bound), bound).astype(kind)


def bell_draw_with(key, shape, deviation, most, shards, heavy, kind=jnp.bfloat16):
    result = deviation * jax.random.normal(key, shape, jnp.float32)
    if shards:
        result = result * block_levels(key, shape, shards, -0.22, 0.18)
    return jnp.clip(strengthened(result, jax.random.fold_in(key, 3), *heavy), -most, most).astype(kind)


def setup_inputs(seed: int = 0, part: int = 0) -> dict:
    streams_of = jax.random.split(jax.random.key(seed), 13)
    part_keys = jax.random.split(jax.random.fold_in(streams_of[12], part), 13)
    return {
        "hidden": noise(part_keys[0], (REQS, D), 1.0, 6.0, ((0, 2), (1, 8))),
        "w_query": noise(streams_of[1], (D, QW), D ** -0.5, 0.0625, ((1, 8),)),
        "output_weight": bell_draw_with(streams_of[2], (QW, D), QW ** -0.5, 0.09375, ((0, 8),), (0, 1, 8, 2.0)),
        "keys": draw_keys(jax.random.fold_in(jax.random.fold_in(streams_of[12], part), 71), part),
        "values": noise(part_keys[4], (REQS, KVS, LEN, HD), 1.0, 6.0, ((0, 2),)),
        "query_down_maps": noise(part_keys[5], (ADAPTERS, RANK, D), D ** -0.5, 0.0625, ((0, 2), (2, 8))),
        "query_up_maps": noise(part_keys[6], (ADAPTERS, RANK, QW), RANK ** -0.5, 0.75, ((0, 2), (2, 8))),
        "output_down_maps": noise(part_keys[7], (ADAPTERS, RANK, QW), QW ** -0.5, 0.0625, ((0, 2), (2, 8))),
        "output_up_maps": noise(part_keys[8], (ADAPTERS, RANK, D), RANK ** -0.5, 0.75, ((0, 2), (2, 8))),
        "adapter_ids": place_ends(skewed_ids(part_keys[9], (REQS,), ADAPTERS, 2), jax.random.fold_in(part_keys[9], 3), 0, ADAPTERS - 1).astype(jnp.int32),
        "owner_map": jax.random.permutation(part_keys[10], ADAPTERS).astype(jnp.int32),
        "kv_lengths": draw_kv_lengths(jax.random.fold_in(jax.random.fold_in(streams_of[12], part), 71), part),
    }


def reference(hidden, w_query, output_weight, keys, values, query_down_maps, query_up_maps, output_down_maps, output_up_maps, adapter_ids, owner_map, kv_lengths):
    slot = owner_map[adapter_ids].astype(jnp.int32)
    pick = (slot[:, None] == jnp.arange(ADAPTERS, dtype=jnp.int32)[None, :]).astype(jnp.float32)

    def adapter_delta(input_rows, down_product, up_product):
        part = jnp.einsum('ah,fth->aft', input_rows.astype(jnp.float32), down_product.astype(jnp.float32))
        low = lax.optimization_barrier(jnp.sum(pick[:, :, None] * part, axis=1)).astype(jnp.bfloat16)
        spread_rows = pick[:, :, None] * low.astype(jnp.float32)[:, None, :]
        return jnp.einsum('xpl,ply->xy', spread_rows, up_product.astype(jnp.float32))
    plain_projection = jnp.dot(hidden, w_query, preferred_element_type=jnp.float32)
    query_rows = (plain_projection + 0.5 * adapter_delta(hidden, query_down_maps, query_up_maps)).astype(jnp.bfloat16)
    heads_q = query_rows.astype(jnp.float32).reshape(REQS, KVS, HEADS // KVS, HD)
    scores = jnp.einsum('rkhd,rkld->rkhl', heads_q, keys.astype(jnp.float32)) / math.sqrt(HD)
    live = jnp.arange(LEN, dtype=jnp.int32)[None, None, None, :] < kv_lengths[:, None, None, None]
    scores = jnp.where(live, scores, -1e+30)
    top = lax.optimization_barrier(jnp.max(scores, axis=-1, keepdims=True))
    weights = jnp.exp(scores - top)
    probs = (weights / lax.optimization_barrier(jnp.sum(weights, axis=-1, keepdims=True))).astype(jnp.bfloat16)
    combined_output = jnp.einsum('rkhl,rkld->rkhd', probs.astype(jnp.float32), values.astype(jnp.float32))
    combined_output = combined_output.astype(jnp.bfloat16).reshape(REQS, QW)
    final_output = jnp.dot(combined_output, output_weight, preferred_element_type=jnp.float32) + 0.5 * adapter_delta(combined_output, output_down_maps, output_up_maps)
    return final_output.astype(jnp.bfloat16)
```

```python
import math

import jax
import jax.numpy as jnp
from jax import lax
from jax.sharding import PartitionSpec as P

HEADS = 64
KVS = 8


def per_device(
    mesh_shape,
    hidden,
    w_query,
    output_weight,
    keys,
    values,
    query_down_maps,
    query_up_maps,
    output_down_maps,
    output_up_maps,
    adapter_ids,
    owner_map,
    kv_lengths,
):
    rows, width = hidden.shape
    head_size = keys.shape[3]
    shards = mesh_shape["tensor"]
    stored = query_down_maps.shape[0]
    replica_at = lax.axis_index("replica")
    tensor_at = lax.axis_index("tensor")
    bits = []
    while (1 << len(bits)) < shards:
        bits.append(1 << len(bits))
    bits.reverse()

    def across(x, bit):
        return lax.ppermute(x, "tensor", [(i, i ^ bit) for i in range(shards)])

    def swapped(x):
        others = mesh_shape["replica"]
        return [
            lax.ppermute(x, "replica", [(i, (i + k) % others) for i in range(others)])
            for k in range(1, others)
        ]

    def all_sum(x):
        for bit in bits:
            x = x + across(x, bit)
        return x

    id_table = lax.broadcasted_iota(jnp.int32, (1, owner_map.shape[0]), 1)
    slots_all = jnp.sum(jnp.where(adapter_ids[:, None] == id_table, owner_map[None, :], 0), axis=1)
    slots = lax.dynamic_slice_in_dim(slots_all, replica_at * rows, rows)

    def picks(k):
        base = ((replica_at - k) % mesh_shape["replica"]) * stored
        return slots[:, None] == base + lax.broadcasted_iota(jnp.int32, (1, stored), 1)

    def low_part(x, downs):
        total = 0.0
        for k, down in enumerate(downs):
            part = jnp.einsum("ah,fth->aft", x, down, preferred_element_type=jnp.float32)
            total = total + jnp.sum(jnp.where(picks(k)[:, :, None], part, 0.0), axis=1)
        return total

    def lora(low, ups):
        total = 0.0
        for k, up in enumerate(ups):
            spread = jnp.where(picks(k)[:, :, None], low[:, None, :], 0)
            total = total + jnp.einsum("xpl,ply->xy", spread, up, preferred_element_type=jnp.float32)
        return total

    query_down = [query_down_maps] + swapped(query_down_maps)
    query_up = [query_up_maps] + swapped(query_up_maps)
    output_down = [output_down_maps] + swapped(output_down_maps)
    output_up = [output_up_maps] + swapped(output_up_maps)

    chunks = {0: hidden}
    for bit in bits:
        for k in list(chunks):
            chunks[k | bit] = across(chunks[k], bit)
    low = all_sum(low_part(hidden, query_down)).astype(jnp.bfloat16)
    query = 0.0
    for k in chunks:
        w = lax.dynamic_slice_in_dim(w_query, (tensor_at ^ k) * width, width, 0)
        query = query + jnp.dot(chunks[k], w, preferred_element_type=jnp.float32)
    query_rows = (query + 0.5 * lora(low, query_up)).astype(jnp.bfloat16)

    local_heads = query_rows.shape[1] // head_size
    group = HEADS // KVS
    kv_count = max(1, local_heads // group)
    first_kv = tensor_at * local_heads // group
    key_block = lax.dynamic_slice_in_dim(keys, first_kv, kv_count, 1)
    value_block = lax.dynamic_slice_in_dim(values, first_kv, kv_count, 1)
    heads_q = query_rows.reshape(rows, kv_count, local_heads // kv_count, head_size)
    scores = jnp.einsum(
        "rkhd,rkld->rkhl", heads_q, key_block, preferred_element_type=jnp.float32
    ) / math.sqrt(head_size)
    live = (
        lax.broadcasted_iota(jnp.int32, (rows, 1, 1, keys.shape[2]), 3)
        < kv_lengths[:, None, None, None]
    )
    scores = jnp.where(live, scores, -1e30)
    top = jnp.max(scores, axis=-1, keepdims=True)
    weights = jnp.exp(scores - top)
    probs = (weights / jnp.sum(weights, axis=-1, keepdims=True)).astype(jnp.bfloat16)
    mixed = jnp.einsum("rkhl,rkld->rkhd", probs, value_block, preferred_element_type=jnp.float32)
    mixed = mixed.astype(jnp.bfloat16).reshape(rows, -1)

    out_width = output_weight.shape[1] // shards
    parts = {}
    for k in reversed(list(chunks)):
        w = lax.dynamic_slice_in_dim(output_weight, (tensor_at ^ k) * out_width, out_width, 1)
        parts[k] = jnp.dot(mixed, w, preferred_element_type=jnp.float32)
    low = all_sum(low_part(mixed, output_down)).astype(jnp.bfloat16)
    for bit in reversed(bits):
        for k in list(parts):
            if k & bit:
                came = across(parts.pop(k).astype(jnp.bfloat16), bit)
                parts[k ^ bit] = parts[k ^ bit] + came.astype(jnp.float32)
    return (parts[0] + 0.5 * lora(low, output_up)).astype(jnp.bfloat16)


def solution(mesh):
    sizes = dict(mesh.shape)

    def body(*arrays):
        return per_device(sizes, *arrays)

    return jax.shard_map(
        body,
        mesh=mesh,
        in_specs=(
            P(("groups", "replica"), "tensor"),
            P(None, "tensor"),
            P("tensor", None),
            P(("groups", "replica"), None, None, None),
            P(("groups", "replica"), None, None, None),
            P(("groups", "replica"), None, "tensor"),
            P(("groups", "replica"), None, "tensor"),
            P(("groups", "replica"), None, "tensor"),
            P(("groups", "replica"), None, "tensor"),
            P("groups"),
            P("groups"),
            P(("groups", "replica")),
        ),
        out_specs=P(("groups", "replica"), "tensor"),
        check_vma=False,
    )
```

```python
import functools
import math

import jax
import jax.numpy as jnp
from jax import lax
from jax.experimental import pallas as pl
from jax.experimental.pallas import tpu as pltpu
from jax.sharding import PartitionSpec as P

HEADS = 64
KVS = 8
VMEM = pl.BlockSpec(memory_space=pltpu.VMEM)
SMEM = pl.BlockSpec(memory_space=pltpu.SMEM)
ANY = pl.BlockSpec(memory_space=pl.ANY)
LANES = 128
PIECES = 2


def dot(a, b):
    return jnp.dot(a, b, preferred_element_type=jnp.float32)


def dot_t(a, b):
    return lax.dot_general(a, b, (((1,), (1,)), ((), ())), preferred_element_type=jnp.float32)


def params(flops_bytes, limit):
    return dict(
        compiler_params=pltpu.CompilerParams(vmem_limit_bytes=limit),
        cost_estimate=pl.CostEstimate(
            flops=flops_bytes[0], bytes_accessed=flops_bytes[1], transcendentals=0
        ),
    )


def low_of(x, downs, picks):
    total = 0.0
    at = 0
    for down in downs:
        wide = down.shape[0]
        part = dot_t(x, down[...]) * picks[:, at : at + wide]
        for g in range(0, wide, LANES):
            total = total + part[:, g : g + LANES]
        at += wide
    return total


def lora_of(low, ups, picks):
    total = 0.0
    at = 0
    low = low.astype(jnp.bfloat16).astype(jnp.float32)
    for up in ups:
        wide = up.shape[0]
        spread = jnp.concatenate([low] * (wide // LANES), axis=1) * picks[:, at : at + wide]
        total = total + dot(spread.astype(jnp.bfloat16), up[...])
        at += wide
    return total


def low_kernel(count, x_ref, picks_ref, *rest):
    downs, out_ref = rest[:count], rest[count]
    out_ref[...] = low_of(x_ref[...], downs, picks_ref[...])


def low_call(x, picks, downs):
    return pl.pallas_call(
        functools.partial(low_kernel, len(downs)),
        in_specs=[VMEM] * (2 + len(downs)),
        out_specs=VMEM,
        out_shape=jax.ShapeDtypeStruct((x.shape[0], LANES), jnp.float32),
        name="low",
        **params((10**8, 10**6), 8 << 20),
    )(x, picks, *downs)


def weight_copies(weight, buf, sems, j, at_ref, along):
    depth, wide = buf.shape[1], buf.shape[2]
    piece = depth // PIECES
    copies = []
    for p in range(PIECES):
        if along == 0:
            src = weight.at[pl.ds(pl.multiple_of(at_ref[j] * depth + p * piece, piece), piece), :]
        else:
            src = weight.at[p * piece : (p + 1) * piece, pl.ds(pl.multiple_of(at_ref[j] * wide, LANES), wide)]
        copies.append(
            pltpu.make_async_copy(src, buf.at[j, p * piece : (p + 1) * piece, :], sems.at[j, p])
        )
    return copies


def block_dot(x_ref_read, buf, j, copies, total):
    piece = buf.shape[1] // PIECES
    for p in range(PIECES):
        copies[p].wait()
        total = total + dot(
            x_ref_read(p * piece, piece), buf[j, p * piece : (p + 1) * piece, :]
        )
    return total


def project_kernel(count, first, at_ref, *rest):
    chunks, rest = rest[:count], rest[count:]
    weight, rest = rest[0], rest[1:]
    if first:
        total = 0.0
    else:
        total, rest = rest[0][...], rest[1:]
    out_ref, buf, sems = rest
    copies = [weight_copies(weight, buf, sems, j, at_ref, 0) for j in range(count)]
    for pieces in copies:
        for c in pieces:
            c.start()
    for j in range(count):
        total = block_dot(lambda a, n, j=j: chunks[j][:, a : a + n], buf, j, copies[j], total)
    out_ref[...] = total


def project_call(chunks, at, weight, before):
    rows, width = chunks[0].shape
    wide = weight.shape[1]
    count = len(chunks)
    extra = [] if before is None else [before]
    return pl.pallas_call(
        functools.partial(project_kernel, count, before is None),
        in_specs=[SMEM] + [VMEM] * count + [ANY] + [VMEM] * len(extra),
        out_specs=VMEM,
        out_shape=jax.ShapeDtypeStruct((rows, wide), jnp.float32),
        scratch_shapes=[
            pltpu.VMEM((count, width, wide), weight.dtype),
            pltpu.SemaphoreType.DMA((count, PIECES)),
        ],
        name="project%d" % count,
        **params(
            (2 * count * rows * width * wide, 2 * count * width * wide),
            (2 * count * width * wide) + (8 << 20),
        ),
    )(at, *chunks, weight, *extra)


def mix_kernel(sizes, *refs):
    n_in, n_out, maps, kv_count, group, head = sizes
    refs = list(refs)
    at_in, at_out, at_kv = refs.pop(0), refs.pop(0), refs.pop(0)
    chunks = [refs.pop(0) for _ in range(n_in)]
    w_in, w_out, before = refs.pop(0), refs.pop(0), refs.pop(0)
    low, picks = refs.pop(0), refs.pop(0)
    ups = [refs.pop(0) for _ in range(maps)]
    downs = [refs.pop(0) for _ in range(maps)]
    keys, values, live = refs.pop(0), refs.pop(0), refs.pop(0)
    outs = [refs.pop(0) for _ in range(n_out)]
    low_out, mixed_out = refs.pop(0), refs.pop(0)
    buf_in, sem_in, buf_out, sem_out, k_buf, v_buf, kv_sem = refs

    copies_in = [weight_copies(w_in, buf_in, sem_in, j, at_in, 0) for j in range(n_in)]
    copies_out = [weight_copies(w_out, buf_out, sem_out, j, at_out, 1) for j in range(n_out)]
    kv = pl.ds(at_kv[0], kv_count)
    k_copy = pltpu.make_async_copy(keys.at[:, kv], k_buf, kv_sem.at[0])
    v_copy = pltpu.make_async_copy(values.at[:, kv], v_buf, kv_sem.at[1])
    for pieces in copies_in:
        for c in pieces:
            c.start()
    k_copy.start()
    v_copy.start()
    for pieces in copies_out:
        for c in pieces:
            c.start()

    rows = before.shape[0]
    picked = picks[...]
    total = before[...] + 0.5 * lora_of(low[...], ups, picked)
    for j in range(n_in):
        total = block_dot(lambda a, n, j=j: chunks[j][:, a : a + n], buf_in, j, copies_in[j], total)
    query = total.astype(jnp.bfloat16)
    k_copy.wait()
    v_copy.wait()
    length = k_buf.shape[2]
    heads = [None] * (kv_count * group)
    alive = jnp.concatenate([live[...]] * group, axis=0) > 0
    for kvh in range(kv_count):
        flat_k = k_buf[:, kvh].reshape(rows * length, head)
        flat_v = v_buf[:, kvh].reshape(rows * length, head)
        q = jnp.concatenate(
            [query[:, (kvh * group + g) * head : (kvh * group + g + 1) * head] for g in range(group)],
            axis=0,
        )
        scores = dot_t(q, flat_k) / math.sqrt(head)
        scores = jnp.where(alive, scores, -1e30)
        top = jnp.max(scores, axis=1, keepdims=True)
        weights = jnp.exp(scores - top)
        probs = (weights / jnp.sum(weights, axis=1, keepdims=True)).astype(jnp.bfloat16)
        got = dot(probs, flat_v).astype(jnp.bfloat16)
        for g in range(group):
            heads[kvh * group + g] = got[g * rows : (g + 1) * rows]
    mixed = jnp.concatenate(heads, axis=1)
    mixed_out[...] = mixed
    low_out[...] = low_of(mixed, downs, picked)
    for j in range(n_out):
        block = block_dot(lambda a, n: mixed[:, a : a + n], buf_out, j, copies_out[j], 0.0)
        outs[j][...] = block.astype(outs[j].dtype)


def out_kernel(count, at_ref, x_ref, weight, *rest):
    outs, (buf, sems) = rest[:count], rest[count:]
    copies = [weight_copies(weight, buf, sems, j, at_ref, 1) for j in range(count)]
    for pieces in copies:
        for c in pieces:
            c.start()
    for j in range(count):
        outs[j][...] = block_dot(lambda a, n: x_ref[:, a : a + n], buf, j, copies[j], 0.0)


def final_kernel(count, maps, low_ref, picks_ref, *rest):
    ups, rest = rest[:maps], rest[maps:]
    terms, out_ref = rest[:count], rest[count]
    total = 0.5 * lora_of(low_ref[...], ups, picks_ref[...])
    for t in terms:
        total = total + t[...].astype(jnp.float32)
    out_ref[...] = total.astype(out_ref.dtype)


def per_device(
    mesh_shape,
    hidden,
    w_query,
    output_weight,
    keys,
    values,
    query_down_maps,
    query_up_maps,
    output_down_maps,
    output_up_maps,
    adapter_ids,
    owner_map,
    kv_lengths,
):
    rows, width = hidden.shape
    head = keys.shape[3]
    length = keys.shape[2]
    shards = mesh_shape["tensor"]
    replicas = mesh_shape["replica"]
    stored, rank = query_down_maps.shape[:2]
    replica_at = lax.axis_index("replica")
    tensor_at = lax.axis_index("tensor")
    bits = []
    while (1 << len(bits)) < shards:
        bits.append(1 << len(bits))
    bits.reverse()

    def across(x, bit):
        return lax.ppermute(x, "tensor", [(i, i ^ bit) for i in range(shards)])

    def with_swapped(x):
        x = x.reshape(stored * rank, x.shape[2])
        return [x] + [
            lax.ppermute(x, "replica", [(i, (i + k) % replicas) for i in range(replicas)])
            for k in range(1, replicas)
        ]

    def all_sum(x):
        for bit in bits:
            x = x + across(x, bit)
        return x

    def at(ks):
        return jnp.stack([tensor_at ^ k for k in ks]).astype(jnp.int32)

    id_table = lax.broadcasted_iota(jnp.int32, (1, owner_map.shape[0]), 1)
    slots_all = jnp.sum(jnp.where(adapter_ids[:, None] == id_table, owner_map[None, :], 0), axis=1)
    slots = lax.dynamic_slice_in_dim(slots_all, replica_at * rows, rows)
    lane = lax.broadcasted_iota(jnp.int32, (1, stored * rank), 1) // rank
    picks = jnp.concatenate(
        [
            (slots[:, None] == ((replica_at - k) % replicas) * stored + lane).astype(jnp.float32)
            for k in range(replicas)
        ],
        axis=1,
    )
    column = lax.broadcasted_iota(jnp.int32, (rows, rows * length), 1)
    row = lax.broadcasted_iota(jnp.int32, (rows, rows * length), 0)
    live = ((column // length == row) & (column % length < kv_lengths[:, None])).astype(jnp.float32)

    query_down = with_swapped(query_down_maps)
    query_up = with_swapped(query_up_maps)
    output_down = with_swapped(output_down_maps)
    output_up = with_swapped(output_up_maps)

    chunks = {0: hidden}
    for bit in bits:
        for k in list(chunks):
            chunks[k | bit] = across(chunks[k], bit)
    low = all_sum(low_call(hidden, picks, query_down))

    order = sorted(chunks, key=lambda k: (bin(k).count("1"), -k))
    last = order[-1:]
    early = order[:-1]
    cuts = [early[:1], early[1:4], early[4:]] if len(early) == 7 else [early[i : i + 8] for i in range(0, len(early), 8)]
    query = None
    for ks in cuts:
        query = project_call([chunks[k] for k in ks], at(ks), w_query, query)

    local_heads = w_query.shape[1] // head
    group_all = HEADS // KVS
    kv_count = max(1, local_heads // group_all)
    group = local_heads // kv_count
    first_kv = (tensor_at * local_heads // group_all).astype(jnp.int32).reshape(1)
    out_width = output_weight.shape[1] // shards
    depth = output_weight.shape[0]
    sent = [k for k in reversed(order) if k & 1]
    head_of = sent[:2]
    tail_of = [k for k in reversed(order) if k not in head_of]
    n_in, n_out = len(last), len(head_of)
    wide = w_query.shape[1]
    results = pl.pallas_call(
        functools.partial(mix_kernel, (n_in, n_out, replicas, kv_count, group, head)),
        in_specs=[SMEM] * 3
        + [VMEM] * n_in
        + [ANY] * 2
        + [VMEM] * 3
        + [VMEM] * (2 * replicas)
        + [ANY] * 2
        + [VMEM],
        out_specs=[VMEM] * (n_out + 2),
        out_shape=[jax.ShapeDtypeStruct((rows, out_width), jnp.bfloat16)] * n_out
        + [
            jax.ShapeDtypeStruct((rows, LANES), jnp.float32),
            jax.ShapeDtypeStruct((rows, wide), jnp.bfloat16),
        ],
        scratch_shapes=[
            pltpu.VMEM((n_in, width, wide), w_query.dtype),
            pltpu.SemaphoreType.DMA((n_in, PIECES)),
            pltpu.VMEM((n_out, depth, out_width), output_weight.dtype),
            pltpu.SemaphoreType.DMA((n_out, PIECES)),
            pltpu.VMEM((rows, kv_count, length, head), keys.dtype),
            pltpu.VMEM((rows, kv_count, length, head), values.dtype),
            pltpu.SemaphoreType.DMA((2,)),
        ],
        name="mix",
        **params((10**9, 6 << 20), 32 << 20),
    )(
        at(last),
        at(head_of),
        first_kv,
        *[chunks[k] for k in last],
        w_query,
        output_weight,
        query,
        low,
        picks,
        *query_up,
        *output_down,
        keys,
        values,
        live,
    )
    parts = dict(zip(head_of, results[:n_out]))
    low2, mixed = results[n_out:]
    for i in range(0, len(tail_of), 6):
        ks = tail_of[i : i + 6]
        blocks = pl.pallas_call(
            functools.partial(out_kernel, len(ks)),
            in_specs=[SMEM, VMEM, ANY],
            out_specs=[VMEM] * len(ks),
            out_shape=[jax.ShapeDtypeStruct((rows, out_width), jnp.float32)] * len(ks),
            scratch_shapes=[
                pltpu.VMEM((len(ks), depth, out_width), output_weight.dtype),
                pltpu.SemaphoreType.DMA((len(ks), PIECES)),
            ],
            name="out%d" % len(ks),
            **params((2 * len(ks) * rows * depth * out_width, 2 * len(ks) * depth * out_width), 24 << 20),
        )(at(ks), mixed, output_weight)
        parts.update(zip(ks, blocks))
    low2 = all_sum(low2)
    terms = []
    for bit in reversed(bits):
        for k in [k for k in reversed(order) if k in parts and k & bit]:
            came = across(parts.pop(k).astype(jnp.bfloat16), bit)
            if k == bit:
                terms.append(came)
            else:
                parts[k ^ bit] = parts[k ^ bit].astype(jnp.float32) + came.astype(jnp.float32)
    terms.append(parts[0])
    return pl.pallas_call(
        functools.partial(final_kernel, len(terms), replicas),
        in_specs=[VMEM] * (2 + replicas + len(terms)),
        out_specs=VMEM,
        out_shape=jax.ShapeDtypeStruct((rows, out_width), jnp.bfloat16),
        name="final",
        **params((10**8, 10**6), 8 << 20),
    )(low2, picks, *output_up, *terms)


def solution(mesh):
    sizes = dict(mesh.shape)

    def body(*arrays):
        return per_device(sizes, *arrays)

    return jax.shard_map(
        body,
        mesh=mesh,
        in_specs=(
            P(("groups", "replica"), "tensor"),
            P(None, "tensor"),
            P("tensor", None),
            P(("groups", "replica"), None, None, None),
            P(("groups", "replica"), None, None, None),
            P(("groups", "replica"), None, "tensor"),
            P(("groups", "replica"), None, "tensor"),
            P(("groups", "replica"), None, "tensor"),
            P(("groups", "replica"), None, "tensor"),
            P("groups"),
            P("groups"),
            P(("groups", "replica")),
        ),
        out_specs=P(("groups", "replica"), "tensor"),
        check_vma=False,
    )
```

```python
import functools
import math

import jax
import jax.numpy as jnp
from jax import lax
from jax.experimental import pallas as pl
from jax.experimental.pallas import tpu as pltpu
from jax.sharding import PartitionSpec as P

HEADS = 64
KVS = 8
VMEM = pl.BlockSpec(memory_space=pltpu.VMEM)
SMEM = pl.BlockSpec(memory_space=pltpu.SMEM)
HBM = pl.BlockSpec(memory_space=pltpu.HBM)
LANES = 128
PIECES = 2


def dot(a, b):
    return jnp.dot(a, b, preferred_element_type=jnp.float32)


def dot_t(a, b):
    return lax.dot_general(a, b, (((1,), (1,)), ((), ())), preferred_element_type=jnp.float32)


def params(flops_bytes, limit):
    return dict(
        compiler_params=pltpu.CompilerParams(vmem_limit_bytes=limit),
        cost_estimate=pl.CostEstimate(
            flops=flops_bytes[0], bytes_accessed=flops_bytes[1], transcendentals=0
        ),
    )


def low_of(x, downs, picks):
    total = 0.0
    at = 0
    for down in downs:
        wide = down.shape[0]
        part = dot_t(x, down[...]) * picks[:, at : at + wide]
        for g in range(0, wide, LANES):
            total = total + part[:, g : g + LANES]
        at += wide
    return total


def lora_of(low, ups, picks):
    total = 0.0
    at = 0
    low = low.astype(jnp.bfloat16).astype(jnp.float32)
    for up in ups:
        wide = up.shape[0]
        spread = jnp.concatenate([low] * (wide // LANES), axis=1) * picks[:, at : at + wide]
        total = total + dot(spread.astype(jnp.bfloat16), up[...])
        at += wide
    return total


def load_all(pairs, sems):
    copies = [pltpu.make_async_copy(src, dst, sems.at[i]) for i, (src, dst) in enumerate(pairs)]
    for c in copies:
        c.start()
    return copies


def low_kernel(count, x_hbm, picks_ref, *rest):
    downs, out_ref, x_ref, bufs, sems = rest[:count], rest[count], rest[count + 1], rest[count + 2 : -1], rest[-1]
    for c in load_all([(x_hbm, x_ref)] + list(zip(downs, bufs)), sems):
        c.wait()
    out_ref[...] = low_of(x_ref[...], bufs, picks_ref[...])


def low_call(x, picks, downs):
    return pl.pallas_call(
        functools.partial(low_kernel, len(downs)),
        in_specs=[HBM, VMEM] + [HBM] * len(downs),
        out_specs=VMEM,
        out_shape=jax.ShapeDtypeStruct((x.shape[0], LANES), jnp.float32),
        scratch_shapes=[pltpu.VMEM(x.shape, x.dtype)]
        + [pltpu.VMEM(d.shape, d.dtype) for d in downs]
        + [pltpu.SemaphoreType.DMA((1 + len(downs),))],
        name="low",
        **params((10**8, 10**6), 8 << 20),
    )(x, picks, *downs)


def weight_copies(weight, buf, sems, j, block, along):
    depth, wide = buf.shape[1], buf.shape[2]
    piece = depth // PIECES
    copies = []
    for p in range(PIECES):
        if along == 0:
            src = weight.at[pl.ds(pl.multiple_of(block * depth + p * piece, piece), piece), :]
        else:
            src = weight.at[p * piece : (p + 1) * piece, pl.ds(pl.multiple_of(block * wide, LANES), wide)]
        copies.append(
            pltpu.make_async_copy(src, buf.at[j, p * piece : (p + 1) * piece, :], sems.at[j, p])
        )
    return copies


def block_dot(x_ref_read, buf, j, copies, total):
    piece = buf.shape[1] // PIECES
    for p in range(PIECES):
        copies[p].wait()
        total = total + dot(
            x_ref_read(p * piece, piece), buf[j, p * piece : (p + 1) * piece, :]
        )
    return total


def project_kernel(ks, spans, first, tensor_ref, *rest):
    count, given = len(ks), len(set(i for i, _ in spans))
    chunks, rest = rest[:given], rest[given:]
    weight, rest = rest[0], rest[1:]
    if first:
        total = 0.0
    else:
        total, rest = rest[0][...], rest[1:]
    out_ref, buf, sems = rest
    rows = out_ref.shape[0]
    copies = [weight_copies(weight, buf, sems, j, tensor_ref[0] ^ k, 0) for j, k in enumerate(ks)]
    for pieces in copies:
        for c in pieces:
            c.start()
    for j, (i, r) in enumerate(spans):
        total = block_dot(
            lambda a, n, i=i, r=r: chunks[i][r : r + rows, a : a + n], buf, j, copies[j], total
        )
    out_ref[...] = total


def project_call(where, ks, tensor_at, weight, before, rows, width):
    wide = weight.shape[1]
    count = len(ks)
    arrays, spans = [], []
    for k in ks:
        array, r = where[k]
        if not any(a is array for a in arrays):
            arrays.append(array)
        spans.append(([a is array for a in arrays].index(True), r))
    extra = [] if before is None else [before]
    return pl.pallas_call(
        functools.partial(project_kernel, ks, spans, before is None),
        in_specs=[SMEM] + [VMEM] * len(arrays) + [HBM] + [VMEM] * len(extra),
        out_specs=VMEM,
        out_shape=jax.ShapeDtypeStruct((rows, wide), jnp.float32),
        scratch_shapes=[
            pltpu.VMEM((count, width, wide), weight.dtype),
            pltpu.SemaphoreType.DMA((count, PIECES)),
        ],
        name="project%d" % count,
        **params(
            (2 * count * rows * width * wide, 2 * count * width * wide),
            (2 * count * width * wide) + (8 << 20),
        ),
    )(tensor_at, *arrays, weight, *extra)


def mix_kernel(sizes, *refs):
    k_in, k_out, maps, kv_count, group, head, local_heads, group_all, width = sizes
    refs = list(refs)
    tensor_ref, chunk, w_in, w_out, before, low, picks = [refs.pop(0) for _ in range(7)]
    ups = [refs.pop(0) for _ in range(maps)]
    downs = [refs.pop(0) for _ in range(maps)]
    keys, values, live = [refs.pop(0) for _ in range(3)]
    block_out, low_out, mixed_out = [refs.pop(0) for _ in range(3)]
    buf_in, sem_in, buf_out, sem_out, k_buf, v_buf, up_buf, down_buf, sems = refs

    tensor_at = tensor_ref[0]
    copies_in = weight_copies(w_in, buf_in, sem_in, 0, tensor_at ^ k_in, 0)
    copies_out = weight_copies(w_out, buf_out, sem_out, 0, tensor_at ^ k_out, 1)
    kv = pl.ds(tensor_at * local_heads // group_all, kv_count)
    up_copies = load_all([(u, up_buf.at[i]) for i, u in enumerate(ups)], sems.at[0])
    for c in copies_in:
        c.start()
    kv_copies = load_all([(keys.at[:, kv], k_buf), (values.at[:, kv], v_buf)], sems.at[1])
    down_copies = load_all([(d, down_buf.at[i]) for i, d in enumerate(downs)], sems.at[2])
    for c in copies_out:
        c.start()

    rows = before.shape[0]
    picked = picks[...]
    for c in up_copies:
        c.wait()
    total = before[...] + 0.5 * lora_of(low[...], [up_buf.at[i] for i in range(maps)], picked)
    total = block_dot(lambda a, n: chunk[:, a : a + n], buf_in, 0, copies_in, total)
    query = total.astype(jnp.bfloat16)
    for c in kv_copies:
        c.wait()
    length = k_buf.shape[2]
    heads = [None] * (kv_count * group)
    alive = jnp.concatenate([live[...]] * group, axis=0) > 0
    for kvh in range(kv_count):
        flat_k = k_buf[:, kvh].reshape(rows * length, head)
        flat_v = v_buf[:, kvh].reshape(rows * length, head)
        q = jnp.concatenate(
            [query[:, (kvh * group + g) * head : (kvh * group + g + 1) * head] for g in range(group)],
            axis=0,
        )
        scores = dot_t(q, flat_k) / math.sqrt(head)
        scores = jnp.where(alive, scores, -1e30)
        top = jnp.max(scores, axis=1, keepdims=True)
        weights = jnp.exp(scores - top)
        probs = (weights / jnp.sum(weights, axis=1, keepdims=True)).astype(jnp.bfloat16)
        got = dot(probs, flat_v).astype(jnp.bfloat16)
        for g in range(group):
            heads[kvh * group + g] = got[g * rows : (g + 1) * rows]
    mixed = jnp.concatenate(heads, axis=1)
    mixed_out[...] = mixed
    for c in down_copies:
        c.wait()
    low_part = low_of(mixed, [down_buf.at[i] for i in range(maps)], picked)
    low_out[...] = low_part
    block = block_dot(lambda a, n: mixed[:, a : a + n], buf_out, 0, copies_out, 0.0)
    wide = block.shape[1]
    block_out[:, :wide] = block.astype(block_out.dtype)
    block_out[:, wide:] = low_part.astype(block_out.dtype)


def out_kernel(ks, spans, tensor_ref, x_ref, weight, *rest):
    outs, (buf, sems) = rest[:-2], rest[-2:]
    rows = x_ref.shape[0]
    copies = [weight_copies(weight, buf, sems, j, tensor_ref[0] ^ k, 1) for j, k in enumerate(ks)]
    for pieces in copies:
        for c in pieces:
            c.start()
    for j, (i, r) in enumerate(spans):
        block = block_dot(lambda a, n: x_ref[:, a : a + n], buf, j, copies[j], 0.0)
        outs[i][r : r + rows, :] = block.astype(outs[i].dtype)


def out_call(groups, tensor_at, mixed, weight, out_width):
    rows, depth = mixed.shape
    ks = [k for group, _ in groups for k in group]
    spans = [(i, r * rows) for i, (group, _) in enumerate(groups) for r in range(len(group))]
    return pl.pallas_call(
        functools.partial(out_kernel, ks, spans),
        in_specs=[SMEM, VMEM, HBM],
        out_specs=[VMEM] * len(groups),
        out_shape=[jax.ShapeDtypeStruct((rows * len(group), out_width), kind) for group, kind in groups],
        scratch_shapes=[
            pltpu.VMEM((len(ks), depth, out_width), weight.dtype),
            pltpu.SemaphoreType.DMA((len(ks), PIECES)),
        ],
        name="out%d" % len(ks),
        **params((2 * len(ks) * rows * depth * out_width, 2 * len(ks) * depth * out_width), 24 << 20),
    )(tensor_at, mixed, weight)


def final_kernel(wide, count, maps, picks_ref, low_ref, *rest):
    ups, rest = rest[:maps], rest[maps:]
    lows, rest = rest[: count[0]], rest[count[0] :]
    terms, rest = rest[: count[1]], rest[count[1] :]
    out_ref, up_buf, sems = rest
    copies = load_all([(u, up_buf.at[i]) for i, u in enumerate(ups)], sems)
    low = low_ref[...]
    total = 0.0
    for ref in lows:
        low = low + ref[:, wide:].astype(jnp.float32)
    total = lows[-1][:, :wide].astype(jnp.float32)
    for t in terms:
        total = total + t[:, :wide].astype(jnp.float32)
    for c in copies:
        c.wait()
    total = total + 0.5 * lora_of(low, [up_buf.at[i] for i in range(maps)], picks_ref[...])
    out_ref[...] = total.astype(out_ref.dtype)


def low_bit(k):
    return k & -k


def per_device(
    mesh_shape,
    hidden,
    w_query,
    output_weight,
    keys,
    values,
    query_down_maps,
    query_up_maps,
    output_down_maps,
    output_up_maps,
    adapter_ids,
    owner_map,
    kv_lengths,
):
    rows, width = hidden.shape
    head = keys.shape[3]
    length = keys.shape[2]
    shards = mesh_shape["tensor"]
    replicas = mesh_shape["replica"]
    stored, rank = query_down_maps.shape[:2]
    replica_at = lax.axis_index("replica")
    tensor_at = lax.axis_index("tensor").astype(jnp.int32).reshape(1)
    bits = []
    while (1 << len(bits)) < shards:
        bits.append(1 << len(bits))

    def across(x, bit):
        return lax.ppermute(x, "tensor", [(i, i ^ bit) for i in range(shards)])

    def with_swapped(x):
        x = x.reshape(stored * rank, x.shape[2])
        return [x] + [
            lax.ppermute(x, "replica", [(i, (i + k) % replicas) for i in range(replicas)])
            for k in range(1, replicas)
        ]

    id_table = lax.broadcasted_iota(jnp.int32, (1, owner_map.shape[0]), 1)
    slots_all = jnp.sum(jnp.where(adapter_ids[:, None] == id_table, owner_map[None, :], 0), axis=1)
    slots = lax.dynamic_slice_in_dim(slots_all, replica_at * rows, rows)
    lane = lax.broadcasted_iota(jnp.int32, (1, stored * rank), 1) // rank
    picks = jnp.concatenate(
        [
            (slots[:, None] == ((replica_at - k) % replicas) * stored + lane).astype(jnp.float32)
            for k in range(replicas)
        ],
        axis=1,
    )
    column = lax.broadcasted_iota(jnp.int32, (rows, rows * length), 1)
    row = lax.broadcasted_iota(jnp.int32, (rows, rows * length), 0)
    live = ((column // length == row) & (column % length < kv_lengths[:, None])).astype(jnp.float32)

    query_down = with_swapped(query_down_maps)
    query_up = with_swapped(query_up_maps)
    output_down = with_swapped(output_down_maps)
    output_up = with_swapped(output_up_maps)

    low = low_call(hidden, picks, query_down)
    where = {0: (hidden, 0)}
    chain = 0
    for bit in reversed(bits):
        held = list(where)
        if chain == 0:
            where[bit] = (across(hidden, bit), 0)
            low = low + across(low, bit)
        else:
            array, r = where[chain]
            joined = jnp.concatenate([array[r : r + rows, :width], low.astype(jnp.bfloat16)], axis=1)
            got = across(joined, bit)
            where[chain | bit] = (got, 0)
            low = low + got[:, width:].astype(jnp.float32)
        rest = [k for k in held if k not in (0, chain)]
        if chain != 0:
            where[bit] = (across(hidden, bit), 0)
            if bit == 1 and len(rest) <= 2:
                rest = rest + [k for k in held if k not in rest + [0, chain]]
        if len(rest) == 1 or (rest and bit != 1):
            for k in rest:
                array, r = where[k]
                where[k | bit] = (across(array[r : r + rows, :width], bit), 0)
        elif rest:
            got = across(jnp.concatenate([where[k][0][where[k][1] : where[k][1] + rows, :width] for k in rest], axis=0), bit)
            for i, k in enumerate(rest):
                where[k | bit] = (got, i * rows)
        chain |= bit

    top = bits[-1] if bits else 0
    order = sorted(where, key=lambda k: (bin(k).count("1"), -k))
    last = order[-1]
    early = order[:-1]
    first = [k for k in early if k in (0, top, top >> 1)]
    others = [k for k in early if k not in first]
    query = project_call(where, first, tensor_at, w_query, None, rows, width)
    for i in range(0, len(others), 6):
        query = project_call(where, others[i : i + 6], tensor_at, w_query, query, rows, width)

    wide = w_query.shape[1]
    local_heads = wide // head
    group_all = HEADS // KVS
    kv_count = max(1, local_heads // group_all)
    group = local_heads // kv_count
    out_width = output_weight.shape[1] // shards
    depth = output_weight.shape[0]
    whole = shards - 1
    sizes = (last, whole, replicas, kv_count, group, head, local_heads, group_all, width)
    map_in, map_out = (stored * rank, wide), (stored * rank, depth)
    payload, low2, mixed = pl.pallas_call(
        functools.partial(mix_kernel, sizes),
        in_specs=[SMEM, VMEM, HBM, HBM, VMEM, VMEM, VMEM] + [HBM] * (2 * replicas) + [HBM, HBM, VMEM],
        out_specs=[VMEM] * 3,
        out_shape=[
            jax.ShapeDtypeStruct((rows, out_width + LANES), jnp.bfloat16),
            jax.ShapeDtypeStruct((rows, LANES), jnp.float32),
            jax.ShapeDtypeStruct((rows, wide), jnp.bfloat16),
        ],
        scratch_shapes=[
            pltpu.VMEM((1, width, wide), w_query.dtype),
            pltpu.SemaphoreType.DMA((1, PIECES)),
            pltpu.VMEM((1, depth, out_width), output_weight.dtype),
            pltpu.SemaphoreType.DMA((1, PIECES)),
            pltpu.VMEM((rows, kv_count, length, head), keys.dtype),
            pltpu.VMEM((rows, kv_count, length, head), values.dtype),
            pltpu.VMEM((replicas,) + map_in, keys.dtype),
            pltpu.VMEM((replicas,) + map_out, keys.dtype),
            pltpu.SemaphoreType.DMA((3, max(2, replicas))),
        ],
        name="mix",
        **params((10**9, 6 << 20), 32 << 20),
    )(
        tensor_at,
        where[last][0],
        w_query,
        output_weight,
        query,
        low,
        picks,
        *query_up,
        *output_down,
        keys,
        values,
        live,
    )

    came = {whole: payload}
    chain = [whole]
    while chain[-1]:
        chain.append(chain[-1] & (chain[-1] - 1))
    odd = [k for k in sorted(where, reverse=True) if k & 1 and k != whole]
    joined = [odd[:1], odd[1:]] if 1 < len(odd) <= 3 else [[k] for k in odd]
    joined = [g for g in joined if g]
    even = [k for k in sorted(where, reverse=True) if not k & 1]
    parts = {}
    plan = [(g, jnp.bfloat16) for g in joined] + [([k], jnp.float32) for k in even]
    sent = {}
    for i in range(0, len(plan), 8):
        some = plan[i : i + 8]
        for (g, kind), array in zip(some, out_call(some, tensor_at, mixed, output_weight, out_width)):
            if kind == jnp.bfloat16:
                sent[tuple(g)] = array
            else:
                parts[g[0]] = array
    came[whole] = across(payload, 1)
    for g, array in sent.items():
        got = across(array, 1)
        for i, k in enumerate(g):
            came[k] = got[i * rows : (i + 1) * rows]
    for k in sorted((k for k in where if k and not k & 1), key=lambda k: (low_bit(k), -k)):
        main = parts[k]
        bit = 1
        while bit < low_bit(k):
            main = main + came[k | bit][:, :out_width].astype(jnp.float32)
            bit *= 2
        if k in chain:
            carried = low2
            for c in chain[: chain.index(k)]:
                carried = carried + came[c][:, out_width:].astype(jnp.float32)
            main = jnp.concatenate([main, carried], axis=1)
        came[k] = across(main.astype(jnp.bfloat16), low_bit(k))
    lows = [came[k] for k in chain[:-1]]
    terms = [parts[0]] + [came[1 << i] for i in range(len(bits) - 1)]
    return pl.pallas_call(
        functools.partial(final_kernel, out_width, (len(lows), len(terms)), replicas),
        in_specs=[VMEM, VMEM] + [HBM] * replicas + [VMEM] * (len(lows) + len(terms)),
        out_specs=VMEM,
        out_shape=jax.ShapeDtypeStruct((rows, out_width), jnp.bfloat16),
        scratch_shapes=[
            pltpu.VMEM((replicas,) + map_in, keys.dtype),
            pltpu.SemaphoreType.DMA((replicas,)),
        ],
        name="final",
        **params((10**8, 10**6), 8 << 20),
    )(picks, low2, *output_up, *lows, *terms)


def solution(mesh):
    sizes = dict(mesh.shape)

    def body(*arrays):
        return per_device(sizes, *arrays)

    return jax.shard_map(
        body,
        mesh=mesh,
        in_specs=(
            P(("groups", "replica"), "tensor"),
            P(None, "tensor"),
            P("tensor", None),
            P(("groups", "replica"), None, None, None),
            P(("groups", "replica"), None, None, None),
            P(("groups", "replica"), None, "tensor"),
            P(("groups", "replica"), None, "tensor"),
            P(("groups", "replica"), None, "tensor"),
            P(("groups", "replica"), None, "tensor"),
            P("groups"),
            P("groups"),
            P(("groups", "replica")),
        ),
        out_specs=P(("groups", "replica"), "tensor"),
        check_vma=False,
    )
```

```python
import functools
import math

import jax
import jax.numpy as jnp
from jax import lax
from jax.experimental import pallas as pl
from jax.experimental.pallas import tpu as pltpu
from jax.sharding import PartitionSpec as P

HEADS = 64
KVS = 8
VMEM = pl.BlockSpec(memory_space=pltpu.VMEM)
SMEM = pl.BlockSpec(memory_space=pltpu.SMEM)
HBM = pl.BlockSpec(memory_space=pltpu.HBM)
LANES = 128
PIECES = 2
GRANT = 49 << 20


def dot(a, b):
    return jnp.dot(a, b, preferred_element_type=jnp.float32)


def dot_t(a, b):
    return lax.dot_general(a, b, (((1,), (1,)), ((), ())), preferred_element_type=jnp.float32)


def params(flops_bytes, limit=GRANT):
    return dict(
        compiler_params=pltpu.CompilerParams(vmem_limit_bytes=limit),
        cost_estimate=pl.CostEstimate(
            flops=flops_bytes[0], bytes_accessed=flops_bytes[1], transcendentals=0
        ),
    )


def low_of(x, downs, picks):
    total = 0.0
    at = 0
    for down in downs:
        wide = down.shape[0]
        part = dot_t(x, down[...]) * picks[:, at : at + wide]
        for g in range(0, wide, LANES):
            total = total + part[:, g : g + LANES]
        at += wide
    return total


def lora_of(low, ups, picks):
    total = 0.0
    at = 0
    low = low.astype(jnp.bfloat16).astype(jnp.float32)
    for up in ups:
        wide = up.shape[0]
        spread = jnp.concatenate([low] * (wide // LANES), axis=1) * picks[:, at : at + wide]
        total = total + dot(spread.astype(jnp.bfloat16), up[...])
        at += wide
    return total


def load_all(pairs, sems):
    copies = [pltpu.make_async_copy(src, dst, sems.at[i]) for i, (src, dst) in enumerate(pairs)]
    for c in copies:
        c.start()
    return copies


def low_kernel(count, x_hbm, picks_ref, *rest):
    downs, out_ref, x_ref, bufs, sems = rest[:count], rest[count], rest[count + 1], rest[count + 2 : -1], rest[-1]
    for c in load_all([(x_hbm, x_ref)] + list(zip(downs, bufs)), sems):
        c.wait()
    out_ref[...] = low_of(x_ref[...], bufs, picks_ref[...])


def low_call(x, picks, downs):
    return pl.pallas_call(
        functools.partial(low_kernel, len(downs)),
        in_specs=[HBM, VMEM] + [HBM] * len(downs),
        out_specs=VMEM,
        out_shape=jax.ShapeDtypeStruct((x.shape[0], LANES), jnp.float32),
        scratch_shapes=[pltpu.VMEM(x.shape, x.dtype)]
        + [pltpu.VMEM(d.shape, d.dtype) for d in downs]
        + [pltpu.SemaphoreType.DMA((1 + len(downs),))],
        name="low",
        **params((10**8, 10**6)),
    )(x, picks, *downs)


def weight_copies(weight, buf, sems, j, block, along):
    depth, wide = buf.shape[1], buf.shape[2]
    piece = depth // PIECES
    copies = []
    for p in range(PIECES):
        if along == 0:
            src = weight.at[pl.ds(pl.multiple_of(block * depth + p * piece, piece), piece), :]
        else:
            src = weight.at[p * piece : (p + 1) * piece, pl.ds(pl.multiple_of(block * wide, LANES), wide)]
        copies.append(
            pltpu.make_async_copy(src, buf.at[j, p * piece : (p + 1) * piece, :], sems.at[j, p])
        )
    return copies


def block_dot(x_ref_read, buf, j, copies, total):
    piece = buf.shape[1] // PIECES
    for p in range(PIECES):
        copies[p].wait()
        total = total + dot(
            x_ref_read(p * piece, piece), buf[j, p * piece : (p + 1) * piece, :]
        )
    return total


def project_kernel(ks, spans, first, tensor_ref, *rest):
    given = len(set(i for i, _ in spans))
    chunks, rest = rest[:given], rest[given:]
    weight, rest = rest[0], rest[1:]
    if first:
        total = 0.0
    else:
        total, rest = rest[0][...], rest[1:]
    out_ref, buf, sems = rest
    rows = out_ref.shape[0]
    copies = [weight_copies(weight, buf, sems, j, tensor_ref[0] ^ k, 0) for j, k in enumerate(ks)]
    for pieces in copies:
        for c in pieces:
            c.start()
    for j, (i, r) in enumerate(spans):
        total = block_dot(
            lambda a, n, i=i, r=r: chunks[i][r : r + rows, a : a + n], buf, j, copies[j], total
        )
    out_ref[...] = total


def project_call(where, ks, tensor_at, weight, before, rows, width):
    wide = weight.shape[1]
    count = len(ks)
    arrays, spans = [], []
    for k in ks:
        array, r = where[k]
        if not any(a is array for a in arrays):
            arrays.append(array)
        spans.append(([a is array for a in arrays].index(True), r))
    extra = [] if before is None else [before]
    return pl.pallas_call(
        functools.partial(project_kernel, ks, spans, before is None),
        in_specs=[SMEM] + [VMEM] * len(arrays) + [HBM] + [VMEM] * len(extra),
        out_specs=VMEM,
        out_shape=jax.ShapeDtypeStruct((rows, wide), jnp.float32),
        scratch_shapes=[
            pltpu.VMEM((count, width, wide), weight.dtype),
            pltpu.SemaphoreType.DMA((count, PIECES)),
        ],
        **params(
            (2 * count * rows * width * wide, 2 * count * width * wide),
        ),
    )(tensor_at, *arrays, weight, *extra)


def mix_kernel(sizes, *refs):
    k_in, k_out, maps, kv_count, group, head, local_heads, group_all, _ = sizes
    refs = list(refs)
    tensor_ref, chunk, w_in, w_out, before, low, picks = [refs.pop(0) for _ in range(7)]
    ups = [refs.pop(0) for _ in range(maps)]
    downs = [refs.pop(0) for _ in range(maps)]
    keys, values, live = [refs.pop(0) for _ in range(3)]
    block_out, low_out, mixed_out = [refs.pop(0) for _ in range(3)]
    buf_in, sem_in, buf_out, sem_out, k_buf, v_buf, up_buf, down_buf, sems = refs

    tensor_at = tensor_ref[0]
    copies_in = weight_copies(w_in, buf_in, sem_in, 0, tensor_at ^ k_in, 0)
    copies_out = weight_copies(w_out, buf_out, sem_out, 0, tensor_at ^ k_out, 1)
    kv = pl.ds(tensor_at * local_heads // group_all, kv_count)
    up_copies = load_all([(u, up_buf.at[i]) for i, u in enumerate(ups)], sems.at[0])
    for c in copies_in:
        c.start()
    kv_copies = load_all([(keys.at[:, kv], k_buf), (values.at[:, kv], v_buf)], sems.at[1])
    down_copies = load_all([(d, down_buf.at[i]) for i, d in enumerate(downs)], sems.at[2])
    for c in copies_out:
        c.start()

    rows = before.shape[0]
    picked = picks[...]
    for c in up_copies:
        c.wait()
    total = before[...] + 0.5 * lora_of(low[...], [up_buf.at[i] for i in range(maps)], picked)
    total = block_dot(lambda a, n: chunk[:, a : a + n], buf_in, 0, copies_in, total)
    query = total.astype(jnp.bfloat16)
    for c in kv_copies:
        c.wait()
    length = k_buf.shape[2]
    heads = [None] * (kv_count * group)
    alive = jnp.concatenate([live[...]] * group, axis=0) > 0
    for kvh in range(kv_count):
        flat_k = k_buf[:, kvh].reshape(rows * length, head)
        flat_v = v_buf[:, kvh].reshape(rows * length, head)
        q = jnp.concatenate(
            [query[:, (kvh * group + g) * head : (kvh * group + g + 1) * head] for g in range(group)],
            axis=0,
        )
        scores = dot_t(q, flat_k) / math.sqrt(head)
        scores = jnp.where(alive, scores, -1e30)
        top = jnp.max(scores, axis=1, keepdims=True)
        weights = jnp.exp(scores - top)
        probs = (weights / jnp.sum(weights, axis=1, keepdims=True)).astype(jnp.bfloat16)
        got = dot(probs, flat_v).astype(jnp.bfloat16)
        for g in range(group):
            heads[kvh * group + g] = got[g * rows : (g + 1) * rows]
    mixed = jnp.concatenate(heads, axis=1)
    mixed_out[...] = mixed
    for c in down_copies:
        c.wait()
    low_part = low_of(mixed, [down_buf.at[i] for i in range(maps)], picked)
    low_out[...] = low_part
    block = block_dot(lambda a, n: mixed[:, a : a + n], buf_out, 0, copies_out, 0.0)
    wide = block.shape[1]
    block_out[:, :wide] = block.astype(block_out.dtype)
    block_out[:, wide:] = low_part.astype(block_out.dtype)


def out_kernel(ks, spans, tensor_ref, x_ref, weight, *rest):
    outs, (buf, sems) = rest[:-2], rest[-2:]
    rows = x_ref.shape[0]
    copies = [weight_copies(weight, buf, sems, j, tensor_ref[0] ^ k, 1) for j, k in enumerate(ks)]
    for pieces in copies:
        for c in pieces:
            c.start()
    for j, (i, r) in enumerate(spans):
        block = block_dot(lambda a, n: x_ref[:, a : a + n], buf, j, copies[j], 0.0)
        outs[i][r : r + rows, :] = block.astype(outs[i].dtype)


def out_call(groups, tensor_at, mixed, weight, out_width):
    rows, depth = mixed.shape
    ks = [k for group, _ in groups for k in group]
    spans = [(i, r * rows) for i, (group, _) in enumerate(groups) for r in range(len(group))]
    return pl.pallas_call(
        functools.partial(out_kernel, ks, spans),
        in_specs=[SMEM, VMEM, HBM],
        out_specs=[VMEM] * len(groups),
        out_shape=[jax.ShapeDtypeStruct((rows * len(group), out_width), kind) for group, kind in groups],
        scratch_shapes=[
            pltpu.VMEM((len(ks), depth, out_width), weight.dtype),
            pltpu.SemaphoreType.DMA((len(ks), PIECES)),
        ],
        **params((2 * len(ks) * rows * depth * out_width, 2 * len(ks) * depth * out_width)),
    )(tensor_at, mixed, weight)


def final_kernel(wide, count, maps, picks_ref, low_ref, *rest):
    ups, rest = rest[:maps], rest[maps:]
    lows, rest = rest[: count[0]], rest[count[0] :]
    terms, rest = rest[: count[1]], rest[count[1] :]
    out_ref, up_buf, sems = rest
    copies = load_all([(u, up_buf.at[i]) for i, u in enumerate(ups)], sems)
    low = low_ref[...]
    total = 0.0
    for ref in lows:
        low = low + ref[:, wide:].astype(jnp.float32)
    total = lows[-1][:, :wide].astype(jnp.float32)
    for t in terms:
        total = total + t[:, :wide].astype(jnp.float32)
    for c in copies:
        c.wait()
    total = total + 0.5 * lora_of(low, [up_buf.at[i] for i in range(maps)], picks_ref[...])
    out_ref[...] = total.astype(out_ref.dtype)


def low_bit(k):
    return k & -k


def per_device(
    mesh_shape,
    hidden,
    w_query,
    output_weight,
    keys,
    values,
    query_down_maps,
    query_up_maps,
    output_down_maps,
    output_up_maps,
    adapter_ids,
    owner_map,
    kv_lengths,
):
    rows, width = hidden.shape
    head = keys.shape[3]
    length = keys.shape[2]
    shards = mesh_shape["tensor"]
    replicas = mesh_shape["replica"]
    stored, rank = query_down_maps.shape[:2]
    replica_at = lax.axis_index("replica")
    tensor_at = lax.axis_index("tensor").astype(jnp.int32).reshape(1)
    bits = []
    while (1 << len(bits)) < shards:
        bits.append(1 << len(bits))

    def across(x, bit):
        return lax.ppermute(x, "tensor", [(i, i ^ bit) for i in range(shards)])

    def with_swapped(x):
        x = x.reshape(stored * rank, x.shape[2])
        return [x] + [
            lax.ppermute(x, "replica", [(i, (i + k) % replicas) for i in range(replicas)])
            for k in range(1, replicas)
        ]

    id_table = lax.broadcasted_iota(jnp.int32, (1, owner_map.shape[0]), 1)
    slots_all = jnp.sum(jnp.where(adapter_ids[:, None] == id_table, owner_map[None, :], 0), axis=1)
    slots = lax.dynamic_slice_in_dim(slots_all, replica_at * rows, rows)
    lane = lax.broadcasted_iota(jnp.int32, (1, stored * rank), 1) // rank
    picks = jnp.concatenate(
        [
            (slots[:, None] == ((replica_at - k) % replicas) * stored + lane).astype(jnp.float32)
            for k in range(replicas)
        ],
        axis=1,
    )
    column = lax.broadcasted_iota(jnp.int32, (rows, rows * length), 1)
    row = lax.broadcasted_iota(jnp.int32, (rows, rows * length), 0)
    live = ((column // length == row) & (column % length < kv_lengths[:, None])).astype(jnp.float32)

    query_down = with_swapped(query_down_maps)
    query_up = with_swapped(query_up_maps)
    output_down = with_swapped(output_down_maps)
    output_up = with_swapped(output_up_maps)

    low = low_call(hidden, picks, query_down)
    where = {0: (hidden, 0)}
    chain = 0
    for bit in reversed(bits):
        held = list(where)
        if bit != 1:
            for k in held:
                where[k | bit] = (across(where[k][0], bit), 0)
            low = low + across(low, bit)
        else:
            where[1] = (across(hidden, 1), 0)
            rest = [k for k in held if k not in (0, chain)]
            if rest:
                got = across(jnp.concatenate([where[k][0] for k in rest], axis=0), 1)
                for i, k in enumerate(rest):
                    where[k | 1] = (got, i * rows)
            if chain:
                joined = jnp.concatenate([where[chain][0], low.astype(jnp.bfloat16)], axis=1)
                got = across(joined, 1)
                where[chain | 1] = (got, 0)
                low = low + got[:, width:].astype(jnp.float32)
            else:
                low = low + across(low, 1)
        chain |= bit

    top = bits[-1] if bits else 0
    order = sorted(where, key=lambda k: (bin(k).count("1"), -k))
    last = order[-1]
    early = order[:-1]
    first = [k for k in early if k in (0, top >> 1, top)]
    others = [k for k in early if k not in first]
    query = project_call(where, first, tensor_at, w_query, None, rows, width)
    for i in range(0, len(others), 6):
        query = project_call(where, others[i : i + 6], tensor_at, w_query, query, rows, width)

    wide = w_query.shape[1]
    local_heads = wide // head
    group_all = HEADS // KVS
    kv_count = max(1, local_heads // group_all)
    group = local_heads // kv_count
    out_width = output_weight.shape[1] // shards
    depth = output_weight.shape[0]
    whole = shards - 1
    sizes = (last, whole, replicas, kv_count, group, head, local_heads, group_all, width)
    map_in, map_out = (stored * rank, wide), (stored * rank, depth)
    payload, low2, mixed = pl.pallas_call(
        functools.partial(mix_kernel, sizes),
        in_specs=[SMEM, VMEM, HBM, HBM, VMEM, VMEM, VMEM] + [HBM] * (2 * replicas) + [HBM, HBM, VMEM],
        out_specs=[VMEM] * 3,
        out_shape=[
            jax.ShapeDtypeStruct((rows, out_width + LANES), jnp.bfloat16),
            jax.ShapeDtypeStruct((rows, LANES), jnp.float32),
            jax.ShapeDtypeStruct((rows, wide), jnp.bfloat16),
        ],
        scratch_shapes=[
            pltpu.VMEM((1, width, wide), w_query.dtype),
            pltpu.SemaphoreType.DMA((1, PIECES)),
            pltpu.VMEM((1, depth, out_width), output_weight.dtype),
            pltpu.SemaphoreType.DMA((1, PIECES)),
            pltpu.VMEM((rows, kv_count, length, head), keys.dtype),
            pltpu.VMEM((rows, kv_count, length, head), values.dtype),
            pltpu.VMEM((replicas,) + map_in, keys.dtype),
            pltpu.VMEM((replicas,) + map_out, keys.dtype),
            pltpu.SemaphoreType.DMA((3, max(2, replicas))),
        ],
        name="mix",
        **params((10**9, 6 << 20)),
    )(
        tensor_at,
        where[last][0],
        w_query,
        output_weight,
        query,
        low,
        picks,
        *query_up,
        *output_down,
        keys,
        values,
        live,
    )

    came = {whole: across(payload, 1)}
    chain = [whole]
    while chain[-1]:
        chain.append(chain[-1] & (chain[-1] - 1))
    odd = [k for k in sorted(where, reverse=True) if k & 1 and k not in (whole, 1)]
    even = [k for k in sorted(where, reverse=True) if not k & 1]
    f32, bf16 = jnp.float32, jnp.bfloat16
    plan = [([k], f32) for k in even[:1]] + [(odd, bf16)] * bool(odd)
    plan = [plan, [([k], f32) for k in even[1:-1]] + [([1], bf16)], [([k], f32) for k in even[-1:]]]
    parts = {}
    for groups in plan:
        arrays = out_call(groups, tensor_at, mixed, output_weight, out_width)
        for (g, kind), array in zip(groups, arrays):
            if kind == bf16:
                got = across(array, 1)
                for i, k in enumerate(g):
                    came[k] = got[i * rows : (i + 1) * rows]
            else:
                parts[g[0]] = array
    for k in sorted((k for k in where if k and not k & 1), key=lambda k: (low_bit(k), -k)):
        main = parts[k]
        bit = 1
        while bit < low_bit(k):
            main = main + came[k | bit][:, :out_width].astype(jnp.float32)
            bit *= 2
        if k in chain:
            carried = low2
            for c in chain[: chain.index(k)]:
                carried = carried + came[c][:, out_width:].astype(jnp.float32)
            main = jnp.concatenate([main, carried], axis=1)
        came[k] = across(main.astype(jnp.bfloat16), low_bit(k))
    lows = [came[k] for k in chain[:-1]]
    terms = [parts[0]] + [came[1 << i] for i in range(len(bits) - 1)]
    return pl.pallas_call(
        functools.partial(final_kernel, out_width, (len(lows), len(terms)), replicas),
        in_specs=[VMEM, VMEM] + [HBM] * replicas + [VMEM] * (len(lows) + len(terms)),
        out_specs=VMEM,
        out_shape=jax.ShapeDtypeStruct((rows, out_width), jnp.bfloat16),
        scratch_shapes=[
            pltpu.VMEM((replicas,) + map_in, keys.dtype),
            pltpu.SemaphoreType.DMA((replicas,)),
        ],
        name="final",
        **params((10**8, 10**6)),
    )(picks, low2, *output_up, *lows, *terms)


def solution(mesh):
    sizes = dict(mesh.shape)

    def body(*arrays):
        return per_device(sizes, *arrays)

    return jax.shard_map(
        body,
        mesh=mesh,
        in_specs=(
            P(("groups", "replica"), "tensor"),
            P(None, "tensor"),
            P("tensor", None),
            P(("groups", "replica"), None, None, None),
            P(("groups", "replica"), None, None, None),
            P(("groups", "replica"), None, "tensor"),
            P(("groups", "replica"), None, "tensor"),
            P(("groups", "replica"), None, "tensor"),
            P(("groups", "replica"), None, "tensor"),
            P("groups"),
            P("groups"),
            P(("groups", "replica")),
        ),
        out_specs=P(("groups", "replica"), "tensor"),
        check_vma=False,
    )
```

```python
import functools
import math

import jax
import jax.numpy as jnp
from jax import lax
from jax.experimental import pallas as pl
from jax.experimental.pallas import tpu as pltpu
from jax.sharding import PartitionSpec as P

HEADS = 64
KVS = 8
VMEM = pl.BlockSpec(memory_space=pltpu.VMEM)
SMEM = pl.BlockSpec(memory_space=pltpu.SMEM)
HBM = pl.BlockSpec(memory_space=pltpu.HBM)
LANES = 128
PIECES = 2
GRANT = 24 << 20


def dot(a, b):
    return jnp.dot(a, b, preferred_element_type=jnp.float32)


def dot_t(a, b):
    return lax.dot_general(a, b, (((1,), (1,)), ((), ())), preferred_element_type=jnp.float32)


def params(flops_bytes, limit=GRANT):
    return dict(
        compiler_params=pltpu.CompilerParams(vmem_limit_bytes=limit),
        cost_estimate=pl.CostEstimate(
            flops=flops_bytes[0], bytes_accessed=flops_bytes[1], transcendentals=0
        ),
    )


def low_of(x, downs, picks):
    total = 0.0
    at = 0
    for down in downs:
        wide = down.shape[0]
        part = dot_t(x, down[...]) * picks[:, at : at + wide]
        for g in range(0, wide, LANES):
            total = total + part[:, g : g + LANES]
        at += wide
    return total


def lora_of(low, ups, picks):
    total = 0.0
    at = 0
    low = low.astype(jnp.bfloat16).astype(jnp.float32)
    for up in ups:
        wide = up.shape[0]
        spread = jnp.concatenate([low] * (wide // LANES), axis=1) * picks[:, at : at + wide]
        total = total + dot(spread.astype(jnp.bfloat16), up[...])
        at += wide
    return total


def in_hbm(x):
    return pltpu.with_memory_space_constraint(x, pltpu.HBM)


def load_all(pairs, sems):
    copies = [pltpu.make_async_copy(src, dst, sems.at[i]) for i, (src, dst) in enumerate(pairs)]
    for c in copies:
        c.start()
    return copies


def low_kernel(count, x_hbm, picks_ref, *rest):
    downs, (out_ref, x_ref), bufs, sems = rest[:count], rest[count : count + 2], rest[count + 2 : -1], rest[-1]
    for c in load_all([(x_hbm, x_ref)] + list(zip(downs, bufs)), sems):
        c.wait()
    out_ref[...] = low_of(x_ref[...], bufs, picks_ref[...])


def low_call(x, picks, downs):
    return pl.pallas_call(
        functools.partial(low_kernel, len(downs)),
        in_specs=[HBM, VMEM] + [HBM] * len(downs),
        out_specs=[VMEM] * 2,
        out_shape=[
            jax.ShapeDtypeStruct((x.shape[0], LANES), jnp.float32),
            jax.ShapeDtypeStruct(x.shape, x.dtype),
        ],
        scratch_shapes=[pltpu.VMEM(d.shape, d.dtype) for d in downs]
        + [pltpu.SemaphoreType.DMA((1 + len(downs),))],
        name="low",
        **params((10**8, 10**6)),
    )(in_hbm(x), picks, in_hbm(downs[0]), *downs[1:])


def weight_copies(weight, buf, sems, j, block, along):
    depth, wide = buf.shape[1], buf.shape[2]
    piece = depth // PIECES
    copies = []
    for p in range(PIECES):
        if along == 0:
            src = weight.at[pl.ds(pl.multiple_of(block * depth + p * piece, piece), piece), :]
        else:
            src = weight.at[p * piece : (p + 1) * piece, pl.ds(pl.multiple_of(block * wide, LANES), wide)]
        copies.append(
            pltpu.make_async_copy(src, buf.at[j, p * piece : (p + 1) * piece, :], sems.at[j, p])
        )
    return copies


def block_dot(x_ref_read, buf, j, copies, total):
    piece = buf.shape[1] // PIECES
    for p in range(PIECES):
        copies[p].wait()
        total = total + dot(
            x_ref_read(p * piece, piece), buf[j, p * piece : (p + 1) * piece, :]
        )
    return total


def project_kernel(ks, spans, first, tensor_ref, *rest):
    given = len(set(i for i, _ in spans))
    chunks, rest = rest[:given], rest[given:]
    weight, rest = rest[0], rest[1:]
    if first:
        total = 0.0
    else:
        total, rest = rest[0][...], rest[1:]
    out_ref, buf, sems = rest
    rows = out_ref.shape[0]
    copies = [weight_copies(weight, buf, sems, j, tensor_ref[0] ^ k, 0) for j, k in enumerate(ks)]
    for pieces in copies:
        for c in pieces:
            c.start()
    for j, (i, r) in enumerate(spans):
        total = block_dot(
            lambda a, n, i=i, r=r: chunks[i][r : r + rows, a : a + n], buf, j, copies[j], total
        )
    out_ref[...] = total


def project_call(where, ks, tensor_at, weight, before, rows, width):
    wide = weight.shape[1]
    count = len(ks)
    arrays, spans = [], []
    for k in ks:
        array, r = where[k]
        if not any(a is array for a in arrays):
            arrays.append(array)
        spans.append(([a is array for a in arrays].index(True), r))
    extra = [] if before is None else [before]
    return pl.pallas_call(
        functools.partial(project_kernel, ks, spans, before is None),
        in_specs=[SMEM] + [VMEM] * len(arrays) + [HBM] + [VMEM] * len(extra),
        out_specs=VMEM,
        out_shape=jax.ShapeDtypeStruct((rows, wide), jnp.float32),
        scratch_shapes=[
            pltpu.VMEM((count, width, wide), weight.dtype),
            pltpu.SemaphoreType.DMA((count, PIECES)),
        ],
        **params(
            (2 * count * rows * width * wide, 2 * count * width * wide),
        ),
    )(tensor_at, *arrays, in_hbm(weight), *extra)


def mix_kernel(sizes, *refs):
    k_in, k_outs, maps, kv_count, group, head, local_heads, group_all, _ = sizes
    refs = list(refs)
    tensor_ref, chunk, w_in, w_out, before, low, picks = [refs.pop(0) for _ in range(7)]
    ups = [refs.pop(0) for _ in range(maps)]
    downs = [refs.pop(0) for _ in range(maps)]
    keys, values, live = [refs.pop(0) for _ in range(3)]
    low_out, mixed_out, block_out = [refs.pop(0) for _ in range(3)]
    more_outs = [refs.pop(0) for _ in k_outs[1:]]
    buf_in, sem_in, buf_out, sem_out, k_buf, v_buf, up_buf, down_buf, sems = refs

    tensor_at = tensor_ref[0]
    copies_in = weight_copies(w_in, buf_in, sem_in, 0, tensor_at ^ k_in, 0)
    copies_out = [
        weight_copies(w_out, buf_out, sem_out, j, tensor_at ^ k, 1) for j, k in enumerate(k_outs)
    ]
    kv = pl.ds(tensor_at * local_heads // group_all, kv_count)
    up_copies = load_all([(u, up_buf.at[i]) for i, u in enumerate(ups)], sems.at[0])
    for c in copies_in:
        c.start()
    kv_copies = load_all([(keys.at[:, kv], k_buf), (values.at[:, kv], v_buf)], sems.at[1])
    down_copies = load_all([(d, down_buf.at[i]) for i, d in enumerate(downs)], sems.at[2])
    for pieces in copies_out:
        for c in pieces:
            c.start()

    rows = before.shape[0]
    picked = picks[...]
    for c in up_copies:
        c.wait()
    total = before[...] + 0.5 * lora_of(low[...], [up_buf.at[i] for i in range(maps)], picked)
    total = block_dot(lambda a, n: chunk[:, a : a + n], buf_in, 0, copies_in, total)
    query = total.astype(jnp.bfloat16)
    for c in kv_copies:
        c.wait()
    length = k_buf.shape[2]
    heads = [None] * (kv_count * group)
    alive = jnp.concatenate([live[...]] * group, axis=0) > 0
    for kvh in range(kv_count):
        flat_k = k_buf[:, kvh].reshape(rows * length, head)
        flat_v = v_buf[:, kvh].reshape(rows * length, head)
        q = jnp.concatenate(
            [query[:, (kvh * group + g) * head : (kvh * group + g + 1) * head] for g in range(group)],
            axis=0,
        )
        scores = dot_t(q, flat_k) / math.sqrt(head)
        scores = jnp.where(alive, scores, -1e30)
        top = jnp.max(scores, axis=1, keepdims=True)
        weights = jnp.exp(scores - top)
        probs = (weights / jnp.sum(weights, axis=1, keepdims=True)).astype(jnp.bfloat16)
        got = dot(probs, flat_v).astype(jnp.bfloat16)
        for g in range(group):
            heads[kvh * group + g] = got[g * rows : (g + 1) * rows]
    mixed = jnp.concatenate(heads, axis=1)
    mixed_out[...] = mixed
    for c in down_copies:
        c.wait()
    low_part = low_of(mixed, [down_buf.at[i] for i in range(maps)], picked)
    low_out[...] = low_part
    block = block_dot(lambda a, n: mixed[:, a : a + n], buf_out, 0, copies_out[0], 0.0)
    wide = block.shape[1]
    block_out[:, :wide] = block.astype(block_out.dtype)
    block_out[:, wide:] = low_part.astype(block_out.dtype)
    for j, ref in enumerate(more_outs):
        ref[...] = block_dot(
            lambda a, n: mixed[:, a : a + n], buf_out, j + 1, copies_out[j + 1], 0.0
        )


def out_kernel(ks, spans, tensor_ref, x_ref, weight, *rest):
    outs, (buf, sems) = rest[:-2], rest[-2:]
    rows = x_ref.shape[0]
    copies = [weight_copies(weight, buf, sems, j, tensor_ref[0] ^ k, 1) for j, k in enumerate(ks)]
    for pieces in copies:
        for c in pieces:
            c.start()
    for j, (i, r) in enumerate(spans):
        block = block_dot(lambda a, n: x_ref[:, a : a + n], buf, j, copies[j], 0.0)
        outs[i][r : r + rows, :] = block.astype(outs[i].dtype)


def out_call(groups, tensor_at, mixed, weight, out_width):
    rows, depth = mixed.shape
    ks = [k for group, _ in groups for k in group]
    spans = [(i, r * rows) for i, (group, _) in enumerate(groups) for r in range(len(group))]
    return pl.pallas_call(
        functools.partial(out_kernel, ks, spans),
        in_specs=[SMEM, VMEM, HBM],
        out_specs=[VMEM] * len(groups),
        out_shape=[jax.ShapeDtypeStruct((rows * len(group), out_width), kind) for group, kind in groups],
        scratch_shapes=[
            pltpu.VMEM((len(ks), depth, out_width), weight.dtype),
            pltpu.SemaphoreType.DMA((len(ks), PIECES)),
        ],
        **params((2 * len(ks) * rows * depth * out_width, 2 * len(ks) * depth * out_width)),
    )(tensor_at, mixed, in_hbm(weight))


def final_kernel(wide, count, maps, picks_ref, low_ref, *rest):
    ups, rest = rest[:maps], rest[maps:]
    lows, rest = rest[: count[0]], rest[count[0] :]
    terms, rest = rest[: count[1]], rest[count[1] :]
    out_ref, up_buf, sems = rest
    copies = load_all([(u, up_buf.at[i]) for i, u in enumerate(ups)], sems)
    low = low_ref[...]
    total = 0.0
    for ref in lows:
        low = low + ref[:, wide:].astype(jnp.float32)
    total = lows[-1][:, :wide].astype(jnp.float32)
    for t in terms:
        total = total + t[:, :wide].astype(jnp.float32)
    for c in copies:
        c.wait()
    total = total + 0.5 * lora_of(low, [up_buf.at[i] for i in range(maps)], picks_ref[...])
    out_ref[...] = total.astype(out_ref.dtype)


def low_bit(k):
    return k & -k


def per_device(
    mesh_shape,
    hidden,
    w_query,
    output_weight,
    keys,
    values,
    query_down_maps,
    query_up_maps,
    output_down_maps,
    output_up_maps,
    adapter_ids,
    owner_map,
    kv_lengths,
):
    rows, width = hidden.shape
    head = keys.shape[3]
    length = keys.shape[2]
    shards = mesh_shape["tensor"]
    replicas = mesh_shape["replica"]
    stored, rank = query_down_maps.shape[:2]
    replica_at = lax.axis_index("replica")
    tensor_at = lax.axis_index("tensor").astype(jnp.int32).reshape(1)
    bits = []
    while (1 << len(bits)) < shards:
        bits.append(1 << len(bits))

    def across(x, bit):
        return lax.ppermute(x, "tensor", [(i, i ^ bit) for i in range(shards)])

    def with_swapped(x):
        x = x.reshape(stored * rank, x.shape[2])
        return [x] + [
            lax.ppermute(x, "replica", [(i, (i + k) % replicas) for i in range(replicas)])
            for k in range(1, replicas)
        ]

    id_table = lax.broadcasted_iota(jnp.int32, (1, owner_map.shape[0]), 1)
    slots_all = jnp.sum(jnp.where(adapter_ids[:, None] == id_table, owner_map[None, :], 0), axis=1)
    slots = lax.dynamic_slice_in_dim(slots_all, replica_at * rows, rows)
    lane = lax.broadcasted_iota(jnp.int32, (1, stored * rank), 1) // rank
    picks = jnp.concatenate(
        [
            (slots[:, None] == ((replica_at - k) % replicas) * stored + lane).astype(jnp.float32)
            for k in range(replicas)
        ],
        axis=1,
    )
    column = lax.broadcasted_iota(jnp.int32, (rows, rows * length), 1)
    row = lax.broadcasted_iota(jnp.int32, (rows, rows * length), 0)
    live = ((column // length == row) & (column % length < kv_lengths[:, None])).astype(jnp.float32)

    query_down = with_swapped(query_down_maps)
    query_up = with_swapped(query_up_maps)
    output_down = with_swapped(output_down_maps)
    output_up = with_swapped(output_up_maps)

    low, near = low_call(hidden, picks, query_down)
    where = {0: (near, 0)}
    chain = 0
    for bit in reversed(bits):
        rest = [k for k in where if k not in (0, chain)]
        where[bit] = (across(hidden, bit), 0)
        if chain:
            joined = jnp.concatenate([where[chain][0][:, :width], low.astype(jnp.bfloat16)], axis=1)
            got = across(joined, bit)
            where[chain | bit] = (got, 0)
            low = low + got[:, width:].astype(jnp.float32)
        else:
            low = low + across(low, bit)
        if rest and bit == 1:
            got = jnp.concatenate([where[k][0][:, :width] for k in rest], axis=0)
            got = across(got, 1)
            for i, k in enumerate(rest):
                where[k | 1] = (got, i * rows)
        else:
            for k in rest:
                where[k | bit] = (across(where[k][0][:, :width], bit), 0)
        chain |= bit

    top = bits[-1] if bits else 0
    order = sorted(where, key=lambda k: (bin(k).count("1"), -k))
    last = order[-1]
    early = order[:-1]
    first = [k for k in early if k in (0, top >> 1, top)]
    others = [k for k in early if k not in first]
    query = project_call(where, first, tensor_at, w_query, None, rows, width)
    for i in range(0, len(others), 6):
        query = project_call(where, others[i : i + 6], tensor_at, w_query, query, rows, width)

    wide = w_query.shape[1]
    local_heads = wide // head
    group_all = HEADS // KVS
    kv_count = max(1, local_heads // group_all)
    group = local_heads // kv_count
    out_width = output_weight.shape[1] // shards
    depth = output_weight.shape[0]
    whole = shards - 1
    even = [k for k in sorted(where, reverse=True) if not k & 1]
    k_outs = [whole] + even[:-1][:1]
    sizes = (last, k_outs, replicas, kv_count, group, head, local_heads, group_all, width)
    map_in, map_out = (stored * rank, wide), (stored * rank, depth)
    low2, mixed, payload, *blocks = pl.pallas_call(
        functools.partial(mix_kernel, sizes),
        in_specs=[SMEM, VMEM, HBM, HBM, VMEM, VMEM, VMEM] + [HBM] * (2 * replicas) + [HBM, HBM, VMEM],
        out_specs=[VMEM] * (2 + len(k_outs)),
        out_shape=[
            jax.ShapeDtypeStruct((rows, LANES), jnp.float32),
            jax.ShapeDtypeStruct((rows, wide), jnp.bfloat16),
            jax.ShapeDtypeStruct((rows, out_width + LANES), jnp.bfloat16),
        ]
        + [jax.ShapeDtypeStruct((rows, out_width), jnp.float32)] * (len(k_outs) - 1),
        scratch_shapes=[
            pltpu.VMEM((1, width, wide), w_query.dtype),
            pltpu.SemaphoreType.DMA((1, PIECES)),
            pltpu.VMEM((len(k_outs), depth, out_width), output_weight.dtype),
            pltpu.SemaphoreType.DMA((len(k_outs), PIECES)),
            pltpu.VMEM((rows, kv_count, length, head), keys.dtype),
            pltpu.VMEM((rows, kv_count, length, head), values.dtype),
            pltpu.VMEM((replicas,) + map_in, keys.dtype),
            pltpu.VMEM((replicas,) + map_out, keys.dtype),
            pltpu.SemaphoreType.DMA((3, max(2, replicas))),
        ],
        name="mix",
        **params((10**9, 6 << 20)),
    )(
        tensor_at,
        where[last][0],
        in_hbm(w_query),
        in_hbm(output_weight),
        query,
        low,
        picks,
        *query_up,
        *output_down,
        in_hbm(keys),
        in_hbm(values),
        live,
    )

    came = {whole: across(payload, 1)}
    chain = [whole]
    while chain[-1]:
        chain.append(chain[-1] & (chain[-1] - 1))
    odd = [k for k in sorted(where, reverse=True) if k & 1 and k not in (whole, 1)]
    f32, bf16 = jnp.float32, jnp.bfloat16
    parts = dict(zip(k_outs[1:], blocks))
    even = [k for k in even if k not in parts]
    plan = [
        [(odd, bf16)] * bool(odd),
        [([k], f32) for k in even[:-1]] + [([1], bf16)] * (whole > 1),
        [([k], f32) for k in even[-1:]],
    ]
    plan = [groups for groups in plan if groups]
    for groups in plan:
        arrays = out_call(groups, tensor_at, mixed, output_weight, out_width)
        for (g, kind), array in zip(groups, arrays):
            if kind == bf16:
                got = across(array, 1)
                for i, k in enumerate(g):
                    came[k] = got[i * rows : (i + 1) * rows]
            else:
                parts[g[0]] = array
    for k in sorted((k for k in where if k and not k & 1), key=lambda k: (low_bit(k), -k)):
        main = parts[k]
        bit = 1
        while bit < low_bit(k):
            main = main + came[k | bit][:, :out_width].astype(jnp.float32)
            bit *= 2
        if k in chain:
            carried = low2
            for c in chain[: chain.index(k)]:
                carried = carried + came[c][:, out_width:].astype(jnp.float32)
            main = jnp.concatenate([main, carried], axis=1)
        came[k] = across(main.astype(jnp.bfloat16), low_bit(k))
    lows = [came[k] for k in chain[:-1]]
    terms = [parts[0]] + [came[1 << i] for i in range(len(bits) - 1)]
    return pl.pallas_call(
        functools.partial(final_kernel, out_width, (len(lows), len(terms)), replicas),
        in_specs=[VMEM, VMEM] + [HBM] * replicas + [VMEM] * (len(lows) + len(terms)),
        out_specs=VMEM,
        out_shape=jax.ShapeDtypeStruct((rows, out_width), jnp.bfloat16),
        scratch_shapes=[
            pltpu.VMEM((replicas,) + map_in, keys.dtype),
            pltpu.SemaphoreType.DMA((replicas,)),
        ],
        name="final",
        **params((10**8, 10**6)),
    )(picks, low2, *output_up, *lows, *terms)


def solution(mesh):
    sizes = dict(mesh.shape)

    def body(*arrays):
        return per_device(sizes, *arrays)

    return jax.shard_map(
        body,
        mesh=mesh,
        in_specs=(
            P(("groups", "replica"), "tensor"),
            P(None, "tensor"),
            P("tensor", None),
            P(("groups", "replica"), None, None, None),
            P(("groups", "replica"), None, None, None),
            P(("groups", "replica"), None, "tensor"),
            P(("groups", "replica"), None, "tensor"),
            P(("groups", "replica"), None, "tensor"),
            P(("groups", "replica"), None, "tensor"),
            P("groups"),
            P("groups"),
            P(("groups", "replica")),
        ),
        out_specs=P(("groups", "replica"), "tensor"),
        check_vma=False,
    )
```

```python
import functools
import math

import jax
import jax.numpy as jnp
from jax import lax
from jax.experimental import pallas as pl
from jax.experimental.pallas import tpu as pltpu
from jax.sharding import PartitionSpec as P

HEADS = 64
KVS = 8
VMEM = pl.BlockSpec(memory_space=pltpu.VMEM)
SMEM = pl.BlockSpec(memory_space=pltpu.SMEM)
HBM = pl.BlockSpec(memory_space=pltpu.HBM)
LANES = 128
PIECES = 2
GRANT = 24 << 20


def dot(a, b):
    return jnp.dot(a, b, preferred_element_type=jnp.float32)


def dot_t(a, b):
    return lax.dot_general(a, b, (((1,), (1,)), ((), ())), preferred_element_type=jnp.float32)


def params(flops_bytes, limit=GRANT):
    return dict(
        compiler_params=pltpu.CompilerParams(vmem_limit_bytes=limit),
        cost_estimate=pl.CostEstimate(
            flops=flops_bytes[0], bytes_accessed=flops_bytes[1], transcendentals=0
        ),
    )


def low_of(x, downs, picks):
    total = 0.0
    at = 0
    for down in downs:
        wide = down.shape[0]
        part = dot_t(x, down[...]) * picks[:, at : at + wide]
        for g in range(0, wide, LANES):
            total = total + part[:, g : g + LANES]
        at += wide
    return total


def lora_of(low, ups, picks):
    total = 0.0
    at = 0
    low = low.astype(jnp.bfloat16).astype(jnp.float32)
    for up in ups:
        wide = up.shape[0]
        spread = jnp.concatenate([low] * (wide // LANES), axis=1) * picks[:, at : at + wide]
        total = total + dot(spread.astype(jnp.bfloat16), up[...])
        at += wide
    return total


def in_hbm(x):
    return pltpu.with_memory_space_constraint(x, pltpu.HBM)


def load_all(pairs, sems):
    copies = [pltpu.make_async_copy(src, dst, sems.at[i]) for i, (src, dst) in enumerate(pairs)]
    for c in copies:
        c.start()
    return copies


def low_kernel(count, x_hbm, picks_ref, *rest):
    downs, (out_ref, x_ref), bufs, sems = rest[:count], rest[count : count + 2], rest[count + 2 : -1], rest[-1]
    for c in load_all([(x_hbm, x_ref)] + list(zip(downs, bufs)), sems):
        c.wait()
    out_ref[...] = low_of(x_ref[...], bufs, picks_ref[...])


def low_call(x, picks, downs):
    return pl.pallas_call(
        functools.partial(low_kernel, len(downs)),
        in_specs=[HBM, VMEM] + [HBM] * len(downs),
        out_specs=[VMEM] * 2,
        out_shape=[
            jax.ShapeDtypeStruct((x.shape[0], LANES), jnp.float32),
            jax.ShapeDtypeStruct(x.shape, x.dtype),
        ],
        scratch_shapes=[pltpu.VMEM(d.shape, d.dtype) for d in downs]
        + [pltpu.SemaphoreType.DMA((1 + len(downs),))],
        name="low",
        **params((10**8, 10**6)),
    )(in_hbm(x), picks, in_hbm(downs[0]), *downs[1:])


def weight_copies(weight, buf, sems, j, block, along):
    depth, wide = buf.shape[1], buf.shape[2]
    piece = depth // PIECES
    copies = []
    for p in range(PIECES):
        if along == 0:
            src = weight.at[pl.ds(pl.multiple_of(block * depth + p * piece, piece), piece), :]
        else:
            src = weight.at[p * piece : (p + 1) * piece, pl.ds(pl.multiple_of(block * wide, LANES), wide)]
        copies.append(
            pltpu.make_async_copy(src, buf.at[j, p * piece : (p + 1) * piece, :], sems.at[j, p])
        )
    return copies


def block_dot(x_ref_read, buf, j, copies, total):
    piece = buf.shape[1] // PIECES
    for p in range(PIECES):
        copies[p].wait()
        total = total + dot(
            x_ref_read(p * piece, piece), buf[j, p * piece : (p + 1) * piece, :]
        )
    return total


def project_kernel(ks, spans, first, tensor_ref, *rest):
    given = len(set(i for i, _ in spans))
    chunks, rest = rest[:given], rest[given:]
    weight, rest = rest[0], rest[1:]
    if first:
        total = 0.0
    else:
        total, rest = rest[0][...], rest[1:]
    out_ref, buf, sems = rest
    rows = out_ref.shape[0]
    copies = [weight_copies(weight, buf, sems, j, tensor_ref[0] ^ k, 0) for j, k in enumerate(ks)]
    for pieces in copies:
        for c in pieces:
            c.start()
    for j, (i, r) in enumerate(spans):
        total = block_dot(
            lambda a, n, i=i, r=r: chunks[i][r : r + rows, a : a + n], buf, j, copies[j], total
        )
    out_ref[...] = total


def project_call(where, ks, tensor_at, weight, before, rows, width):
    wide = weight.shape[1]
    count = len(ks)
    arrays, spans = [], []
    for k in ks:
        array, r = where[k]
        if not any(a is array for a in arrays):
            arrays.append(array)
        spans.append(([a is array for a in arrays].index(True), r))
    extra = [] if before is None else [before]
    return pl.pallas_call(
        functools.partial(project_kernel, ks, spans, before is None),
        in_specs=[SMEM] + [VMEM] * len(arrays) + [HBM] + [VMEM] * len(extra),
        out_specs=VMEM,
        out_shape=jax.ShapeDtypeStruct((rows, wide), jnp.float32),
        scratch_shapes=[
            pltpu.VMEM((count, width, wide), weight.dtype),
            pltpu.SemaphoreType.DMA((count, PIECES)),
        ],
        **params(
            (2 * count * rows * width * wide, 2 * count * width * wide),
        ),
    )(tensor_at, *arrays, in_hbm(weight), *extra)


def mix_kernel(sizes, *refs):
    k_in, k_outs, maps, kv_count, group, head, local_heads, group_all, _ = sizes
    refs = list(refs)
    tensor_ref, chunk, w_in, w_out, before, low, picks = [refs.pop(0) for _ in range(7)]
    ups = [refs.pop(0) for _ in range(maps)]
    downs = [refs.pop(0) for _ in range(maps)]
    keys, values, live = [refs.pop(0) for _ in range(3)]
    low_out, mixed_out, block_out = [refs.pop(0) for _ in range(3)]
    more_outs = [refs.pop(0) for _ in k_outs[1:]]
    buf_in, sem_in, buf_out, sem_out, k_buf, v_buf, sems = refs

    tensor_at = tensor_ref[0]
    copies_in = weight_copies(w_in, buf_in, sem_in, 0, tensor_at ^ k_in, 0)
    copies_out = [
        weight_copies(w_out, buf_out, sem_out, j, tensor_at ^ k, 1) for j, k in enumerate(k_outs)
    ]
    kv = pl.ds(tensor_at * local_heads // group_all, kv_count)
    for c in copies_in:
        c.start()
    kv_copies = load_all([(keys.at[:, kv], k_buf), (values.at[:, kv], v_buf)], sems)
    for pieces in copies_out:
        for c in pieces:
            c.start()

    rows = before.shape[0]
    picked = picks[...]
    total = before[...] + 0.5 * lora_of(low[...], ups, picked)
    total = block_dot(lambda a, n: chunk[:, a : a + n], buf_in, 0, copies_in, total)
    query = total.astype(jnp.bfloat16)
    for c in kv_copies:
        c.wait()
    length = k_buf.shape[2]
    heads = [None] * (kv_count * group)
    alive = jnp.concatenate([live[...]] * group, axis=0) > 0
    for kvh in range(kv_count):
        flat_k = k_buf[:, kvh].reshape(rows * length, head)
        flat_v = v_buf[:, kvh].reshape(rows * length, head)
        q = jnp.concatenate(
            [query[:, (kvh * group + g) * head : (kvh * group + g + 1) * head] for g in range(group)],
            axis=0,
        )
        scores = dot_t(q, flat_k) / math.sqrt(head)
        scores = jnp.where(alive, scores, -1e30)
        top = jnp.max(scores, axis=1, keepdims=True)
        weights = jnp.exp(scores - top)
        probs = (weights / jnp.sum(weights, axis=1, keepdims=True)).astype(jnp.bfloat16)
        got = dot(probs, flat_v).astype(jnp.bfloat16)
        for g in range(group):
            heads[kvh * group + g] = got[g * rows : (g + 1) * rows]
    mixed = jnp.concatenate(heads, axis=1)
    mixed_out[...] = mixed
    low_part = low_of(mixed, downs, picked)
    low_out[...] = low_part
    block = block_dot(lambda a, n: mixed[:, a : a + n], buf_out, 0, copies_out[0], 0.0)
    wide = block.shape[1]
    block_out[:, :wide] = block.astype(block_out.dtype)
    block_out[:, wide:] = low_part.astype(block_out.dtype)
    for j, ref in enumerate(more_outs):
        block = block_dot(lambda a, n: mixed[:, a : a + n], buf_out, j + 1, copies_out[j + 1], 0.0)
        ref[...] = block.astype(ref.dtype)


def out_kernel(ks, spans, tensor_ref, x_ref, weight, *rest):
    outs, (buf, sems) = rest[:-2], rest[-2:]
    rows = x_ref.shape[0]
    copies = [weight_copies(weight, buf, sems, j, tensor_ref[0] ^ k, 1) for j, k in enumerate(ks)]
    for pieces in copies:
        for c in pieces:
            c.start()
    for j, (i, r) in enumerate(spans):
        block = block_dot(lambda a, n: x_ref[:, a : a + n], buf, j, copies[j], 0.0)
        outs[i][r : r + rows, :] = block.astype(outs[i].dtype)


def out_call(groups, tensor_at, mixed, weight, out_width):
    rows, depth = mixed.shape
    ks = [k for group, _ in groups for k in group]
    spans = [(i, r * rows) for i, (group, _) in enumerate(groups) for r in range(len(group))]
    return pl.pallas_call(
        functools.partial(out_kernel, ks, spans),
        in_specs=[SMEM, VMEM, HBM],
        out_specs=[VMEM] * len(groups),
        out_shape=[jax.ShapeDtypeStruct((rows * len(group), out_width), kind) for group, kind in groups],
        scratch_shapes=[
            pltpu.VMEM((len(ks), depth, out_width), weight.dtype),
            pltpu.SemaphoreType.DMA((len(ks), PIECES)),
        ],
        **params((2 * len(ks) * rows * depth * out_width, 2 * len(ks) * depth * out_width)),
    )(tensor_at, mixed, in_hbm(weight))


def final_kernel(wide, count, maps, picks_ref, low_ref, *rest):
    ups, rest = rest[:maps], rest[maps:]
    lows, rest = rest[: count[0]], rest[count[0] :]
    terms, rest = rest[: count[1]], rest[count[1] :]
    (out_ref,) = rest
    low = low_ref[...]
    total = 0.0
    for ref in lows:
        low = low + ref[:, wide:].astype(jnp.float32)
    total = lows[-1][:, :wide].astype(jnp.float32)
    for t in terms:
        total = total + t[:, :wide].astype(jnp.float32)
    total = total + 0.5 * lora_of(low, ups, picks_ref[...])
    out_ref[...] = total.astype(out_ref.dtype)


def low_bit(k):
    return k & -k


def per_device(
    mesh_shape,
    hidden,
    w_query,
    output_weight,
    keys,
    values,
    query_down_maps,
    query_up_maps,
    output_down_maps,
    output_up_maps,
    adapter_ids,
    owner_map,
    kv_lengths,
):
    rows, width = hidden.shape
    head = keys.shape[3]
    length = keys.shape[2]
    shards = mesh_shape["tensor"]
    replicas = mesh_shape["replica"]
    stored, rank = query_down_maps.shape[:2]
    replica_at = lax.axis_index("replica")
    tensor_at = lax.axis_index("tensor").astype(jnp.int32).reshape(1)
    bits = []
    while (1 << len(bits)) < shards:
        bits.append(1 << len(bits))

    def across(x, bit):
        return lax.ppermute(x, "tensor", [(i, i ^ bit) for i in range(shards)])

    def with_swapped(x):
        x = x.reshape(stored * rank, x.shape[2])
        return [x] + [
            lax.ppermute(x, "replica", [(i, (i + k) % replicas) for i in range(replicas)])
            for k in range(1, replicas)
        ]

    id_table = lax.broadcasted_iota(jnp.int32, (1, owner_map.shape[0]), 1)
    slots_all = jnp.sum(jnp.where(adapter_ids[:, None] == id_table, owner_map[None, :], 0), axis=1)
    slots = lax.dynamic_slice_in_dim(slots_all, replica_at * rows, rows)
    lane = lax.broadcasted_iota(jnp.int32, (1, stored * rank), 1) // rank
    picks = jnp.concatenate(
        [
            (slots[:, None] == ((replica_at - k) % replicas) * stored + lane).astype(jnp.float32)
            for k in range(replicas)
        ],
        axis=1,
    )
    column = lax.broadcasted_iota(jnp.int32, (rows, rows * length), 1)
    row = lax.broadcasted_iota(jnp.int32, (rows, rows * length), 0)
    live = ((column // length == row) & (column % length < kv_lengths[:, None])).astype(jnp.float32)

    query_down = with_swapped(query_down_maps)
    query_up = with_swapped(query_up_maps)
    output_down = with_swapped(output_down_maps)
    output_up = with_swapped(output_up_maps)

    low, near = low_call(hidden, picks, query_down)
    where = {0: (near, 0)}
    chain = 0
    for bit in reversed(bits):
        rest = [k for k in where if k not in (0, chain)]
        where[bit] = (across(hidden, bit), 0)
        if chain:
            joined = jnp.concatenate([where[chain][0][:, :width], low.astype(jnp.bfloat16)], axis=1)
            got = across(joined, bit)
            where[chain | bit] = (got, 0)
            low = low + got[:, width:].astype(jnp.float32)
        else:
            low = low + across(low, bit)
        if rest and bit == 1:
            got = jnp.concatenate([where[k][0][:, :width] for k in rest], axis=0)
            got = across(got, 1)
            for i, k in enumerate(rest):
                where[k | 1] = (got, i * rows)
        else:
            for k in rest:
                where[k | bit] = (across(where[k][0][:, :width], bit), 0)
        chain |= bit

    top = bits[-1] if bits else 0
    order = sorted(where, key=lambda k: (bin(k).count("1"), -k))
    last = order[-1]
    early = order[:-1]
    first = [k for k in early if k in (0, top >> 1, top)]
    others = [k for k in early if k not in first]
    query = project_call(where, first, tensor_at, w_query, None, rows, width)
    for i in range(0, len(others), 6):
        query = project_call(where, others[i : i + 6], tensor_at, w_query, query, rows, width)

    wide = w_query.shape[1]
    local_heads = wide // head
    group_all = HEADS // KVS
    kv_count = max(1, local_heads // group_all)
    group = local_heads // kv_count
    out_width = output_weight.shape[1] // shards
    depth = output_weight.shape[0]
    whole = shards - 1
    even = [k for k in sorted(where, reverse=True) if not k & 1]
    odd = [k for k in sorted(where, reverse=True) if k & 1 and k != whole]
    k_outs = [whole] + odd[:-1][:1]
    sizes = (last, k_outs, replicas, kv_count, group, head, local_heads, group_all, width)
    low2, mixed, payload, *blocks = pl.pallas_call(
        functools.partial(mix_kernel, sizes),
        in_specs=[SMEM, VMEM, HBM, HBM, VMEM, VMEM, VMEM] + [VMEM] * (2 * replicas) + [HBM, HBM, VMEM],
        out_specs=[VMEM] * (2 + len(k_outs)),
        out_shape=[
            jax.ShapeDtypeStruct((rows, LANES), jnp.float32),
            jax.ShapeDtypeStruct((rows, wide), jnp.bfloat16),
            jax.ShapeDtypeStruct((rows, out_width + LANES), jnp.bfloat16),
        ]
        + [jax.ShapeDtypeStruct((rows, out_width), jnp.bfloat16)] * (len(k_outs) - 1),
        scratch_shapes=[
            pltpu.VMEM((1, width, wide), w_query.dtype),
            pltpu.SemaphoreType.DMA((1, PIECES)),
            pltpu.VMEM((len(k_outs), depth, out_width), output_weight.dtype),
            pltpu.SemaphoreType.DMA((len(k_outs), PIECES)),
            pltpu.VMEM((rows, kv_count, length, head), keys.dtype),
            pltpu.VMEM((rows, kv_count, length, head), values.dtype),
            pltpu.SemaphoreType.DMA((2,)),
        ],
        name="mix",
        **params((10**9, 6 << 20)),
    )(
        tensor_at,
        where[last][0],
        in_hbm(w_query),
        in_hbm(output_weight),
        query,
        low,
        picks,
        *query_up,
        *output_down,
        in_hbm(keys),
        in_hbm(values),
        live,
    )

    came = {whole: across(payload, 1)}
    chain = [whole]
    while chain[-1]:
        chain.append(chain[-1] & (chain[-1] - 1))
    for k, array in zip(k_outs[1:], blocks):
        came[k] = across(array, 1)
    odd = [k for k in odd if k not in k_outs]
    parts = {}
    plan = [even[:1] + odd[:-1] + even[1:2], even[2:-1] + odd[-1:], even[-1:]]
    for ks in plan:
        if not ks:
            continue
        groups = [([k], jnp.bfloat16 if k & 1 else jnp.float32) for k in ks if k not in parts]
        arrays = out_call(groups, tensor_at, mixed, output_weight, out_width)
        for k, array in zip(ks, arrays):
            if k & 1:
                came[k] = across(array, 1)
            else:
                parts[k] = array
    for k in sorted((k for k in where if k and not k & 1), key=lambda k: (low_bit(k), -k)):
        main = parts[k]
        bit = 1
        while bit < low_bit(k):
            main = main + came[k | bit][:, :out_width].astype(jnp.float32)
            bit *= 2
        if k in chain:
            carried = low2
            for c in chain[: chain.index(k)]:
                carried = carried + came[c][:, out_width:].astype(jnp.float32)
            main = jnp.concatenate([main, carried], axis=1)
        came[k] = across(main.astype(jnp.bfloat16), low_bit(k))
    lows = [came[k] for k in chain[:-1]]
    terms = [parts[0]] + [came[1 << i] for i in range(len(bits) - 1)]
    return pl.pallas_call(
        functools.partial(final_kernel, out_width, (len(lows), len(terms)), replicas),
        in_specs=[VMEM] * (2 + replicas + len(lows) + len(terms)),
        out_specs=VMEM,
        out_shape=jax.ShapeDtypeStruct((rows, out_width), jnp.bfloat16),
        name="final",
        **params((10**8, 10**6)),
    )(picks, low2, *output_up, *lows, *terms)


def solution(mesh):
    sizes = dict(mesh.shape)

    def body(*arrays):
        return per_device(sizes, *arrays)

    return jax.shard_map(
        body,
        mesh=mesh,
        in_specs=(
            P(("groups", "replica"), "tensor"),
            P(None, "tensor"),
            P("tensor", None),
            P(("groups", "replica"), None, None, None),
            P(("groups", "replica"), None, None, None),
            P(("groups", "replica"), None, "tensor"),
            P(("groups", "replica"), None, "tensor"),
            P(("groups", "replica"), None, "tensor"),
            P(("groups", "replica"), None, "tensor"),
            P("groups"),
            P("groups"),
            P(("groups", "replica")),
        ),
        out_specs=P(("groups", "replica"), "tensor"),
        check_vma=False,
    )
```

```python
import functools
import math

import jax
import jax.numpy as jnp
from jax import lax
from jax.experimental import pallas as pl
from jax.experimental.pallas import tpu as pltpu
from jax.sharding import PartitionSpec as P

HEADS = 64
KVS = 8
VMEM = pl.BlockSpec(memory_space=pltpu.VMEM)
SMEM = pl.BlockSpec(memory_space=pltpu.SMEM)
HBM = pl.BlockSpec(memory_space=pltpu.HBM)
LANES = 128
PIECES = 4
GRANT = 24 << 20
SOON = 2
BAND = 32


def dot(a, b):
    return jnp.dot(a, b, preferred_element_type=jnp.float32)


def dot_t(a, b):
    return lax.dot_general(a, b, (((1,), (1,)), ((), ())), preferred_element_type=jnp.float32)


def params(flops_bytes, limit=GRANT):
    return dict(
        compiler_params=pltpu.CompilerParams(vmem_limit_bytes=limit),
        cost_estimate=pl.CostEstimate(
            flops=flops_bytes[0], bytes_accessed=flops_bytes[1], transcendentals=0
        ),
    )


def low_of(x, downs, picks):
    total = 0.0
    at = 0
    for down in downs:
        wide = down.shape[0]
        part = dot_t(x, down[...]) * picks[:, at : at + wide]
        for g in range(0, wide, LANES):
            total = total + part[:, g : g + LANES]
        at += wide
    return total


def lora_of(low, ups, picks):
    total = 0.0
    at = 0
    low = low.astype(jnp.bfloat16).astype(jnp.float32)
    for up in ups:
        wide = up.shape[0]
        spread = jnp.concatenate([low] * (wide // LANES), axis=1) * picks[:, at : at + wide]
        total = total + dot(spread.astype(jnp.bfloat16), up[...])
        at += wide
    return total


def in_hbm(x):
    return pltpu.with_memory_space_constraint(x, pltpu.HBM)


def load_all(pairs, sems):
    copies = [pltpu.make_async_copy(src, dst, sems.at[i]) for i, (src, dst) in enumerate(pairs)]
    for c in copies:
        c.start()
    return copies


def low_kernel(count, x_hbm, picks_ref, *rest):
    downs, (out_ref, x_ref), bufs, sems = rest[:count], rest[count : count + 2], rest[count + 2 : -1], rest[-1]
    for c in load_all([(x_hbm, x_ref)] + list(zip(downs, bufs)), sems):
        c.wait()
    out_ref[...] = low_of(x_ref[...], bufs, picks_ref[...])


def low_call(x, picks, downs):
    return pl.pallas_call(
        functools.partial(low_kernel, len(downs)),
        in_specs=[HBM, VMEM] + [HBM] * len(downs),
        out_specs=[VMEM] * 2,
        out_shape=[
            jax.ShapeDtypeStruct((x.shape[0], LANES), jnp.float32),
            jax.ShapeDtypeStruct(x.shape, x.dtype),
        ],
        scratch_shapes=[pltpu.VMEM(d.shape, d.dtype) for d in downs]
        + [pltpu.SemaphoreType.DMA((1 + len(downs),))],
        name="low",
        **params((10**8, 10**6)),
    )(in_hbm(x), picks, in_hbm(downs[0]), *downs[1:])


def weight_copies(weight, buf, sems, j, block, along):
    depth, wide = buf.shape[1], buf.shape[2]
    piece = depth // PIECES
    copies = []
    for p in range(PIECES):
        if along == 0:
            src = weight.at[pl.ds(pl.multiple_of(block * depth + p * piece, piece), piece), :]
        else:
            src = weight.at[p * piece : (p + 1) * piece, pl.ds(pl.multiple_of(block * wide, LANES), wide)]
        copies.append(
            pltpu.make_async_copy(src, buf.at[j, p * piece : (p + 1) * piece, :], sems.at[j, p])
        )
    return copies


def block_dot(x_ref_read, buf, j, copies, total):
    piece = buf.shape[1] // PIECES
    for p in range(PIECES):
        copies[p].wait()
        total = total + dot(
            x_ref_read(p * piece, piece), buf[j, p * piece : (p + 1) * piece, :]
        )
    return total


def project_kernel(ks, held_count, spans, given, tensor_ref, *rest):
    arrays, rest = rest[:given], rest[given:]
    weight, before, rest = rest[0], rest[1], rest[2:]
    if held_count:
        held, rest = rest[0], rest[1:]
    out_ref, buf, sems = rest
    rows = out_ref.shape[0]
    width = buf.shape[1]
    later = ks[held_count:]
    copies = [weight_copies(weight, buf, sems, j, tensor_ref[0] ^ k, 0) for j, k in enumerate(later)]
    for c in sum(copies, []):
        c.start()
    total = before[...]
    for j, (i, r) in enumerate(spans):
        if j < held_count:
            total = total + dot(arrays[i][r : r + rows, :width], held[j])
        else:
            total = block_dot(
                lambda a, n, i=i, r=r: arrays[i][r : r + rows, a : a + n],
                buf,
                j - held_count,
                copies[j - held_count],
                total,
            )
    out_ref[...] = total


def project_call(where, ks, tensor_at, weight, before, width, held=None):
    rows, wide = before.shape
    arrays, spans = [], []
    for k in ks:
        array, r = where[k]
        if not any(a is array for a in arrays):
            arrays.append(array)
        spans.append(([a is array for a in arrays].index(True), r))
    extra = [] if held is None else [held]
    held_count = 0 if held is None else held.shape[0]
    count = len(ks) - held_count
    return pl.pallas_call(
        functools.partial(project_kernel, ks, held_count, spans, len(arrays)),
        in_specs=[SMEM] + [VMEM] * len(arrays) + [HBM] + [VMEM] * (1 + len(extra)),
        out_specs=VMEM,
        out_shape=jax.ShapeDtypeStruct((rows, wide), jnp.float32),
        scratch_shapes=[
            pltpu.VMEM((count, width, wide), weight.dtype),
            pltpu.SemaphoreType.DMA((count, PIECES)),
        ],
        **params((2 * len(ks) * rows * width * wide, 2 * count * width * wide)),
    )(tensor_at, *arrays, in_hbm(weight), before, *extra)


def lead_kernel(k, ahead, tensor_ref, chunk, weight, out_ref, ahead_ref, buf, sems, ahead_sems):
    copies = weight_copies(weight, buf, sems, 0, tensor_ref[0] ^ k, 0)
    later = [
        weight_copies(weight, ahead_ref, ahead_sems, j, tensor_ref[0] ^ a, 0)
        for j, a in enumerate(ahead)
    ]
    for c in copies + sum(later, []):
        c.start()
    out_ref[...] = block_dot(lambda a, n: chunk[:, a : a + n], buf, 0, copies, 0.0)
    for c in sum(later, []):
        c.wait()


def lead_call(chunk, k, ahead, tensor_at, weight):
    rows, width = chunk.shape
    wide = weight.shape[1]
    return pl.pallas_call(
        functools.partial(lead_kernel, k, ahead),
        in_specs=[SMEM, VMEM, HBM],
        out_specs=[VMEM] * 2,
        out_shape=[
            jax.ShapeDtypeStruct((rows, wide), jnp.float32),
            jax.ShapeDtypeStruct((len(ahead), width, wide), weight.dtype),
        ],
        scratch_shapes=[
            pltpu.VMEM((1, width, wide), weight.dtype),
            pltpu.SemaphoreType.DMA((1, PIECES)),
            pltpu.SemaphoreType.DMA((len(ahead), PIECES)),
        ],
        name="lead",
        **params((2 * rows * width * wide, 2 * (1 + len(ahead)) * width * wide)),
    )(tensor_at, chunk, in_hbm(weight))


def held_kernel(count, ahead, tensor_ref, *refs):
    chunks, refs = refs[:count], refs[count:]
    held, before, weight, out_ref, ahead_ref, ahead_sems = refs
    later = [
        weight_copies(weight, ahead_ref, ahead_sems, j, tensor_ref[0] ^ a, 0)
        for j, a in enumerate(ahead)
    ]
    for c in sum(later, []):
        c.start()
    rows, width = out_ref.shape[0], held.shape[1]
    total = before[...]
    for j in range(count):
        total = total + dot(chunks[j][:rows, :width], held[j])
    out_ref[...] = total
    for c in sum(later, []):
        c.wait()


def held_call(chunks, held, before, ahead, tensor_at, weight):
    _, width, wide = held.shape
    return pl.pallas_call(
        functools.partial(held_kernel, len(chunks), ahead),
        in_specs=[SMEM] + [VMEM] * (len(chunks) + 2) + [HBM],
        out_specs=[VMEM] * 2,
        out_shape=[
            jax.ShapeDtypeStruct(before.shape, before.dtype),
            jax.ShapeDtypeStruct((len(ahead), width, wide), weight.dtype),
        ],
        scratch_shapes=[pltpu.SemaphoreType.DMA((len(ahead), PIECES))],
        name="held",
        **params((2 * before.size * width * len(chunks), 2 * len(ahead) * width * wide), 8 << 20),
    )(tensor_at, *chunks, held, before, in_hbm(weight))


def mix_kernel(sizes, *refs):
    k_in, k_outs, maps, kv_count, group, head, local_heads, group_all, _ = sizes
    refs = list(refs)
    tensor_ref, chunk, w_in, w_out, before, low, picks = [refs.pop(0) for _ in range(7)]
    ups = [refs.pop(0) for _ in range(maps)]
    downs = [refs.pop(0) for _ in range(maps)]
    keys, values, live = [refs.pop(0) for _ in range(3)]
    low_out, mixed_out, block_out = [refs.pop(0) for _ in range(3)]
    more_outs = [refs.pop(0) for _ in k_outs[1:]]
    buf_in, sem_in, buf_out, sem_out, k_buf, v_buf, up_buf, down_buf, sems = refs

    tensor_at = tensor_ref[0]
    copies_in = weight_copies(w_in, buf_in, sem_in, 0, tensor_at ^ k_in, 0)
    copies_out = [
        weight_copies(w_out, buf_out, sem_out, j, tensor_at ^ k, 1) for j, k in enumerate(k_outs)
    ]
    kv = pl.ds(tensor_at * local_heads // group_all, kv_count)
    up_copies = load_all([(u, up_buf.at[i]) for i, u in enumerate(ups)], sems.at[0])
    for c in copies_in:
        c.start()
    kv_copies = load_all([(keys.at[:, kv], k_buf), (values.at[:, kv], v_buf)], sems.at[1])
    down_copies = load_all([(d, down_buf.at[i]) for i, d in enumerate(downs)], sems.at[2])
    for pieces in copies_out:
        for c in pieces:
            c.start()

    rows = before.shape[0]
    picked = picks[...]
    for c in up_copies:
        c.wait()
    total = before[...] + 0.5 * lora_of(low[...], [up_buf.at[i] for i in range(maps)], picked)
    total = block_dot(lambda a, n: chunk[:, a : a + n], buf_in, 0, copies_in, total)
    for c in kv_copies:
        c.wait()
    length = k_buf.shape[2]
    bands = []
    for r in range(0, rows, BAND):
        alive = jnp.concatenate([live[r : r + BAND, :]] * group, axis=0) > 0
        heads = []
        for kvh in range(kv_count):
            flat_k = k_buf[r : r + BAND, kvh].reshape(BAND * length, head)
            flat_v = v_buf[r : r + BAND, kvh].reshape(BAND * length, head)
            at = [slice((kvh * group + g) * head, (kvh * group + g + 1) * head) for g in range(group)]
            q = jnp.concatenate([total[r : r + BAND, span] for span in at], axis=0)
            scores = dot_t(q.astype(jnp.bfloat16), flat_k) * (1.0 / math.sqrt(head))
            scores = jnp.where(alive, scores, -1e30)
            top = jnp.max(scores, axis=1, keepdims=True)
            weights = jnp.exp(scores - top)
            probs = weights * (1.0 / jnp.sum(weights, axis=1, keepdims=True))
            got = dot(probs.astype(jnp.bfloat16), flat_v)
            heads += [got[g * BAND : (g + 1) * BAND] for g in range(group)]
        bands.append(jnp.concatenate(heads, axis=1))
    mixed = jnp.concatenate(bands, axis=0).astype(jnp.bfloat16)
    mixed_out[...] = mixed
    for c in down_copies:
        c.wait()
    low_part = low_of(mixed, [down_buf.at[i] for i in range(maps)], picked)
    low_out[...] = low_part
    block = block_dot(lambda a, n: mixed[:, a : a + n], buf_out, 0, copies_out[0], 0.0)
    wide = block.shape[1]
    block_out[:, :wide] = block.astype(block_out.dtype)
    block_out[:, wide:] = low_part.astype(block_out.dtype)
    for j, ref in enumerate(more_outs):
        ref[...] = block_dot(
            lambda a, n: mixed[:, a : a + n], buf_out, j + 1, copies_out[j + 1], 0.0
        )


def out_kernel(ks, spans, tensor_ref, x_ref, weight, *rest):
    outs, (buf, sems) = rest[:-2], rest[-2:]
    rows = x_ref.shape[0]
    copies = [weight_copies(weight, buf, sems, j, tensor_ref[0] ^ k, 1) for j, k in enumerate(ks)]
    for pieces in copies:
        for c in pieces:
            c.start()
    for j, (i, r) in enumerate(spans):
        block = block_dot(lambda a, n: x_ref[:, a : a + n], buf, j, copies[j], 0.0)
        outs[i][r : r + rows, :] = block.astype(outs[i].dtype)


def out_call(groups, tensor_at, mixed, weight, out_width):
    rows, depth = mixed.shape
    ks = [k for group, _ in groups for k in group]
    spans = [(i, r * rows) for i, (group, _) in enumerate(groups) for r in range(len(group))]
    return pl.pallas_call(
        functools.partial(out_kernel, ks, spans),
        in_specs=[SMEM, VMEM, HBM],
        out_specs=[VMEM] * len(groups),
        out_shape=[jax.ShapeDtypeStruct((rows * len(group), out_width), kind) for group, kind in groups],
        scratch_shapes=[
            pltpu.VMEM((len(ks), depth, out_width), weight.dtype),
            pltpu.SemaphoreType.DMA((len(ks), PIECES)),
        ],
        **params((2 * len(ks) * rows * depth * out_width, 2 * len(ks) * depth * out_width)),
    )(tensor_at, mixed, in_hbm(weight))


def final_kernel(wide, count, maps, picks_ref, low_ref, *rest):
    ups, rest = rest[:maps], rest[maps:]
    lows, rest = rest[: count[0]], rest[count[0] :]
    terms, rest = rest[: count[1]], rest[count[1] :]
    (out_ref,) = rest
    low = low_ref[...]
    total = 0.0
    for ref in lows:
        low = low + ref[:, wide:].astype(jnp.float32)
    total = lows[-1][:, :wide].astype(jnp.float32)
    for t in terms:
        total = total + t[:, :wide].astype(jnp.float32)
    total = total + 0.5 * lora_of(low, ups, picks_ref[...])
    out_ref[...] = total.astype(out_ref.dtype)


def low_bit(k):
    return k & -k


def per_device(
    mesh_shape,
    hidden,
    w_query,
    output_weight,
    keys,
    values,
    query_down_maps,
    query_up_maps,
    output_down_maps,
    output_up_maps,
    adapter_ids,
    owner_map,
    kv_lengths,
):
    rows, width = hidden.shape
    head = keys.shape[3]
    length = keys.shape[2]
    shards = mesh_shape["tensor"]
    replicas = mesh_shape["replica"]
    stored, rank = query_down_maps.shape[:2]
    replica_at = lax.axis_index("replica")
    tensor_at = lax.axis_index("tensor").astype(jnp.int32).reshape(1)
    bits = []
    while (1 << len(bits)) < shards:
        bits.append(1 << len(bits))

    def across(x, bit):
        return lax.ppermute(x, "tensor", [(i, i ^ bit) for i in range(shards)])

    def with_swapped(x):
        x = x.reshape(stored * rank, x.shape[2])
        return [x] + [
            lax.ppermute(x, "replica", [(i, (i + k) % replicas) for i in range(replicas)])
            for k in range(1, replicas)
        ]

    id_table = lax.broadcasted_iota(jnp.int32, (1, owner_map.shape[0]), 1)
    slots_all = jnp.sum(jnp.where(adapter_ids[:, None] == id_table, owner_map[None, :], 0), axis=1)
    slots = lax.dynamic_slice_in_dim(slots_all, replica_at * rows, rows)
    lane = lax.broadcasted_iota(jnp.int32, (1, stored * rank), 1) // rank
    picks = jnp.concatenate(
        [
            (slots[:, None] == ((replica_at - k) % replicas) * stored + lane).astype(jnp.float32)
            for k in range(replicas)
        ],
        axis=1,
    )
    column = lax.broadcasted_iota(jnp.int32, (rows, BAND * length), 1)
    row = lax.broadcasted_iota(jnp.int32, (rows, BAND * length), 0)
    live = (column // length == row % BAND) & (column % length < kv_lengths[:, None])
    live = live.astype(jnp.float32)

    query_down = with_swapped(query_down_maps)
    query_up = with_swapped(query_up_maps)
    output_down = with_swapped(output_down_maps)
    output_up = with_swapped(output_up_maps)

    low, near = low_call(hidden, picks, query_down)
    where = {0: (near, 0)}
    chain = 0
    for bit in reversed(bits):
        rest = [k for k in where if k != chain]
        if chain == 0:
            where[bit] = (across(hidden, bit), 0)
            low = low + across(low, bit)
        else:
            joined = jnp.concatenate([where[chain][0][:, :width], low.astype(jnp.bfloat16)], axis=1)
            got = across(joined, bit)
            where[chain | bit] = (got, 0)
            low = low + got[:, width:].astype(jnp.float32)
        if rest and bit == 1:
            got = jnp.concatenate([where[k][0][:, :width] for k in rest], axis=0)
            got = across(got, 1)
            for i, k in enumerate(rest):
                where[k | 1] = (got, i * rows)
        else:
            for k in rest:
                array = hidden if k == 0 else where[k][0][:, :width]
                where[k | bit] = (across(array, bit), 0)
        chain |= bit

    last = chain
    ahead = [k for k in where if k and not k & 1 and k != last ^ 1]
    second = [last ^ 1] + [k for k in where if k & 1 and k != last]
    query, held = lead_call(near, 0, ahead, tensor_at, w_query)
    chunks = [where[k][0] for k in ahead]
    query, held = held_call(chunks, held, query, second[:SOON], tensor_at, w_query)
    query = project_call(where, second, tensor_at, w_query, query, width, held)

    wide = w_query.shape[1]
    local_heads = wide // head
    group_all = HEADS // KVS
    kv_count = max(1, local_heads // group_all)
    group = local_heads // kv_count
    out_width = output_weight.shape[1] // shards
    depth = output_weight.shape[0]
    whole = shards - 1
    even = [k for k in sorted(where, reverse=True) if not k & 1]
    k_outs = [whole] + even[:-1][:1]
    sizes = (last, k_outs, replicas, kv_count, group, head, local_heads, group_all, width)
    map_in, map_out = (stored * rank, wide), (stored * rank, depth)
    low2, mixed, payload, *blocks = pl.pallas_call(
        functools.partial(mix_kernel, sizes),
        in_specs=[SMEM, VMEM, HBM, HBM, VMEM, VMEM, VMEM] + [HBM] * (2 * replicas) + [HBM, HBM, VMEM],
        out_specs=[VMEM] * (2 + len(k_outs)),
        out_shape=[
            jax.ShapeDtypeStruct((rows, LANES), jnp.float32),
            jax.ShapeDtypeStruct((rows, wide), jnp.bfloat16),
            jax.ShapeDtypeStruct((rows, out_width + LANES), jnp.bfloat16),
        ]
        + [jax.ShapeDtypeStruct((rows, out_width), jnp.float32)] * (len(k_outs) - 1),
        scratch_shapes=[
            pltpu.VMEM((1, width, wide), w_query.dtype),
            pltpu.SemaphoreType.DMA((1, PIECES)),
            pltpu.VMEM((len(k_outs), depth, out_width), output_weight.dtype),
            pltpu.SemaphoreType.DMA((len(k_outs), PIECES)),
            pltpu.VMEM((rows, kv_count, length, head), keys.dtype),
            pltpu.VMEM((rows, kv_count, length, head), values.dtype),
            pltpu.VMEM((replicas,) + map_in, keys.dtype),
            pltpu.VMEM((replicas,) + map_out, keys.dtype),
            pltpu.SemaphoreType.DMA((3, max(2, replicas))),
        ],
        name="mix",
        **params((10**9, 6 << 20)),
    )(
        tensor_at,
        where[last][0],
        in_hbm(w_query),
        in_hbm(output_weight),
        query,
        low,
        picks,
        *query_up,
        *output_down,
        in_hbm(keys),
        in_hbm(values),
        live,
    )

    came = {whole: across(payload, 1)}
    chain = [whole]
    while chain[-1]:
        chain.append(chain[-1] & (chain[-1] - 1))
    odd = [k for k in sorted(where, reverse=True) if k & 1 and k not in (whole, 1)]
    f32, bf16 = jnp.float32, jnp.bfloat16
    parts = dict(zip(k_outs[1:], blocks))
    even = [k for k in even if k not in parts]
    plan = [
        [(odd, bf16)] * bool(odd),
        [([k], f32) for k in even[:-1]] + [([1], bf16)] * (whole > 1),
        [([k], f32) for k in even[-1:]],
    ]
    plan = [groups for groups in plan if groups]
    for groups in plan:
        arrays = out_call(groups, tensor_at, mixed, output_weight, out_width)
        for (g, kind), array in zip(groups, arrays):
            if kind == bf16:
                got = across(array, 1)
                for i, k in enumerate(g):
                    came[k] = got[i * rows : (i + 1) * rows]
            else:
                parts[g[0]] = array
    for k in sorted((k for k in where if k and not k & 1), key=lambda k: (low_bit(k), -k)):
        main = parts[k]
        bit = 1
        while bit < low_bit(k):
            main = main + came[k | bit][:, :out_width].astype(jnp.float32)
            bit *= 2
        if k in chain:
            carried = low2
            for c in chain[: chain.index(k)]:
                carried = carried + came[c][:, out_width:].astype(jnp.float32)
            main = jnp.concatenate([main, carried], axis=1)
        came[k] = across(main.astype(jnp.bfloat16), low_bit(k))
    lows = [came[k] for k in chain[:-1]]
    terms = [parts[0]] + [came[1 << i] for i in range(len(bits) - 1)]
    return pl.pallas_call(
        functools.partial(final_kernel, out_width, (len(lows), len(terms)), replicas),
        in_specs=[VMEM] * (2 + replicas + len(lows) + len(terms)),
        out_specs=VMEM,
        out_shape=jax.ShapeDtypeStruct((rows, out_width), jnp.bfloat16),
        name="final",
        **params((10**8, 10**6)),
    )(picks, low2, *output_up, *lows, *terms)


def solution(mesh):
    sizes = dict(mesh.shape)

    def body(*arrays):
        return per_device(sizes, *arrays)

    return jax.shard_map(
        body,
        mesh=mesh,
        in_specs=(
            P(("groups", "replica"), "tensor"),
            P(None, "tensor"),
            P("tensor", None),
            P(("groups", "replica"), None, None, None),
            P(("groups", "replica"), None, None, None),
            P(("groups", "replica"), None, "tensor"),
            P(("groups", "replica"), None, "tensor"),
            P(("groups", "replica"), None, "tensor"),
            P(("groups", "replica"), None, "tensor"),
            P("groups"),
            P("groups"),
            P(("groups", "replica")),
        ),
        out_specs=P(("groups", "replica"), "tensor"),
        check_vma=False,
    )
```

```python
import functools
import math

import jax
import jax.numpy as jnp
from jax import lax
from jax.experimental import pallas as pl
from jax.experimental.pallas import tpu as pltpu
from jax.sharding import PartitionSpec as P

HEADS = 64
KVS = 8
VMEM = pl.BlockSpec(memory_space=pltpu.VMEM)
SMEM = pl.BlockSpec(memory_space=pltpu.SMEM)
HBM = pl.BlockSpec(memory_space=pltpu.HBM)
LANES = 128
PIECES = 4
GRANT = 12 << 20
BAND = 32


def dot(a, b):
    return jnp.dot(a, b, preferred_element_type=jnp.float32)


def dot_t(a, b):
    return lax.dot_general(a, b, (((1,), (1,)), ((), ())), preferred_element_type=jnp.float32)


def params(flops_bytes, limit=GRANT):
    return dict(
        compiler_params=pltpu.CompilerParams(vmem_limit_bytes=limit),
        cost_estimate=pl.CostEstimate(
            flops=flops_bytes[0], bytes_accessed=flops_bytes[1], transcendentals=0
        ),
    )


def low_of(x, downs, picks):
    total = 0.0
    at = 0
    for down in downs:
        wide = down.shape[0]
        part = dot_t(x, down[...]) * picks[:, at : at + wide]
        for g in range(0, wide, LANES):
            total = total + part[:, g : g + LANES]
        at += wide
    return total


def lora_of(low, ups, picks):
    total = 0.0
    at = 0
    low = low.astype(jnp.bfloat16).astype(jnp.float32)
    for up in ups:
        wide = up.shape[0]
        spread = jnp.concatenate([low] * (wide // LANES), axis=1) * picks[:, at : at + wide]
        total = total + dot(spread.astype(jnp.bfloat16), up[...])
        at += wide
    return total


def in_hbm(x):
    return pltpu.with_memory_space_constraint(x, pltpu.HBM)


def load_all(pairs, sems):
    copies = [pltpu.make_async_copy(src, dst, sems.at[i]) for i, (src, dst) in enumerate(pairs)]
    for c in copies:
        c.start()
    return copies


def low_kernel(count, hints, x_hbm, picks_ref, *rest):
    rest = rest[hints:]
    downs, (out_ref, x_ref), bufs, sems = rest[:count], rest[count : count + 2], rest[count + 2 : -1], rest[-1]
    for c in load_all([(x_hbm, x_ref)] + list(zip(downs, bufs)), sems):
        c.wait()
    out_ref[...] = low_of(x_ref[...], bufs, picks_ref[...])


def low_call(x, picks, downs, hints):
    return pl.pallas_call(
        functools.partial(low_kernel, len(downs), len(hints)),
        in_specs=[HBM, VMEM] + [HBM] * (len(hints) + len(downs)),
        out_specs=[VMEM] * 2,
        out_shape=[
            jax.ShapeDtypeStruct((x.shape[0], LANES), jnp.float32),
            jax.ShapeDtypeStruct(x.shape, x.dtype),
        ],
        scratch_shapes=[pltpu.VMEM(d.shape, d.dtype) for d in downs]
        + [pltpu.SemaphoreType.DMA((1 + len(downs),))],
        name="low",
        **params((10**8, 10**6)),
    )(in_hbm(x), picks, *[in_hbm(h) for h in hints], in_hbm(downs[0]), *downs[1:])


def lead_kernel(tensor_ref, chunk, weight, out_ref, buf, sems):
    width = buf.shape[0]
    piece = width // PIECES
    copies = []
    for p in range(PIECES):
        at = pl.multiple_of(tensor_ref[0] * width + p * piece, piece)
        spot = pl.ds(p * piece, piece)
        copies.append(pltpu.make_async_copy(weight.at[pl.ds(at, piece), :], buf.at[spot, :], sems.at[p]))
    for c in copies:
        c.start()
    total = 0.0
    for p, c in enumerate(copies):
        c.wait()
        span = slice(p * piece, (p + 1) * piece)
        total = total + dot(chunk[:, span], buf[span, :])
    out_ref[...] = total


def lead_call(chunk, tensor_at, weight):
    rows, width = chunk.shape
    wide = weight.shape[1]
    return pl.pallas_call(
        lead_kernel,
        in_specs=[SMEM, VMEM, HBM],
        out_specs=VMEM,
        out_shape=jax.ShapeDtypeStruct((rows, wide), jnp.float32),
        scratch_shapes=[
            pltpu.VMEM((width, wide), weight.dtype),
            pltpu.SemaphoreType.DMA((PIECES,)),
        ],
        name="lead",
        **params((2 * rows * width * wide, 2 * width * wide)),
    )(tensor_at, chunk, in_hbm(weight))


def dense_kernel(shards, ks, spans, given, first, tensor_ref, weight, *rest):
    arrays, rest = rest[:given], rest[given:]
    out_ref = rest[-1]
    rows, width = out_ref.shape[0], weight.shape[0] // shards
    total = 0.0 if first else rest[0][...]
    for k, (i, r) in zip(ks, spans):
        at = pl.multiple_of((tensor_ref[0] ^ k) * width, width)
        total = total + dot(arrays[i][r : r + rows, :width], weight[pl.ds(at, width), :])
    out_ref[...] = total


def dense_call(shards, where, ks, tensor_at, weight, before, rows, hints):
    wide = weight.shape[1]
    arrays, spans = [], []
    for k in ks:
        array, r = where[k]
        if not any(a is array for a in arrays):
            arrays.append(array)
        spans.append(([a is array for a in arrays].index(True), r))
    extra = [] if before is None else [before]
    return pl.pallas_call(
        functools.partial(dense_kernel, shards, ks, spans, len(arrays), before is None),
        in_specs=[SMEM, VMEM] + [VMEM] * (len(arrays) + len(extra)) + [HBM] * len(hints),
        out_specs=VMEM,
        out_shape=jax.ShapeDtypeStruct((rows, wide), jnp.float32),
        **params((2 * len(ks) * rows * weight.size // shards, 10**6), 6 << 20),
    )(tensor_at, weight, *arrays, *extra, *[in_hbm(h) for h in hints])


def mix_kernel(sizes, *refs):
    k_in, k_outs, maps, kv_count, group, head, local_heads, group_all, width = sizes
    refs = list(refs)
    tensor_ref, chunk, w_in, w_out, before, low, picks = [refs.pop(0) for _ in range(7)]
    ups = [refs.pop(0) for _ in range(maps)]
    downs = [refs.pop(0) for _ in range(maps)]
    keys, values, live = [refs.pop(0) for _ in range(3)]
    low_out, mixed_out, block_out = [refs.pop(0) for _ in range(3)]
    more_outs = [refs.pop(0) for _ in k_outs[1:]]
    k_buf, v_buf, up_buf, down_buf, sems = refs

    tensor_at = tensor_ref[0]
    kv = pl.ds(tensor_at * local_heads // group_all, kv_count)
    up_copies = load_all([(u, up_buf.at[i]) for i, u in enumerate(ups)], sems.at[0])
    kv_copies = load_all([(keys.at[:, kv], k_buf), (values.at[:, kv], v_buf)], sems.at[1])
    down_copies = load_all([(d, down_buf.at[i]) for i, d in enumerate(downs)], sems.at[2])

    rows = before.shape[0]
    picked = picks[...]
    for c in up_copies:
        c.wait()
    total = before[...] + 0.5 * lora_of(low[...], [up_buf.at[i] for i in range(maps)], picked)
    at = pl.multiple_of((tensor_at ^ k_in) * width, width)
    total = total + dot(chunk[:, :width], w_in[pl.ds(at, width), :])
    for c in kv_copies:
        c.wait()
    length = k_buf.shape[2]
    bands = []
    for r in range(0, rows, BAND):
        alive = jnp.concatenate([live[r : r + BAND, :]] * group, axis=0) > 0
        heads = []
        for kvh in range(kv_count):
            flat_k = k_buf[r : r + BAND, kvh].reshape(BAND * length, head)
            flat_v = v_buf[r : r + BAND, kvh].reshape(BAND * length, head)
            at = [slice((kvh * group + g) * head, (kvh * group + g + 1) * head) for g in range(group)]
            q = jnp.concatenate([total[r : r + BAND, span] for span in at], axis=0)
            scores = dot_t(q.astype(jnp.bfloat16), flat_k) * (1.0 / math.sqrt(head))
            scores = jnp.where(alive, scores, -1e30)
            top = jnp.max(scores, axis=1, keepdims=True)
            weights = jnp.exp(scores - top)
            probs = weights * (1.0 / jnp.sum(weights, axis=1, keepdims=True))
            got = dot(probs.astype(jnp.bfloat16), flat_v)
            heads += [got[g * BAND : (g + 1) * BAND] for g in range(group)]
        bands.append(jnp.concatenate(heads, axis=1))
    mixed = jnp.concatenate(bands, axis=0).astype(jnp.bfloat16)
    mixed_out[...] = mixed
    for c in down_copies:
        c.wait()
    low_part = low_of(mixed, [down_buf.at[i] for i in range(maps)], picked)
    low_out[...] = low_part
    wide = block_out.shape[1] - LANES
    block_out[:, wide:] = low_part.astype(block_out.dtype)
    for j, k in enumerate(k_outs):
        at = pl.multiple_of((tensor_at ^ k) * wide, LANES)
        block = dot(mixed, w_out[:, pl.ds(at, wide)])
        if j == 0:
            block_out[:, :wide] = block.astype(block_out.dtype)
        else:
            more_outs[j - 1][...] = block


def resident_kernel(ks, spans, tensor_ref, x_ref, weight, *outs):
    rows = x_ref.shape[0]
    wide = outs[0].shape[1]
    for k, (i, r) in zip(ks, spans):
        at = pl.multiple_of((tensor_ref[0] ^ k) * wide, LANES)
        block = dot(x_ref[...], weight[:, pl.ds(at, wide)])
        outs[i][r : r + rows, :] = block.astype(outs[i].dtype)


def resident_call(groups, tensor_at, mixed, weight, out_width):
    rows, _ = mixed.shape
    ks = [k for group, _ in groups for k in group]
    spans = [(i, r * rows) for i, (group, _) in enumerate(groups) for r in range(len(group))]
    return pl.pallas_call(
        functools.partial(resident_kernel, ks, spans),
        in_specs=[SMEM, VMEM, VMEM],
        out_specs=[VMEM] * len(groups),
        out_shape=[
            jax.ShapeDtypeStruct((rows * len(group), out_width), kind) for group, kind in groups
        ],
        compiler_params=pltpu.CompilerParams(vmem_limit_bytes=6 << 20),
    )(tensor_at, mixed, weight)


def final_kernel(wide, count, maps, picks_ref, low_ref, *rest):
    ups, rest = rest[:maps], rest[maps:]
    lows, rest = rest[: count[0]], rest[count[0] :]
    terms, rest = rest[: count[1]], rest[count[1] :]
    (out_ref,) = rest
    low = low_ref[...]
    total = 0.0
    for ref in lows:
        low = low + ref[:, wide:].astype(jnp.float32)
    total = lows[-1][:, :wide].astype(jnp.float32)
    for t in terms:
        total = total + t[:, :wide].astype(jnp.float32)
    total = total + 0.5 * lora_of(low, ups, picks_ref[...])
    out_ref[...] = total.astype(out_ref.dtype)


def low_bit(k):
    return k & -k


def per_device(
    mesh_shape,
    hidden,
    w_query,
    output_weight,
    keys,
    values,
    query_down_maps,
    query_up_maps,
    output_down_maps,
    output_up_maps,
    adapter_ids,
    owner_map,
    kv_lengths,
):
    rows, width = hidden.shape
    head = keys.shape[3]
    length = keys.shape[2]
    shards = mesh_shape["tensor"]
    replicas = mesh_shape["replica"]
    stored, rank = query_down_maps.shape[:2]
    replica_at = lax.axis_index("replica")
    tensor_at = lax.axis_index("tensor").astype(jnp.int32).reshape(1)
    bits = []
    while (1 << len(bits)) < shards:
        bits.append(1 << len(bits))

    def across(x, bit):
        return lax.ppermute(x, "tensor", [(i, i ^ bit) for i in range(shards)])

    def with_swapped(x):
        x = x.reshape(stored * rank, x.shape[2])
        return [x] + [
            lax.ppermute(x, "replica", [(i, (i + k) % replicas) for i in range(replicas)])
            for k in range(1, replicas)
        ]

    id_table = lax.broadcasted_iota(jnp.int32, (1, owner_map.shape[0]), 1)
    slots_all = jnp.sum(jnp.where(adapter_ids[:, None] == id_table, owner_map[None, :], 0), axis=1)
    slots = lax.dynamic_slice_in_dim(slots_all, replica_at * rows, rows)
    lane = lax.broadcasted_iota(jnp.int32, (1, stored * rank), 1) // rank
    picks = jnp.concatenate(
        [
            (slots[:, None] == ((replica_at - k) % replicas) * stored + lane).astype(jnp.float32)
            for k in range(replicas)
        ],
        axis=1,
    )
    column = lax.broadcasted_iota(jnp.int32, (rows, BAND * length), 1)
    row = lax.broadcasted_iota(jnp.int32, (rows, BAND * length), 0)
    live = (column // length == row % BAND) & (column % length < kv_lengths[:, None])
    live = live.astype(jnp.float32)

    query_down = with_swapped(query_down_maps)
    query_up = with_swapped(query_up_maps)
    output_down = with_swapped(output_down_maps)
    output_up = with_swapped(output_up_maps)

    low, near = low_call(hidden, picks, query_down, [])
    where = {0: (near, 0)}
    chain = 0
    for bit in reversed(bits):
        rest = [k for k in where if k != chain]
        if chain == 0:
            where[bit] = (across(hidden, bit), 0)
            low = low + across(low, bit)
        else:
            joined = jnp.concatenate([where[chain][0][:, :width], low.astype(jnp.bfloat16)], axis=1)
            got = across(joined, bit)
            where[chain | bit] = (got, 0)
            low = low + got[:, width:].astype(jnp.float32)
        if rest and bit == 1:
            got = jnp.concatenate([where[k][0][:, :width] for k in rest], axis=0)
            got = across(got, 1)
            for i, k in enumerate(rest):
                where[k | 1] = (got, i * rows)
        else:
            for k in rest:
                array = hidden if k == 0 else where[k][0][:, :width]
                where[k | bit] = (across(array, bit), 0)
        chain |= bit

    last = chain
    ahead = [k for k in where if k and not k & 1 and k != last ^ 1]
    second = [last ^ 1] + [k for k in where if k & 1 and k != last]
    query = lead_call(near, tensor_at, w_query)
    for ks, hints in ((ahead, [output_weight]), (second, [])):
        query = dense_call(shards, where, ks, tensor_at, w_query, query, rows, hints)

    wide = w_query.shape[1]
    local_heads = wide // head
    group_all = HEADS // KVS
    kv_count = max(1, local_heads // group_all)
    group = local_heads // kv_count
    out_width = output_weight.shape[1] // shards
    depth = output_weight.shape[0]
    whole = shards - 1
    even = [k for k in sorted(where, reverse=True) if not k & 1]
    k_outs = [whole] + even[:-1][:1]
    sizes = (last, k_outs, replicas, kv_count, group, head, local_heads, group_all, width)
    map_in, map_out = (stored * rank, wide), (stored * rank, depth)
    low2, mixed, payload, *blocks = pl.pallas_call(
        functools.partial(mix_kernel, sizes),
        in_specs=[SMEM, VMEM, VMEM, VMEM, VMEM, VMEM, VMEM] + [HBM] * (2 * replicas) + [HBM, HBM, VMEM],
        out_specs=[VMEM] * (2 + len(k_outs)),
        out_shape=[
            jax.ShapeDtypeStruct((rows, LANES), jnp.float32),
            jax.ShapeDtypeStruct((rows, wide), jnp.bfloat16),
            jax.ShapeDtypeStruct((rows, out_width + LANES), jnp.bfloat16),
        ]
        + [jax.ShapeDtypeStruct((rows, out_width), jnp.float32)] * (len(k_outs) - 1),
        scratch_shapes=[
            pltpu.VMEM((rows, kv_count, length, head), keys.dtype),
            pltpu.VMEM((rows, kv_count, length, head), values.dtype),
            pltpu.VMEM((replicas,) + map_in, keys.dtype),
            pltpu.VMEM((replicas,) + map_out, keys.dtype),
            pltpu.SemaphoreType.DMA((3, max(2, replicas))),
        ],
        name="mix",
        **params((10**9, 6 << 20)),
    )(
        tensor_at,
        where[last][0],
        w_query,
        output_weight,
        query,
        low,
        picks,
        *query_up,
        *output_down,
        in_hbm(keys),
        in_hbm(values),
        live,
    )

    came = {whole: across(payload, 1)}
    chain = [whole]
    while chain[-1]:
        chain.append(chain[-1] & (chain[-1] - 1))
    odd = [k for k in sorted(where, reverse=True) if k & 1 and k not in (whole, 1)]
    f32, bf16 = jnp.float32, jnp.bfloat16
    parts = dict(zip(k_outs[1:], blocks))
    even = [k for k in even if k not in parts]
    plan = [
        [(odd, bf16)] * bool(odd),
        [([k], f32) for k in even[:-1]] + [([1], bf16)] * (whole > 1) + [([k], f32) for k in even[-1:]],
    ]
    plan = [groups for groups in plan if groups]
    for groups in plan:
        arrays = resident_call(groups, tensor_at, mixed, output_weight, out_width)
        for (g, kind), array in zip(groups, arrays):
            if kind == bf16:
                got = across(array, 1)
                for i, k in enumerate(g):
                    came[k] = got[i * rows : (i + 1) * rows]
            else:
                parts[g[0]] = array
    for k in sorted((k for k in where if k and not k & 1), key=lambda k: (low_bit(k), -k)):
        main = parts[k]
        bit = 1
        while bit < low_bit(k):
            main = main + came[k | bit][:, :out_width].astype(jnp.float32)
            bit *= 2
        if k in chain:
            carried = low2
            for c in chain[: chain.index(k)]:
                carried = carried + came[c][:, out_width:].astype(jnp.float32)
            main = jnp.concatenate([main, carried], axis=1)
        came[k] = across(main.astype(jnp.bfloat16), low_bit(k))
    lows = [came[k] for k in chain[:-1]]
    terms = [parts[0]] + [came[1 << i] for i in range(len(bits) - 1)]
    return pl.pallas_call(
        functools.partial(final_kernel, out_width, (len(lows), len(terms)), replicas),
        in_specs=[VMEM] * (2 + replicas + len(lows) + len(terms)),
        out_specs=VMEM,
        out_shape=jax.ShapeDtypeStruct((rows, out_width), jnp.bfloat16),
        name="final",
        **params((10**8, 10**6)),
    )(picks, low2, *output_up, *lows, *terms)


def solution(mesh):
    sizes = dict(mesh.shape)

    def body(*arrays):
        return per_device(sizes, *arrays)

    return jax.shard_map(
        body,
        mesh=mesh,
        in_specs=(
            P(("groups", "replica"), "tensor"),
            P(None, "tensor"),
            P("tensor", None),
            P(("groups", "replica"), None, None, None),
            P(("groups", "replica"), None, None, None),
            P(("groups", "replica"), None, "tensor"),
            P(("groups", "replica"), None, "tensor"),
            P(("groups", "replica"), None, "tensor"),
            P(("groups", "replica"), None, "tensor"),
            P("groups"),
            P("groups"),
            P(("groups", "replica")),
        ),
        out_specs=P(("groups", "replica"), "tensor"),
        check_vma=False,
    )
```

```python
import functools
import math

import jax
import jax.numpy as jnp
from jax import lax
from jax.experimental import pallas as pl
from jax.experimental.pallas import tpu as pltpu
from jax.sharding import PartitionSpec as P

HEADS = 64
KVS = 8
VMEM = pl.BlockSpec(memory_space=pltpu.VMEM)
SMEM = pl.BlockSpec(memory_space=pltpu.SMEM)
HBM = pl.BlockSpec(memory_space=pltpu.HBM)
LANES = 128
GRANT = 12 << 20
BAND = 32


def dot(a, b):
    return jnp.dot(a, b, preferred_element_type=jnp.float32)


def dot_t(a, b):
    return lax.dot_general(a, b, (((1,), (1,)), ((), ())), preferred_element_type=jnp.float32)


def params(flops_bytes, limit=GRANT):
    return dict(
        compiler_params=pltpu.CompilerParams(vmem_limit_bytes=limit),
        cost_estimate=pl.CostEstimate(
            flops=flops_bytes[0], bytes_accessed=flops_bytes[1], transcendentals=0
        ),
    )


def low_of(x, downs, picks):
    total = 0.0
    at = 0
    for down in downs:
        wide = down.shape[0]
        part = dot_t(x, down[...]) * picks[:, at : at + wide]
        for g in range(0, wide, LANES):
            total = total + part[:, g : g + LANES]
        at += wide
    return total


def lora_of(low, ups, picks):
    total = 0.0
    at = 0
    low = low.astype(jnp.bfloat16).astype(jnp.float32)
    for up in ups:
        wide = up.shape[0]
        spread = jnp.concatenate([low] * (wide // LANES), axis=1) * picks[:, at : at + wide]
        total = total + dot(spread.astype(jnp.bfloat16), up[...])
        at += wide
    return total


def in_hbm(x):
    return pltpu.with_memory_space_constraint(x, pltpu.HBM)


def load_all(pairs, sems):
    copies = [pltpu.make_async_copy(src, dst, sems.at[i]) for i, (src, dst) in enumerate(pairs)]
    for c in copies:
        c.start()
    return copies


def low_kernel(count, hints, x_hbm, picks_ref, *rest):
    rest = rest[hints:]
    downs, (out_ref, x_ref), bufs, sems = rest[:count], rest[count : count + 2], rest[count + 2 : -1], rest[-1]
    for c in load_all([(x_hbm, x_ref)] + list(zip(downs, bufs)), sems):
        c.wait()
    out_ref[...] = low_of(x_ref[...], bufs, picks_ref[...])


def low_call(x, picks, downs, hints):
    return pl.pallas_call(
        functools.partial(low_kernel, len(downs), len(hints)),
        in_specs=[HBM, VMEM] + [HBM] * (len(hints) + len(downs)),
        out_specs=[VMEM] * 2,
        out_shape=[
            jax.ShapeDtypeStruct((x.shape[0], LANES), jnp.float32),
            jax.ShapeDtypeStruct(x.shape, x.dtype),
        ],
        scratch_shapes=[pltpu.VMEM(d.shape, d.dtype) for d in downs]
        + [pltpu.SemaphoreType.DMA((1 + len(downs),))],
        name="low",
        **params((10**8, 10**6)),
    )(in_hbm(x), picks, *[in_hbm(h) for h in hints], in_hbm(downs[0]), *downs[1:])


def begin_kernel(tensor_ref, weight, out_ref):
    out_ref[0] = tensor_ref[0]


def begin_call(tensor_at, weight):
    return pl.pallas_call(
        begin_kernel,
        in_specs=[SMEM, HBM],
        out_specs=SMEM,
        out_shape=jax.ShapeDtypeStruct(tensor_at.shape, tensor_at.dtype),
        name="begin",
        compiler_params=pltpu.CompilerParams(vmem_limit_bytes=4 << 20, has_side_effects=True),
        cost_estimate=pl.CostEstimate(flops=1000, bytes_accessed=1000, transcendentals=0),
    )(tensor_at, in_hbm(weight))


def dense_kernel(shards, ks, spans, given, first, tensor_ref, weight, *rest):
    arrays, rest = rest[:given], rest[given:]
    out_ref = rest[-1]
    rows, width = out_ref.shape[0], weight.shape[0] // shards
    total = 0.0 if first else rest[0][...]
    for k, (i, r) in zip(ks, spans):
        at = pl.multiple_of((tensor_ref[0] ^ k) * width, width)
        total = total + dot(arrays[i][r : r + rows, :width], weight[pl.ds(at, width), :])
    out_ref[...] = total


def dense_call(shards, where, ks, tensor_at, weight, before, rows, hints):
    wide = weight.shape[1]
    arrays, spans = [], []
    for k in ks:
        array, r = where[k]
        if not any(a is array for a in arrays):
            arrays.append(array)
        spans.append(([a is array for a in arrays].index(True), r))
    extra = [] if before is None else [before]
    return pl.pallas_call(
        functools.partial(dense_kernel, shards, ks, spans, len(arrays), before is None),
        in_specs=[SMEM, VMEM] + [VMEM] * (len(arrays) + len(extra)) + [HBM] * len(hints),
        out_specs=VMEM,
        out_shape=jax.ShapeDtypeStruct((rows, wide), jnp.float32),
        **params((2 * len(ks) * rows * weight.size // shards, 10**6), 6 << 20),
    )(tensor_at, weight, *arrays, *extra, *[in_hbm(h) for h in hints])


def mix_kernel(sizes, *refs):
    k_in, k_outs, maps, kv_count, group, head, local_heads, group_all, width = sizes
    refs = list(refs)
    tensor_ref, chunk, w_in, w_out, before, low, picks = [refs.pop(0) for _ in range(7)]
    ups = [refs.pop(0) for _ in range(maps)]
    downs = [refs.pop(0) for _ in range(maps)]
    keys, values, live = [refs.pop(0) for _ in range(3)]
    low_out, mixed_out, block_out = [refs.pop(0) for _ in range(3)]
    more_outs = [refs.pop(0) for _ in k_outs[1:]]
    k_buf, v_buf, up_buf, down_buf, sems = refs

    tensor_at = tensor_ref[0]
    kv = pl.ds(tensor_at * local_heads // group_all, kv_count)
    up_copies = load_all([(u, up_buf.at[i]) for i, u in enumerate(ups)], sems.at[0])
    kv_copies = load_all([(keys.at[:, kv], k_buf), (values.at[:, kv], v_buf)], sems.at[1])
    down_copies = load_all([(d, down_buf.at[i]) for i, d in enumerate(downs)], sems.at[2])

    rows = before.shape[0]
    picked = picks[...]
    for c in up_copies:
        c.wait()
    total = before[...] + 0.5 * lora_of(low[...], [up_buf.at[i] for i in range(maps)], picked)
    at = pl.multiple_of((tensor_at ^ k_in) * width, width)
    total = total + dot(chunk[:, :width], w_in[pl.ds(at, width), :])
    for c in kv_copies:
        c.wait()
    length = k_buf.shape[2]
    bands = []
    for r in range(0, rows, BAND):
        alive = jnp.concatenate([live[r : r + BAND, :]] * group, axis=0) > 0
        heads = []
        for kvh in range(kv_count):
            flat_k = k_buf[r : r + BAND, kvh].reshape(BAND * length, head)
            flat_v = v_buf[r : r + BAND, kvh].reshape(BAND * length, head)
            at = [slice((kvh * group + g) * head, (kvh * group + g + 1) * head) for g in range(group)]
            q = jnp.concatenate([total[r : r + BAND, span] for span in at], axis=0)
            scores = dot_t(q.astype(jnp.bfloat16), flat_k) * (1.0 / math.sqrt(head))
            scores = jnp.where(alive, scores, -1e30)
            top = jnp.max(scores, axis=1, keepdims=True)
            weights = jnp.exp(scores - top)
            probs = weights * (1.0 / jnp.sum(weights, axis=1, keepdims=True))
            got = dot(probs.astype(jnp.bfloat16), flat_v)
            heads += [got[g * BAND : (g + 1) * BAND] for g in range(group)]
        bands.append(jnp.concatenate(heads, axis=1))
    mixed = jnp.concatenate(bands, axis=0).astype(jnp.bfloat16)
    mixed_out[...] = mixed
    for c in down_copies:
        c.wait()
    low_part = low_of(mixed, [down_buf.at[i] for i in range(maps)], picked)
    low_out[...] = low_part
    wide = block_out.shape[1] - LANES
    block_out[:, wide:] = low_part.astype(block_out.dtype)
    for j, k in enumerate(k_outs):
        at = pl.multiple_of((tensor_at ^ k) * wide, LANES)
        block = dot(mixed, w_out[:, pl.ds(at, wide)])
        if j == 0:
            block_out[:, :wide] = block.astype(block_out.dtype)
        else:
            more_outs[j - 1][...] = block


def resident_kernel(ks, spans, tensor_ref, x_ref, weight, *outs):
    rows = x_ref.shape[0]
    wide = outs[0].shape[1]
    for k, (i, r) in zip(ks, spans):
        at = pl.multiple_of((tensor_ref[0] ^ k) * wide, LANES)
        block = dot(x_ref[...], weight[:, pl.ds(at, wide)])
        outs[i][r : r + rows, :] = block.astype(outs[i].dtype)


def resident_call(groups, tensor_at, mixed, weight, out_width):
    rows, _ = mixed.shape
    ks = [k for group, _ in groups for k in group]
    spans = [(i, r * rows) for i, (group, _) in enumerate(groups) for r in range(len(group))]
    return pl.pallas_call(
        functools.partial(resident_kernel, ks, spans),
        in_specs=[SMEM, VMEM, VMEM],
        out_specs=[VMEM] * len(groups),
        out_shape=[
            jax.ShapeDtypeStruct((rows * len(group), out_width), kind) for group, kind in groups
        ],
        compiler_params=pltpu.CompilerParams(vmem_limit_bytes=6 << 20),
    )(tensor_at, mixed, weight)


def final_kernel(wide, count, maps, picks_ref, low_ref, *rest):
    ups, rest = rest[:maps], rest[maps:]
    lows, rest = rest[: count[0]], rest[count[0] :]
    terms, rest = rest[: count[1]], rest[count[1] :]
    (out_ref,) = rest
    low = low_ref[...]
    total = 0.0
    for ref in lows:
        low = low + ref[:, wide:].astype(jnp.float32)
    total = lows[-1][:, :wide].astype(jnp.float32)
    for t in terms:
        total = total + t[:, :wide].astype(jnp.float32)
    total = total + 0.5 * lora_of(low, ups, picks_ref[...])
    out_ref[...] = total.astype(out_ref.dtype)


def low_bit(k):
    return k & -k


def per_device(
    mesh_shape,
    hidden,
    w_query,
    output_weight,
    keys,
    values,
    query_down_maps,
    query_up_maps,
    output_down_maps,
    output_up_maps,
    adapter_ids,
    owner_map,
    kv_lengths,
):
    rows, width = hidden.shape
    head = keys.shape[3]
    length = keys.shape[2]
    shards = mesh_shape["tensor"]
    replicas = mesh_shape["replica"]
    stored, rank = query_down_maps.shape[:2]
    replica_at = lax.axis_index("replica")
    tensor_at = lax.axis_index("tensor").astype(jnp.int32).reshape(1)
    bits = []
    while (1 << len(bits)) < shards:
        bits.append(1 << len(bits))

    def across(x, bit):
        return lax.ppermute(x, "tensor", [(i, i ^ bit) for i in range(shards)])

    def with_swapped(x):
        x = x.reshape(stored * rank, x.shape[2])
        return [x] + [
            lax.ppermute(x, "replica", [(i, (i + k) % replicas) for i in range(replicas)])
            for k in range(1, replicas)
        ]

    id_table = lax.broadcasted_iota(jnp.int32, (1, owner_map.shape[0]), 1)
    slots_all = jnp.sum(jnp.where(adapter_ids[:, None] == id_table, owner_map[None, :], 0), axis=1)
    slots = lax.dynamic_slice_in_dim(slots_all, replica_at * rows, rows)
    lane = lax.broadcasted_iota(jnp.int32, (1, stored * rank), 1) // rank
    picks = jnp.concatenate(
        [
            (slots[:, None] == ((replica_at - k) % replicas) * stored + lane).astype(jnp.float32)
            for k in range(replicas)
        ],
        axis=1,
    )
    column = lax.broadcasted_iota(jnp.int32, (rows, BAND * length), 1)
    row = lax.broadcasted_iota(jnp.int32, (rows, BAND * length), 0)
    live = (column // length == row % BAND) & (column % length < kv_lengths[:, None])
    live = live.astype(jnp.float32)

    query_down = with_swapped(query_down_maps)
    query_up = with_swapped(query_up_maps)
    output_down = with_swapped(output_down_maps)
    output_up = with_swapped(output_up_maps)

    low, near = low_call(hidden, picks, query_down, [])
    where = {0: (near, 0)}
    chain = 0
    for bit in reversed(bits):
        rest = [k for k in where if k not in (0, chain)]
        if bit != 1 or not chain:
            where[bit] = (across(hidden, bit), 0)
        if chain:
            joined = jnp.concatenate([where[chain][0][:, :width], low.astype(jnp.bfloat16)], axis=1)
            got = across(joined, bit)
            where[chain | bit] = (got, 0)
            low = low + got[:, width:].astype(jnp.float32)
        else:
            low = low + across(low, bit)
        if chain and bit == 1:
            for ks in ([0, bits[-1]], rest):
                ks = [k for k in ks if k != chain and k | 1 not in where]
                if ks:
                    got = jnp.concatenate([where[k][0][:, :width] for k in ks], axis=0)
                    got = across(got, 1)
                    for i, k in enumerate(ks):
                        where[k | 1] = (got, i * rows)
        else:
            for k in rest:
                where[k | bit] = (across(where[k][0][:, :width], bit), 0)
        chain |= bit

    last = chain
    first = [k for k in where if not k & 1 and k != last ^ 1]
    second = [last ^ 1] + [k for k in where if k & 1 and k != last]
    begin_call(tensor_at, w_query)
    query = None
    for ks, hints in ((first, [output_weight]), (second, [])):
        query = dense_call(shards, where, ks, tensor_at, w_query, query, rows, hints)

    wide = w_query.shape[1]
    local_heads = wide // head
    group_all = HEADS // KVS
    kv_count = max(1, local_heads // group_all)
    group = local_heads // kv_count
    out_width = output_weight.shape[1] // shards
    depth = output_weight.shape[0]
    whole = shards - 1
    even = [k for k in sorted(where, reverse=True) if not k & 1]
    k_outs = [whole]
    sizes = (last, k_outs, replicas, kv_count, group, head, local_heads, group_all, width)
    map_in, map_out = (stored * rank, wide), (stored * rank, depth)
    low2, mixed, payload, *blocks = pl.pallas_call(
        functools.partial(mix_kernel, sizes),
        in_specs=[SMEM, VMEM, VMEM, VMEM, VMEM, VMEM, VMEM] + [HBM] * (2 * replicas) + [HBM, HBM, VMEM],
        out_specs=[VMEM] * (2 + len(k_outs)),
        out_shape=[
            jax.ShapeDtypeStruct((rows, LANES), jnp.float32),
            jax.ShapeDtypeStruct((rows, wide), jnp.bfloat16),
            jax.ShapeDtypeStruct((rows, out_width + LANES), jnp.bfloat16),
        ]
        + [jax.ShapeDtypeStruct((rows, out_width), jnp.float32)] * (len(k_outs) - 1),
        scratch_shapes=[
            pltpu.VMEM((rows, kv_count, length, head), keys.dtype),
            pltpu.VMEM((rows, kv_count, length, head), values.dtype),
            pltpu.VMEM((replicas,) + map_in, keys.dtype),
            pltpu.VMEM((replicas,) + map_out, keys.dtype),
            pltpu.SemaphoreType.DMA((3, max(2, replicas))),
        ],
        name="mix",
        **params((10**9, 6 << 20)),
    )(
        tensor_at,
        where[last][0],
        w_query,
        output_weight,
        query,
        low,
        picks,
        *query_up,
        *output_down,
        in_hbm(keys),
        in_hbm(values),
        live,
    )

    came = {whole: across(payload, 1)}
    chain = [whole]
    while chain[-1]:
        chain.append(chain[-1] & (chain[-1] - 1))
    odd = [k for k in sorted(where, reverse=True) if k & 1 and k not in (whole, 1)]
    f32, bf16 = jnp.float32, jnp.bfloat16
    parts = dict(zip(k_outs[1:], blocks))
    even = [k for k in even if k not in parts]
    plan = [
        [([k], f32) for k in even[:1]] + [(odd, bf16)] * bool(odd) + [([1], bf16)] * (whole > 1),
        [([k], f32) for k in even[1:]],
    ]
    plan = [groups for groups in plan if groups]
    for groups in plan:
        arrays = resident_call(groups, tensor_at, mixed, output_weight, out_width)
        for (g, kind), array in zip(groups, arrays):
            if kind == bf16:
                got = across(array, 1)
                for i, k in enumerate(g):
                    came[k] = got[i * rows : (i + 1) * rows]
            else:
                parts[g[0]] = array
    for k in sorted((k for k in where if k and not k & 1), key=lambda k: (low_bit(k), -k)):
        main = parts[k]
        bit = 1
        while bit < low_bit(k):
            term = came[k | bit][:, :out_width]
            if k not in chain:
                term = lax.optimization_barrier(term)
            main = main + term.astype(jnp.float32)
            bit *= 2
        if k in chain:
            carried = low2
            for c in chain[: chain.index(k)]:
                carried = carried + came[c][:, out_width:].astype(jnp.float32)
            main = jnp.concatenate([main, carried], axis=1)
        came[k] = across(main.astype(jnp.bfloat16), low_bit(k))
    lows = [came[k] for k in chain[:-1]]
    terms = [parts[0]] + [came[1 << i] for i in range(len(bits) - 1)]
    return pl.pallas_call(
        functools.partial(final_kernel, out_width, (len(lows), len(terms)), replicas),
        in_specs=[VMEM] * (2 + replicas + len(lows) + len(terms)),
        out_specs=VMEM,
        out_shape=jax.ShapeDtypeStruct((rows, out_width), jnp.bfloat16),
        name="final",
        **params((10**8, 10**6)),
    )(picks, low2, *output_up, *lows, *terms)


def solution(mesh):
    sizes = dict(mesh.shape)

    def body(*arrays):
        return per_device(sizes, *arrays)

    return jax.shard_map(
        body,
        mesh=mesh,
        in_specs=(
            P(("groups", "replica"), "tensor"),
            P(None, "tensor"),
            P("tensor", None),
            P(("groups", "replica"), None, None, None),
            P(("groups", "replica"), None, None, None),
            P(("groups", "replica"), None, "tensor"),
            P(("groups", "replica"), None, "tensor"),
            P(("groups", "replica"), None, "tensor"),
            P(("groups", "replica"), None, "tensor"),
            P("groups"),
            P("groups"),
            P(("groups", "replica")),
        ),
        out_specs=P(("groups", "replica"), "tensor"),
        check_vma=False,
    )
```

```python
import functools
import math

import jax
import jax.numpy as jnp
from jax import lax
from jax.experimental import pallas as pl
from jax.experimental.pallas import tpu as pltpu
from jax.sharding import PartitionSpec as P

HEADS = 64
KVS = 8
VMEM = pl.BlockSpec(memory_space=pltpu.VMEM)
SMEM = pl.BlockSpec(memory_space=pltpu.SMEM)
HBM = pl.BlockSpec(memory_space=pltpu.HBM)
LANES = 128
GRANT = 12 << 20
BAND = 32


def dot(a, b):
    return jnp.dot(a, b, preferred_element_type=jnp.float32)


def dot_t(a, b):
    return lax.dot_general(a, b, (((1,), (1,)), ((), ())), preferred_element_type=jnp.float32)


def params(flops_bytes, limit=GRANT):
    return dict(
        compiler_params=pltpu.CompilerParams(vmem_limit_bytes=limit),
        cost_estimate=pl.CostEstimate(
            flops=flops_bytes[0], bytes_accessed=flops_bytes[1], transcendentals=0
        ),
    )


def low_of(x, downs, picks):
    total = 0.0
    at = 0
    for down in downs:
        wide = down.shape[0]
        part = dot_t(x, down[...]) * picks[:, at : at + wide]
        for g in range(0, wide, LANES):
            total = total + part[:, g : g + LANES]
        at += wide
    return total


def lora_of(low, ups, picks):
    total = 0.0
    at = 0
    low = low.astype(jnp.bfloat16).astype(jnp.float32)
    for up in ups:
        wide = up.shape[0]
        spread = jnp.concatenate([low] * (wide // LANES), axis=1) * picks[:, at : at + wide]
        total = total + dot(spread.astype(jnp.bfloat16), up[...])
        at += wide
    return total


def in_hbm(x):
    return pltpu.with_memory_space_constraint(x, pltpu.HBM)


def load_all(pairs, sems):
    copies = [pltpu.make_async_copy(src, dst, sems.at[i]) for i, (src, dst) in enumerate(pairs)]
    for c in copies:
        c.start()
    return copies


def low_kernel(count, hints, x_hbm, picks_ref, *rest):
    rest = rest[hints:]
    downs, (out_ref, x_ref), bufs, sems = rest[:count], rest[count : count + 2], rest[count + 2 : -1], rest[-1]
    for c in load_all([(x_hbm, x_ref)] + list(zip(downs, bufs)), sems):
        c.wait()
    out_ref[...] = low_of(x_ref[...], bufs, picks_ref[...])


def low_call(x, picks, downs, hints):
    return pl.pallas_call(
        functools.partial(low_kernel, len(downs), len(hints)),
        in_specs=[HBM, VMEM] + [HBM] * (len(hints) + len(downs)),
        out_specs=[VMEM] * 2,
        out_shape=[
            jax.ShapeDtypeStruct((x.shape[0], LANES), jnp.float32),
            jax.ShapeDtypeStruct(x.shape, x.dtype),
        ],
        scratch_shapes=[pltpu.VMEM(d.shape, d.dtype) for d in downs]
        + [pltpu.SemaphoreType.DMA((1 + len(downs),))],
        name="low",
        **params((10**8, 10**6)),
    )(in_hbm(x), picks, *[in_hbm(h) for h in hints], in_hbm(downs[0]), *downs[1:])


def begin_kernel(tensor_ref, weight, out_ref):
    out_ref[0] = tensor_ref[0]


def begin_call(tensor_at, weight):
    return pl.pallas_call(
        begin_kernel,
        in_specs=[SMEM, HBM],
        out_specs=SMEM,
        out_shape=jax.ShapeDtypeStruct(tensor_at.shape, tensor_at.dtype),
        name="begin",
        compiler_params=pltpu.CompilerParams(vmem_limit_bytes=4 << 20, has_side_effects=True),
        cost_estimate=pl.CostEstimate(flops=1000, bytes_accessed=1000, transcendentals=0),
    )(tensor_at, in_hbm(weight))


def dense_kernel(shards, ks, spans, given, first, kv, tensor_ref, weight, *rest):
    arrays, rest = rest[:given], rest[given:]
    copies = []
    if kv:
        keys, values, out_ref, k_out, v_out, sems = rest[-6:]
        at = pl.ds(tensor_ref[0] * kv[0] // kv[1], kv[2])
        copies = load_all([(keys.at[:, at], k_out), (values.at[:, at], v_out)], sems)
    else:
        out_ref = rest[-1]
    rows, width = out_ref.shape[0], weight.shape[0] // shards
    total = 0.0 if first else rest[0][...]
    for k, (i, r) in zip(ks, spans):
        at = pl.multiple_of((tensor_ref[0] ^ k) * width, width)
        total = total + dot(arrays[i][r : r + rows, :width], weight[pl.ds(at, width), :])
    out_ref[...] = total
    for c in copies:
        c.wait()


def dense_call(shards, where, ks, tensor_at, weight, before, rows, hints, kv, caches):
    wide = weight.shape[1]
    arrays, spans = [], []
    for k in ks:
        array, r = where[k]
        if not any(a is array for a in arrays):
            arrays.append(array)
        spans.append(([a is array for a in arrays].index(True), r))
    extra = [] if before is None else [before]
    return pl.pallas_call(
        functools.partial(dense_kernel, shards, ks, spans, len(arrays), before is None, kv),
        in_specs=[SMEM, VMEM] + [VMEM] * (len(arrays) + len(extra)) + [HBM] * (len(hints) + len(caches)),
        out_specs=[VMEM] * (1 + len(caches)),
        out_shape=[jax.ShapeDtypeStruct((rows, wide), jnp.float32)]
        + [jax.ShapeDtypeStruct((c.shape[0], kv[2]) + c.shape[2:], c.dtype) for c in caches],
        scratch_shapes=[pltpu.SemaphoreType.DMA((len(caches),))] * bool(caches),
        **params((2 * len(ks) * rows * weight.size // shards, 10**6), 6 << 20),
    )(tensor_at, weight, *arrays, *extra, *[in_hbm(h) for h in hints], *[in_hbm(c) for c in caches])


def mix_kernel(sizes, *refs):
    k_in, k_outs, maps, kv_count, group, head, _, _, width = sizes
    refs = list(refs)
    tensor_ref, chunk, w_in, w_out, before, low, picks = [refs.pop(0) for _ in range(7)]
    ups = [refs.pop(0) for _ in range(maps)]
    downs = [refs.pop(0) for _ in range(maps)]
    k_buf, v_buf, live = [refs.pop(0) for _ in range(3)]
    low_out, mixed_out, block_out = [refs.pop(0) for _ in range(3)]
    more_outs = [refs.pop(0) for _ in k_outs[1:]]

    tensor_at = tensor_ref[0]

    rows = before.shape[0]
    picked = picks[...]
    total = before[...] + 0.5 * lora_of(low[...], ups, picked)
    at = pl.multiple_of((tensor_at ^ k_in) * width, width)
    total = total + dot(chunk[:, :width], w_in[pl.ds(at, width), :])
    length = k_buf.shape[2]
    bands = []
    for r in range(0, rows, BAND):
        alive = jnp.concatenate([live[r : r + BAND, :]] * group, axis=0) > 0
        heads = []
        for kvh in range(kv_count):
            flat_k = k_buf[r : r + BAND, kvh].reshape(BAND * length, head)
            flat_v = v_buf[r : r + BAND, kvh].reshape(BAND * length, head)
            at = [slice((kvh * group + g) * head, (kvh * group + g + 1) * head) for g in range(group)]
            q = jnp.concatenate([total[r : r + BAND, span] for span in at], axis=0)
            scores = dot_t(q.astype(jnp.bfloat16), flat_k) * (1.0 / math.sqrt(head))
            scores = jnp.where(alive, scores, -1e30)
            top = jnp.max(scores, axis=1, keepdims=True)
            weights = jnp.exp(scores - top)
            probs = weights * (1.0 / jnp.sum(weights, axis=1, keepdims=True))
            got = dot(probs.astype(jnp.bfloat16), flat_v)
            heads += [got[g * BAND : (g + 1) * BAND] for g in range(group)]
        bands.append(jnp.concatenate(heads, axis=1))
    mixed = jnp.concatenate(bands, axis=0).astype(jnp.bfloat16)
    mixed_out[...] = mixed
    low_part = low_of(mixed, downs, picked)
    low_out[...] = low_part
    wide = block_out.shape[1] - LANES
    block_out[:, wide:] = low_part.astype(block_out.dtype)
    for j, k in enumerate(k_outs):
        at = pl.multiple_of((tensor_at ^ k) * wide, LANES)
        block = dot(mixed, w_out[:, pl.ds(at, wide)])
        if j == 0:
            block_out[:, :wide] = block.astype(block_out.dtype)
        else:
            more_outs[j - 1][...] = block


def resident_kernel(ks, spans, tensor_ref, x_ref, weight, *outs):
    rows = x_ref.shape[0]
    wide = outs[0].shape[1]
    for k, (i, r) in zip(ks, spans):
        at = pl.multiple_of((tensor_ref[0] ^ k) * wide, LANES)
        block = dot(x_ref[...], weight[:, pl.ds(at, wide)])
        outs[i][r : r + rows, :] = block.astype(outs[i].dtype)


def resident_call(groups, tensor_at, mixed, weight, out_width):
    rows, _ = mixed.shape
    ks = [k for group, _ in groups for k in group]
    spans = [(i, r * rows) for i, (group, _) in enumerate(groups) for r in range(len(group))]
    return pl.pallas_call(
        functools.partial(resident_kernel, ks, spans),
        in_specs=[SMEM, VMEM, VMEM],
        out_specs=[VMEM] * len(groups),
        out_shape=[
            jax.ShapeDtypeStruct((rows * len(group), out_width), kind) for group, kind in groups
        ],
        compiler_params=pltpu.CompilerParams(vmem_limit_bytes=6 << 20),
    )(tensor_at, mixed, weight)


def final_kernel(wide, count, maps, picks_ref, low_ref, *rest):
    ups, rest = rest[:maps], rest[maps:]
    lows, rest = rest[: count[0]], rest[count[0] :]
    terms, rest = rest[: count[1]], rest[count[1] :]
    (out_ref,) = rest
    low = low_ref[...]
    total = 0.0
    for ref in lows:
        low = low + ref[:, wide:].astype(jnp.float32)
    total = lows[-1][:, :wide].astype(jnp.float32)
    for t in terms:
        total = total + t[:, :wide].astype(jnp.float32)
    total = total + 0.5 * lora_of(low, ups, picks_ref[...])
    out_ref[...] = total.astype(out_ref.dtype)


def low_bit(k):
    return k & -k


def per_device(
    mesh_shape,
    hidden,
    w_query,
    output_weight,
    keys,
    values,
    query_down_maps,
    query_up_maps,
    output_down_maps,
    output_up_maps,
    adapter_ids,
    owner_map,
    kv_lengths,
):
    rows, width = hidden.shape
    head = keys.shape[3]
    length = keys.shape[2]
    shards = mesh_shape["tensor"]
    replicas = mesh_shape["replica"]
    stored, rank = query_down_maps.shape[:2]
    replica_at = lax.axis_index("replica")
    tensor_at = lax.axis_index("tensor").astype(jnp.int32).reshape(1)
    bits = []
    while (1 << len(bits)) < shards:
        bits.append(1 << len(bits))

    def across(x, bit):
        return lax.ppermute(x, "tensor", [(i, i ^ bit) for i in range(shards)])

    def with_swapped(x):
        x = x.reshape(stored * rank, x.shape[2])
        return [x] + [
            lax.ppermute(x, "replica", [(i, (i + k) % replicas) for i in range(replicas)])
            for k in range(1, replicas)
        ]

    id_table = lax.broadcasted_iota(jnp.int32, (1, owner_map.shape[0]), 1)
    slots_all = jnp.sum(jnp.where(adapter_ids[:, None] == id_table, owner_map[None, :], 0), axis=1)
    slots = lax.dynamic_slice_in_dim(slots_all, replica_at * rows, rows)
    lane = lax.broadcasted_iota(jnp.int32, (1, stored * rank), 1) // rank
    picks = jnp.concatenate(
        [
            (slots[:, None] == ((replica_at - k) % replicas) * stored + lane).astype(jnp.float32)
            for k in range(replicas)
        ],
        axis=1,
    )
    column = lax.broadcasted_iota(jnp.int32, (rows, BAND * length), 1)
    row = lax.broadcasted_iota(jnp.int32, (rows, BAND * length), 0)
    live = (column // length == row % BAND) & (column % length < kv_lengths[:, None])
    live = live.astype(jnp.float32)

    query_down = with_swapped(query_down_maps)
    query_up = with_swapped(query_up_maps)
    output_down = with_swapped(output_down_maps)
    output_up = with_swapped(output_up_maps)

    low, near = low_call(hidden, picks, query_down, [])
    where = {0: (near, 0)}
    chain = 0
    for bit in reversed(bits):
        rest = [k for k in where if k not in (0, chain)]
        if bit != 1 or not chain:
            where[bit] = (across(hidden, bit), 0)
        if chain:
            joined = jnp.concatenate([where[chain][0][:, :width], low.astype(jnp.bfloat16)], axis=1)
            got = across(joined, bit)
            where[chain | bit] = (got, 0)
            low = low + got[:, width:].astype(jnp.float32)
        else:
            low = low + across(low, bit)
        if chain and bit == 1:
            for ks in ([0, bits[-1]], rest):
                ks = [k for k in ks if k != chain and k | 1 not in where]
                if ks:
                    got = jnp.concatenate([where[k][0][:, :width] for k in ks], axis=0)
                    got = across(got, 1)
                    for i, k in enumerate(ks):
                        where[k | 1] = (got, i * rows)
        else:
            for k in rest:
                where[k | bit] = (across(where[k][0][:, :width], bit), 0)
        chain |= bit

    last = chain
    first = [k for k in where if not k & 1 and k != last ^ 1]
    second = [last ^ 1] + [k for k in where if k & 1 and k != last]
    begin_call(tensor_at, w_query)
    wide = w_query.shape[1]
    local_heads = wide // head
    group_all = HEADS // KVS
    kv_count = max(1, local_heads // group_all)
    group = local_heads // kv_count
    kv = (local_heads, group_all, kv_count)
    (query,) = dense_call(
        shards, where, first, tensor_at, w_query, None, rows, [output_weight], None, []
    )
    query, near_keys, near_values = dense_call(
        shards, where, second, tensor_at, w_query, query, rows, [], kv, [keys, values]
    )

    out_width = output_weight.shape[1] // shards
    depth = output_weight.shape[0]
    whole = shards - 1
    even = [k for k in sorted(where, reverse=True) if not k & 1]
    k_outs = [whole]
    sizes = (last, k_outs, replicas, kv_count, group, head, local_heads, group_all, width)
    map_in, map_out = (stored * rank, wide), (stored * rank, depth)
    low2, mixed, payload, *blocks = pl.pallas_call(
        functools.partial(mix_kernel, sizes),
        in_specs=[SMEM, VMEM, VMEM, VMEM, VMEM, VMEM, VMEM] + [VMEM] * (2 * replicas) + [VMEM, VMEM, VMEM],
        out_specs=[VMEM] * (2 + len(k_outs)),
        out_shape=[
            jax.ShapeDtypeStruct((rows, LANES), jnp.float32),
            jax.ShapeDtypeStruct((rows, wide), jnp.bfloat16),
            jax.ShapeDtypeStruct((rows, out_width + LANES), jnp.bfloat16),
        ]
        + [jax.ShapeDtypeStruct((rows, out_width), jnp.float32)] * (len(k_outs) - 1),
        scratch_shapes=[
            pltpu.VMEM((replicas,) + map_in, keys.dtype),
            pltpu.VMEM((replicas,) + map_out, keys.dtype),
            pltpu.SemaphoreType.DMA((3, max(2, replicas))),
        ],
        name="mix",
        **params((10**9, 6 << 20)),
    )(
        tensor_at,
        where[last][0],
        w_query,
        output_weight,
        query,
        low,
        picks,
        *query_up,
        *output_down,
        near_keys,
        near_values,
        live,
    )

    came = {whole: across(payload, 1)}
    chain = [whole]
    while chain[-1]:
        chain.append(chain[-1] & (chain[-1] - 1))
    odd = [k for k in sorted(where, reverse=True) if k & 1 and k not in (whole, 1)]
    f32, bf16 = jnp.float32, jnp.bfloat16
    parts = dict(zip(k_outs[1:], blocks))
    even = [k for k in even if k not in parts]
    plan = [
        [([k], f32) for k in even[:1]] + [(odd, bf16)] * bool(odd) + [([1], bf16)] * (whole > 1),
        [([k], f32) for k in even[1:]],
    ]
    plan = [groups for groups in plan if groups]
    for groups in plan:
        arrays = resident_call(groups, tensor_at, mixed, output_weight, out_width)
        for (g, kind), array in zip(groups, arrays):
            if kind == bf16:
                got = across(array, 1)
                for i, k in enumerate(g):
                    came[k] = got[i * rows : (i + 1) * rows]
            else:
                parts[g[0]] = array
    for k in sorted((k for k in where if k and not k & 1), key=lambda k: (low_bit(k), -k)):
        main = parts[k]
        bit = 1
        while bit < low_bit(k):
            term = came[k | bit][:, :out_width]
            if k not in chain:
                term = lax.optimization_barrier(term)
            main = main + term.astype(jnp.float32)
            bit *= 2
        if k in chain:
            carried = low2
            for c in chain[: chain.index(k)]:
                carried = carried + came[c][:, out_width:].astype(jnp.float32)
            main = jnp.concatenate([main, carried], axis=1)
        came[k] = across(main.astype(jnp.bfloat16), low_bit(k))
    lows = [came[k] for k in chain[:-1]]
    terms = [parts[0]] + [came[1 << i] for i in range(len(bits) - 1)]
    return pl.pallas_call(
        functools.partial(final_kernel, out_width, (len(lows), len(terms)), replicas),
        in_specs=[VMEM] * (2 + replicas + len(lows) + len(terms)),
        out_specs=VMEM,
        out_shape=jax.ShapeDtypeStruct((rows, out_width), jnp.bfloat16),
        name="final",
        **params((10**8, 10**6)),
    )(picks, low2, *output_up, *lows, *terms)


def solution(mesh):
    sizes = dict(mesh.shape)

    def body(*arrays):
        return per_device(sizes, *arrays)

    return jax.shard_map(
        body,
        mesh=mesh,
        in_specs=(
            P(("groups", "replica"), "tensor"),
            P(None, "tensor"),
            P("tensor", None),
            P(("groups", "replica"), None, None, None),
            P(("groups", "replica"), None, None, None),
            P(("groups", "replica"), None, "tensor"),
            P(("groups", "replica"), None, "tensor"),
            P(("groups", "replica"), None, "tensor"),
            P(("groups", "replica"), None, "tensor"),
            P("groups"),
            P("groups"),
            P(("groups", "replica")),
        ),
        out_specs=P(("groups", "replica"), "tensor"),
        check_vma=False,
    )
```

```python
import functools
import math

import jax
import jax.numpy as jnp
from jax import lax
from jax.experimental import pallas as pl
from jax.experimental.pallas import tpu as pltpu
from jax.sharding import PartitionSpec as P

HEADS = 64
KVS = 8
VMEM = pl.BlockSpec(memory_space=pltpu.VMEM)
SMEM = pl.BlockSpec(memory_space=pltpu.SMEM)
HBM = pl.BlockSpec(memory_space=pltpu.HBM)
LANES = 128
GRANT = 12 << 20
BAND = 32


def dot(a, b):
    return jnp.dot(a, b, preferred_element_type=jnp.float32)


def dot_t(a, b):
    return lax.dot_general(a, b, (((1,), (1,)), ((), ())), preferred_element_type=jnp.float32)


def params(flops_bytes, limit=GRANT):
    return dict(
        compiler_params=pltpu.CompilerParams(vmem_limit_bytes=limit),
        cost_estimate=pl.CostEstimate(
            flops=flops_bytes[0], bytes_accessed=flops_bytes[1], transcendentals=0
        ),
    )


def low_of(x, downs, picks):
    total = 0.0
    at = 0
    for down in downs:
        wide = down.shape[0]
        part = dot_t(x, down[...]) * picks[:, at : at + wide]
        for g in range(0, wide, LANES):
            total = total + part[:, g : g + LANES]
        at += wide
    return total


def lora_of(low, ups, picks):
    total = 0.0
    at = 0
    low = low.astype(jnp.bfloat16).astype(jnp.float32)
    for up in ups:
        wide = up.shape[0]
        spread = jnp.concatenate([low] * (wide // LANES), axis=1) * picks[:, at : at + wide]
        total = total + dot(spread.astype(jnp.bfloat16), up[...])
        at += wide
    return total


def in_hbm(x):
    return pltpu.with_memory_space_constraint(x, pltpu.HBM)


def load_all(pairs, sems):
    copies = [pltpu.make_async_copy(src, dst, sems.at[i]) for i, (src, dst) in enumerate(pairs)]
    for c in copies:
        c.start()
    return copies


def low_kernel(count, hints, x_hbm, picks_ref, *rest):
    rest = rest[hints:]
    downs, (out_ref, x_ref), bufs, sems = rest[:count], rest[count : count + 2], rest[count + 2 : -1], rest[-1]
    for c in load_all([(x_hbm, x_ref)] + list(zip(downs, bufs)), sems):
        c.wait()
    out_ref[...] = low_of(x_ref[...], bufs, picks_ref[...])


def low_call(x, picks, downs, hints):
    return pl.pallas_call(
        functools.partial(low_kernel, len(downs), len(hints)),
        in_specs=[HBM, VMEM] + [HBM] * (len(hints) + len(downs)),
        out_specs=[VMEM] * 2,
        out_shape=[
            jax.ShapeDtypeStruct((x.shape[0], LANES), jnp.float32),
            jax.ShapeDtypeStruct(x.shape, x.dtype),
        ],
        scratch_shapes=[pltpu.VMEM(d.shape, d.dtype) for d in downs]
        + [pltpu.SemaphoreType.DMA((1 + len(downs),))],
        name="low",
        **params((10**8, 10**6)),
    )(in_hbm(x), picks, *[in_hbm(h) for h in hints], in_hbm(downs[0]), *downs[1:])


def begin_kernel(tensor_ref, *rest):
    rest[-1][0] = tensor_ref[0]


def begin_call(tensor_at, weights):
    return pl.pallas_call(
        begin_kernel,
        in_specs=[SMEM] + [HBM] * len(weights),
        out_specs=SMEM,
        out_shape=jax.ShapeDtypeStruct(tensor_at.shape, tensor_at.dtype),
        name="begin",
        compiler_params=pltpu.CompilerParams(vmem_limit_bytes=4 << 20, has_side_effects=True),
        cost_estimate=pl.CostEstimate(flops=1000, bytes_accessed=1000, transcendentals=0),
    )(tensor_at, *[in_hbm(w) for w in weights])


def dense_kernel(shards, ks, spans, given, first, kv, tensor_ref, weight, *rest):
    arrays, rest = rest[:given], rest[given:]
    copies = []
    if kv:
        keys, values, out_ref, k_out, v_out, sems = rest[-6:]
        at = pl.ds(tensor_ref[0] * kv[0] // kv[1], kv[2])
        copies = load_all([(keys.at[:, at], k_out), (values.at[:, at], v_out)], sems)
    else:
        out_ref = rest[-1]
    rows, width = out_ref.shape[0], weight.shape[0] // shards
    total = 0.0 if first else rest[0][...]
    for k, (i, r) in zip(ks, spans):
        at = pl.multiple_of((tensor_ref[0] ^ k) * width, width)
        total = total + dot(arrays[i][r : r + rows, :width], weight[pl.ds(at, width), :])
    out_ref[...] = total
    for c in copies:
        c.wait()


def dense_call(shards, where, ks, tensor_at, weight, before, rows, hints, kv, caches):
    wide = weight.shape[1]
    arrays, spans = [], []
    for k in ks:
        array, r = where[k]
        if not any(a is array for a in arrays):
            arrays.append(array)
        spans.append(([a is array for a in arrays].index(True), r))
    extra = [] if before is None else [before]
    return pl.pallas_call(
        functools.partial(dense_kernel, shards, ks, spans, len(arrays), before is None, kv),
        in_specs=[SMEM, VMEM] + [VMEM] * (len(arrays) + len(extra)) + [HBM] * (len(hints) + len(caches)),
        out_specs=[VMEM] * (1 + len(caches)),
        out_shape=[jax.ShapeDtypeStruct((rows, wide), jnp.float32)]
        + [jax.ShapeDtypeStruct((c.shape[0], kv[2]) + c.shape[2:], c.dtype) for c in caches],
        scratch_shapes=[pltpu.SemaphoreType.DMA((len(caches),))] * bool(caches),
        **params((2 * len(ks) * rows * weight.size // shards, 10**6), 6 << 20),
    )(tensor_at, weight, *arrays, *extra, *[in_hbm(h) for h in hints], *[in_hbm(c) for c in caches])


def mix_kernel(sizes, *refs):
    k_in, k_outs, maps, kv_count, group, head, _, _, width = sizes
    refs = list(refs)
    tensor_ref, chunk, w_in, w_out, before, low, picks = [refs.pop(0) for _ in range(7)]
    ups = [refs.pop(0) for _ in range(maps)]
    downs = [refs.pop(0) for _ in range(maps)]
    k_buf, v_buf, live = [refs.pop(0) for _ in range(3)]
    low_out, mixed_out, block_out = [refs.pop(0) for _ in range(3)]
    more_outs = [refs.pop(0) for _ in k_outs[1:]]

    tensor_at = tensor_ref[0]

    rows = before.shape[0]
    picked = picks[...]
    total = before[...] + 0.5 * lora_of(low[...], ups, picked)
    at = pl.multiple_of((tensor_at ^ k_in) * width, width)
    total = total + dot(chunk[:, :width], w_in[pl.ds(at, width), :])
    length = k_buf.shape[2]
    bands = []
    for r in range(0, rows, BAND):
        alive = jnp.concatenate([live[r : r + BAND, :]] * group, axis=0) > 0
        heads = []
        for kvh in range(kv_count):
            flat_k = k_buf[r : r + BAND, kvh].reshape(BAND * length, head)
            flat_v = v_buf[r : r + BAND, kvh].reshape(BAND * length, head)
            at = [slice((kvh * group + g) * head, (kvh * group + g + 1) * head) for g in range(group)]
            q = jnp.concatenate([total[r : r + BAND, span] for span in at], axis=0)
            scores = dot_t(q.astype(jnp.bfloat16), flat_k) * (1.0 / math.sqrt(head))
            scores = jnp.where(alive, scores, -1e30)
            top = jnp.max(scores, axis=1, keepdims=True)
            weights = jnp.exp(scores - top)
            probs = weights * (1.0 / jnp.sum(weights, axis=1, keepdims=True))
            got = dot(probs.astype(jnp.bfloat16), flat_v)
            heads += [got[g * BAND : (g + 1) * BAND] for g in range(group)]
        bands.append(jnp.concatenate(heads, axis=1))
    mixed = jnp.concatenate(bands, axis=0).astype(jnp.bfloat16)
    mixed_out[...] = mixed
    low_part = low_of(mixed, downs, picked)
    low_out[...] = low_part
    wide = block_out.shape[1] - LANES
    block_out[:, wide:] = low_part.astype(block_out.dtype)
    for j, k in enumerate(k_outs):
        at = pl.multiple_of((tensor_at ^ k) * wide, LANES)
        block = dot(mixed, w_out[:, pl.ds(at, wide)])
        if j == 0:
            block_out[:, :wide] = block.astype(block_out.dtype)
        else:
            more_outs[j - 1][...] = block


def resident_kernel(ks, spans, tensor_ref, x_ref, weight, *outs):
    rows = x_ref.shape[0]
    wide = outs[0].shape[1]
    for k, (i, r) in zip(ks, spans):
        at = pl.multiple_of((tensor_ref[0] ^ k) * wide, LANES)
        block = dot(x_ref[...], weight[:, pl.ds(at, wide)])
        outs[i][r : r + rows, :] = block.astype(outs[i].dtype)


def resident_call(groups, tensor_at, mixed, weight, out_width):
    rows, _ = mixed.shape
    ks = [k for group, _ in groups for k in group]
    spans = [(i, r * rows) for i, (group, _) in enumerate(groups) for r in range(len(group))]
    return pl.pallas_call(
        functools.partial(resident_kernel, ks, spans),
        in_specs=[SMEM, VMEM, VMEM],
        out_specs=[VMEM] * len(groups),
        out_shape=[
            jax.ShapeDtypeStruct((rows * len(group), out_width), kind) for group, kind in groups
        ],
        compiler_params=pltpu.CompilerParams(vmem_limit_bytes=6 << 20),
    )(tensor_at, mixed, weight)


def final_kernel(wide, count, maps, picks_ref, low_ref, *rest):
    ups, rest = rest[:maps], rest[maps:]
    lows, rest = rest[: count[0]], rest[count[0] :]
    terms, rest = rest[: count[1]], rest[count[1] :]
    (out_ref,) = rest
    low = low_ref[...]
    total = 0.0
    for ref in lows:
        low = low + ref[:, wide:].astype(jnp.float32)
    total = lows[-1][:, :wide].astype(jnp.float32)
    for t in terms:
        total = total + t[:, :wide].astype(jnp.float32)
    total = total + 0.5 * lora_of(low, ups, picks_ref[...])
    out_ref[...] = total.astype(out_ref.dtype)


def low_bit(k):
    return k & -k


def per_device(
    mesh_shape,
    hidden,
    w_query,
    output_weight,
    keys,
    values,
    query_down_maps,
    query_up_maps,
    output_down_maps,
    output_up_maps,
    adapter_ids,
    owner_map,
    kv_lengths,
):
    rows, width = hidden.shape
    head = keys.shape[3]
    length = keys.shape[2]
    shards = mesh_shape["tensor"]
    replicas = mesh_shape["replica"]
    stored, rank = query_down_maps.shape[:2]
    replica_at = lax.axis_index("replica")
    tensor_at = lax.axis_index("tensor").astype(jnp.int32).reshape(1)
    bits = []
    while (1 << len(bits)) < shards:
        bits.append(1 << len(bits))

    def across(x, bit):
        return lax.ppermute(x, "tensor", [(i, i ^ bit) for i in range(shards)])

    def with_swapped(x):
        x = x.reshape(stored * rank, x.shape[2])
        return [x] + [
            lax.ppermute(x, "replica", [(i, (i + k) % replicas) for i in range(replicas)])
            for k in range(1, replicas)
        ]

    id_table = lax.broadcasted_iota(jnp.int32, (1, owner_map.shape[0]), 1)
    slots_all = jnp.sum(jnp.where(adapter_ids[:, None] == id_table, owner_map[None, :], 0), axis=1)
    slots = lax.dynamic_slice_in_dim(slots_all, replica_at * rows, rows)
    lane = lax.broadcasted_iota(jnp.int32, (1, stored * rank), 1) // rank
    picks = jnp.concatenate(
        [
            (slots[:, None] == ((replica_at - k) % replicas) * stored + lane).astype(jnp.float32)
            for k in range(replicas)
        ],
        axis=1,
    )
    column = lax.broadcasted_iota(jnp.int32, (rows, BAND * length), 1)
    row = lax.broadcasted_iota(jnp.int32, (rows, BAND * length), 0)
    live = (column // length == row % BAND) & (column % length < kv_lengths[:, None])
    live = live.astype(jnp.float32)

    query_down = with_swapped(query_down_maps)
    query_up = with_swapped(query_up_maps)
    output_down = with_swapped(output_down_maps)
    output_up = with_swapped(output_up_maps)

    low, near = low_call(hidden, picks, query_down, [])
    where = {0: (near, 0)}
    chain = 0
    for bit in reversed(bits):
        rest = [k for k in where if k not in (0, chain)]
        if bit != 1 or not chain:
            where[bit] = (across(hidden, bit), 0)
        if chain:
            joined = jnp.concatenate([where[chain][0][:, :width], low.astype(jnp.bfloat16)], axis=1)
            got = across(joined, bit)
            where[chain | bit] = (got, 0)
            low = low + got[:, width:].astype(jnp.float32)
        else:
            low = low + across(low, bit)
        if chain and bit == 1:
            for ks in ([0, bits[-1]], rest):
                ks = [k for k in ks if k != chain and k | 1 not in where]
                if ks:
                    got = jnp.concatenate([where[k][0][:, :width] for k in ks], axis=0)
                    got = across(got, 1)
                    for i, k in enumerate(ks):
                        where[k | 1] = (got, i * rows)
        else:
            for k in rest:
                where[k | bit] = (across(where[k][0][:, :width], bit), 0)
        chain |= bit

    last = chain
    first = [k for k in where if not k & 1 and k != last ^ 1]
    second = [last ^ 1] + [k for k in where if k & 1 and k != last]
    begin_call(tensor_at, [w_query, output_weight])
    wide = w_query.shape[1]
    local_heads = wide // head
    group_all = HEADS // KVS
    kv_count = max(1, local_heads // group_all)
    group = local_heads // kv_count
    kv = (local_heads, group_all, kv_count)
    (query,) = dense_call(
        shards, where, first, tensor_at, w_query, None, rows, [output_weight], None, []
    )
    query, near_keys, near_values = dense_call(
        shards, where, second, tensor_at, w_query, query, rows, [], kv, [keys, values]
    )

    out_width = output_weight.shape[1] // shards
    depth = output_weight.shape[0]
    whole = shards - 1
    even = [k for k in sorted(where, reverse=True) if not k & 1]
    k_outs = [whole]
    sizes = (last, k_outs, replicas, kv_count, group, head, local_heads, group_all, width)
    map_in, map_out = (stored * rank, wide), (stored * rank, depth)
    low2, mixed, payload, *blocks = pl.pallas_call(
        functools.partial(mix_kernel, sizes),
        in_specs=[SMEM, VMEM, VMEM, VMEM, VMEM, VMEM, VMEM] + [VMEM] * (2 * replicas) + [VMEM, VMEM, VMEM],
        out_specs=[VMEM] * (2 + len(k_outs)),
        out_shape=[
            jax.ShapeDtypeStruct((rows, LANES), jnp.float32),
            jax.ShapeDtypeStruct((rows, wide), jnp.bfloat16),
            jax.ShapeDtypeStruct((rows, out_width + LANES), jnp.bfloat16),
        ]
        + [jax.ShapeDtypeStruct((rows, out_width), jnp.float32)] * (len(k_outs) - 1),
        scratch_shapes=[
            pltpu.VMEM((replicas,) + map_in, keys.dtype),
            pltpu.VMEM((replicas,) + map_out, keys.dtype),
            pltpu.SemaphoreType.DMA((3, max(2, replicas))),
        ],
        name="mix",
        **params((10**9, 6 << 20)),
    )(
        tensor_at,
        where[last][0],
        w_query,
        output_weight,
        query,
        low,
        picks,
        *query_up,
        *output_down,
        near_keys,
        near_values,
        live,
    )

    came = {whole: across(payload, 1)}
    chain = [whole]
    while chain[-1]:
        chain.append(chain[-1] & (chain[-1] - 1))
    odd = [k for k in sorted(where, reverse=True) if k & 1 and k not in (whole, 1)]
    f32, bf16 = jnp.float32, jnp.bfloat16
    parts = dict(zip(k_outs[1:], blocks))
    even = [k for k in even if k not in parts]
    plan = [
        [(odd, bf16)] * bool(odd),
        [([k], f32) for k in even] + [([1], bf16)] * (whole > 1),
    ]
    plan = [groups for groups in plan if groups]
    for groups in plan:
        arrays = resident_call(groups, tensor_at, mixed, output_weight, out_width)
        for (g, kind), array in zip(groups, arrays):
            if kind == bf16:
                got = across(array, 1)
                for i, k in enumerate(g):
                    came[k] = got[i * rows : (i + 1) * rows]
            else:
                parts[g[0]] = array
    for k in sorted((k for k in where if k and not k & 1), key=lambda k: (low_bit(k), -k)):
        main = parts[k]
        bit = 1
        while bit < low_bit(k):
            term = came[k | bit][:, :out_width]
            if k not in chain:
                term = lax.optimization_barrier(term)
            main = main + term.astype(jnp.float32)
            bit *= 2
        if k in chain:
            carried = low2
            for c in chain[: chain.index(k)]:
                carried = carried + came[c][:, out_width:].astype(jnp.float32)
            main = jnp.concatenate([main, carried], axis=1)
        came[k] = across(main.astype(jnp.bfloat16), low_bit(k))
    lows = [came[k] for k in chain[:-1]]
    terms = [parts[0]] + [came[1 << i] for i in range(len(bits) - 1)]
    return pl.pallas_call(
        functools.partial(final_kernel, out_width, (len(lows), len(terms)), replicas),
        in_specs=[VMEM] * (2 + replicas + len(lows) + len(terms)),
        out_specs=VMEM,
        out_shape=jax.ShapeDtypeStruct((rows, out_width), jnp.bfloat16),
        name="final",
        **params((10**8, 10**6)),
    )(picks, low2, *output_up, *lows, *terms)


def solution(mesh):
    sizes = dict(mesh.shape)

    def body(*arrays):
        return per_device(sizes, *arrays)

    return jax.shard_map(
        body,
        mesh=mesh,
        in_specs=(
            P(("groups", "replica"), "tensor"),
            P(None, "tensor"),
            P("tensor", None),
            P(("groups", "replica"), None, None, None),
            P(("groups", "replica"), None, None, None),
            P(("groups", "replica"), None, "tensor"),
            P(("groups", "replica"), None, "tensor"),
            P(("groups", "replica"), None, "tensor"),
            P(("groups", "replica"), None, "tensor"),
            P("groups"),
            P("groups"),
            P(("groups", "replica")),
        ),
        out_specs=P(("groups", "replica"), "tensor"),
        check_vma=False,
    )
```
